256 devices in a mesh: head: 4 (over x), batch: 64 (over y, z, core).
Axes of the slice: x: 4, y: 4, z: 8, core: 2. Of those that a mesh axis runs over, the one named last changes fastest.
Arguments:
- query_symbol_numbers: int32 [64, 4], P('batch'), may hold values from 0 to 65535
- alive_span_sizes: int32 [64], P('batch'), may hold values from 1 to 4
- former_positions: int32 [64], P('batch'), may hold values from 0 to 63, each once
- previous_normed_vectors: bfloat16 [2, 64, 4096], P(None, 'batch'), may hold values from -6 to 6
- memory_matrices: bfloat16 [64, 64, 64, 64], P('batch', 'head'), may hold values from -6 to 6
- vocabulary_vectors: bfloat16 [4096, 65536], P('batch', 'head'), may hold values from -6 to 6
- standardize_scales: float32 [2, 4096], P(None, 'batch'), may hold values from 0.5 to 1.5
- standardize_shifts: float32 [2, 4096], P(None, 'batch'), may hold values from -2 to 2
- timemix_blend_factors: float32 [5, 4096], P(None, 'batch'), may hold values from 0 to 1
- timemix_linear_maps: bfloat16 [4, 4096, 4096], P(None, 'batch', 'head'), may hold values from -0.09375 to 0.09375
- forgetting_first_lowrank: bfloat16 [4096, 128], P('batch'), may hold values from -0.09375 to 0.09375
- forgetting_second_lowrank: bfloat16 [128, 4096], P(None, 'head'), may hold values from -0.5 to 0.5
- forgetting_loglog_floor: float32 [4096], P('head'), may hold values from -6 to 0
- current_reward_factor: float32 [4096], P('head'), may hold values from -3 to 3
- perspan_standardize_scale: float32 [4096], P('head'), may hold values from 0.5 to 1.5
- perspan_standardize_shift: float32 [4096], P('head'), may hold values from -2 to 2
- timemix_emit_matrix: bfloat16 [4096, 4096], P('batch', 'head'), may hold values from -0.09375 to 0.09375
- feedforward_blend_factors: float32 [2, 4096], P(None, 'batch'), may hold values from 0 to 1
- feedforward_lookup_matrix: bfloat16 [4096, 14336], P('batch', 'head'), may hold values from -0.09375 to 0.09375
- feedforward_accept_matrix: bfloat16 [4096, 4096], P('batch'), may hold values from -0.09375 to 0.09375
- feedforward_emit_matrix: bfloat16 [4096, 14336], P('batch', 'head'), may hold values from -0.046875 to 0.046875
Outputs:
- hidden: float32 [64, 4, 4096], P(None, None, 'batch')
- new_edges: bfloat16 [2, 64, 4096], P(None, None, 'batch')
- new_states: bfloat16 [64, 64, 64, 64], P('batch', 'head')
The draws below stay inside these ranges and needn't reach their ends.
Inputs may be any that keep to these rules, and one draw needn't show every extreme that they name: `alive_span_sizes`: some request has 4 live tokens. `former_positions`: each old index appears exactly once.
All inputs are finite; a program needn't handle non-finite values.
Results may differ from the reference program's by a relative error of at most 0.015.
Values may be sent and summed in bfloat16 or wider, within the bound.
A program may use at most 128 MiB of HBM per device.

```python
import math
import jax
import jax.numpy as jnp
import numpy as np
from jax import lax

EMBEDDING_DIM = 4096
SUBSPACE_TOTAL = 64
SUBSPACE_SIZE = 64
FF = 14336
VOCAB = 65536
DR = 128
SLOTS = 4
REQUESTS = 64


def with_ends(values, own_key, least, largest):
    longest = values.shape.index(max(values.shape))
    spots = []
    for shift in (0, 1):
        where = [jax.random.randint(jax.random.fold_in(own_key, axis), (), 0, length) for axis, length in enumerate(values.shape)]
        where[longest] = (where[longest] + shift) % values.shape[longest]
        spots.append(tuple(where))
    return values.at[spots[0]].set(least).at[spots[1]].set(largest)


def shard_levels(own_key, dims, shards, low, top_value):
    def one(axis_at, shards_of):
        draws = jax.random.uniform(jax.random.fold_in(jax.random.fold_in(own_key, 6), axis_at), (shards_of,), jnp.float32, low / len(shards), top_value / len(shards))
        return jnp.repeat(jnp.exp(draws), dims[axis_at] // shards_of).reshape((-1,) + (1,) * (len(dims) - axis_at - 1))

    loudness = one(*shards[0])
    for cut in shards[1:]:
        loudness = loudness * one(*cut)
    return loudness


def rank_table(amount, slope):
    weights = [(1 << 20) // math.isqrt(rank ** slope) + 1 for rank in range(1, amount + 1)]
    scale = 1 + sum(weights) // (1 << 30)
    return np.cumsum(np.array([max(1, weight // scale) for weight in weights]))


def skewed_ids(key, dims, amount, lean):
    table = rank_table(amount, lean)
    ticket = jax.random.randint(jax.random.fold_in(key, 1), dims, 0, int(table[amount - 1]))
    standing = jnp.searchsorted(jnp.asarray(table, jnp.int32), ticket, side="right")
    return jax.random.permutation(jax.random.fold_in(key, 2), amount)[standing].astype(jnp.int32)


def gaussian(key, extent, scale, reach, cuts=(), kind=jnp.bfloat16):
    level = shard_levels(key, extent, cuts, -0.22, 0.18) if cuts else 1.0
    array = jax.random.normal(key, extent, jnp.float32) * scale * level
    return jnp.minimum(jnp.maximum(array, -reach), reach).astype(kind)


def setup_inputs(seed: int = 0) -> dict:
    seeds = jax.random.split(jax.random.key(seed), 22)
    query_symbol_numbers = with_ends(skewed_ids(seeds[0], (REQUESTS, SLOTS), VOCAB, 2), jax.random.fold_in(seeds[0], 3), 0, VOCAB - 1).astype(jnp.int32)
    alive_span_sizes = with_ends(jax.random.randint(seeds[1], (REQUESTS,), 1, SLOTS + 1), jax.random.fold_in(seeds[1], 1), 1, SLOTS).astype(jnp.int32)
    former_positions = jax.random.permutation(seeds[2], REQUESTS).astype(jnp.int32)
    previous_normed_vectors = gaussian(seeds[3], (2, REQUESTS, EMBEDDING_DIM), 1.0, 6.0, ((1, 64),))
    memory_matrices = gaussian(seeds[4], (REQUESTS, SUBSPACE_TOTAL, SUBSPACE_SIZE, SUBSPACE_SIZE), 1.0, 6.0, ((0, 64), (1, 4)))
    vocabulary_vectors = gaussian(seeds[5], (EMBEDDING_DIM, VOCAB), 1.0, 6.0, ((0, 64), (1, 4)))
    standardize_scales = jnp.clip(1.0 + 0.1 * jax.random.normal(seeds[6], (2, EMBEDDING_DIM), jnp.float32), 0.5, 1.5)
    standardize_shifts = gaussian(seeds[7], (2, EMBEDDING_DIM), 0.3, 2.0, ((1, 64),), jnp.float32)
    timemix_blend_factors = jnp.clip(1.0 * jax.random.uniform(seeds[8], (5, EMBEDDING_DIM), jnp.float32) ** shard_levels(seeds[8], (5, EMBEDDING_DIM), ((1, 64),), -0.2, 0.2), 0.0, 1.0)
    timemix_linear_maps = gaussian(seeds[9], (4, EMBEDDING_DIM, EMBEDDING_DIM), EMBEDDING_DIM ** -0.5, 0.09375, ((1, 64), (2, 4)))
    forgetting_first_lowrank = gaussian(seeds[10], (EMBEDDING_DIM, DR), EMBEDDING_DIM ** -0.5, 0.09375, ((0, 64),))
    forgetting_second_lowrank = gaussian(seeds[11], (DR, EMBEDDING_DIM), DR ** -0.5, 0.5, ((1, 4),))
    forgetting_loglog_floor = jnp.clip(-6.0 + 6.0 * jax.random.uniform(seeds[12], (EMBEDDING_DIM,), jnp.float32) ** shard_levels(seeds[12], (EMBEDDING_DIM,), ((0, 4),), -0.2, 0.2), -6.0, 0.0)
    current_reward_factor = gaussian(seeds[13], (EMBEDDING_DIM,), 0.5, 3.0, ((0, 4),), jnp.float32)
    perspan_standardize_scale = jnp.clip(1.0 + 0.1 * jax.random.normal(seeds[14], (EMBEDDING_DIM,), jnp.float32), 0.5, 1.5)
    perspan_standardize_shift = gaussian(seeds[15], (EMBEDDING_DIM,), 0.3, 2.0, ((0, 4),), jnp.float32)
    timemix_emit_matrix = gaussian(seeds[16], (EMBEDDING_DIM, EMBEDDING_DIM), EMBEDDING_DIM ** -0.5, 0.09375, ((0, 64), (1, 4)))
    feedforward_blend_factors = jnp.clip(1.0 * jax.random.uniform(seeds[17], (2, EMBEDDING_DIM), jnp.float32) ** shard_levels(seeds[17], (2, EMBEDDING_DIM), ((1, 64),), -0.2, 0.2), 0.0, 1.0)
    feedforward_lookup_matrix = gaussian(seeds[18], (EMBEDDING_DIM, FF), EMBEDDING_DIM ** -0.5, 0.09375, ((0, 64), (1, 4)))
    feedforward_accept_matrix = gaussian(seeds[19], (EMBEDDING_DIM, EMBEDDING_DIM), EMBEDDING_DIM ** -0.5, 0.09375, ((0, 64),))
    feedforward_emit_matrix = gaussian(seeds[20], (EMBEDDING_DIM, FF), FF ** -0.5, 0.046875, ((0, 64), (1, 4)))
    return {"query_symbol_numbers": query_symbol_numbers, "alive_span_sizes": alive_span_sizes, "former_positions": former_positions, "previous_normed_vectors": previous_normed_vectors, "memory_matrices": memory_matrices, "vocabulary_vectors": vocabulary_vectors, "standardize_scales": standardize_scales, "standardize_shifts": standardize_shifts, "timemix_blend_factors": timemix_blend_factors, "timemix_linear_maps": timemix_linear_maps, "forgetting_first_lowrank": forgetting_first_lowrank, "forgetting_second_lowrank": forgetting_second_lowrank, "forgetting_loglog_floor": forgetting_loglog_floor, "current_reward_factor": current_reward_factor, "perspan_standardize_scale": perspan_standardize_scale, "perspan_standardize_shift": perspan_standardize_shift, "timemix_emit_matrix": timemix_emit_matrix, "feedforward_blend_factors": feedforward_blend_factors, "feedforward_lookup_matrix": feedforward_lookup_matrix, "feedforward_accept_matrix": feedforward_accept_matrix, "feedforward_emit_matrix": feedforward_emit_matrix}


EPS_LN = 1e-05
EPS_GN = 0.00064

def layer_norm(stream, gain, bias):
    mean = lax.optimization_barrier(jnp.mean(stream, axis=-1, keepdims=True))
    spread = lax.optimization_barrier(jnp.mean(jnp.square(stream - mean), axis=-1, keepdims=True))
    return (stream - mean) * lax.rsqrt(spread + EPS_LN) * gain + bias

def shifted(normed, edge, mixes):
    before = jnp.concatenate([edge[:, None], normed[:, :-1]], axis=1)
    delta = before.astype(jnp.float32) - normed.astype(jnp.float32)
    return (normed.astype(jnp.float32)[None] + delta[None] * mixes[:, None, None, :]).astype(jnp.bfloat16)

def reference(query_symbol_numbers, alive_span_sizes, former_positions, previous_normed_vectors, memory_matrices, vocabulary_vectors, standardize_scales, standardize_shifts, timemix_blend_factors, timemix_linear_maps, forgetting_first_lowrank, forgetting_second_lowrank, forgetting_loglog_floor, current_reward_factor, perspan_standardize_scale, perspan_standardize_shift, timemix_emit_matrix, feedforward_blend_factors, feedforward_lookup_matrix, feedforward_accept_matrix, feedforward_emit_matrix):
    count = REQUESTS * SLOTS
    live = jnp.arange(SLOTS, dtype=jnp.int32)[None, :] < alive_span_sizes[:, None]
    stream = vocabulary_vectors.T[query_symbol_numbers].astype(jnp.float32)
    edges = previous_normed_vectors[:, former_positions]
    memory_collection = memory_matrices[former_positions].astype(jnp.float32)
    normed = layer_norm(stream, standardize_scales[0], standardize_shifts[0]).astype(jnp.bfloat16)
    mixed = shifted(normed, edges[0], timemix_blend_factors).reshape(5, count, EMBEDDING_DIM)
    proj = jnp.einsum('ntd,nde->nte', mixed[:4].astype(jnp.float32), timemix_linear_maps.astype(jnp.float32))
    low = jnp.tanh(jnp.dot(mixed[4], forgetting_first_lowrank, preferred_element_type=jnp.float32)).astype(jnp.bfloat16)
    decay = jnp.exp(-jnp.exp(forgetting_loglog_floor + jnp.dot(low, forgetting_second_lowrank, preferred_element_type=jnp.float32)))
    shape = (REQUESTS, SLOTS, SUBSPACE_TOTAL, SUBSPACE_SIZE)
    arriving_memories = proj[0].reshape(shape)
    key = proj[1].reshape(shape)
    value = proj[2].reshape(shape)
    gate = proj[3]
    decay = decay.reshape(shape)
    subspace_reward_contribution = current_reward_factor.reshape(SUBSPACE_TOTAL, SUBSPACE_SIZE)
    result_vectors = []
    for position_number in range(SLOTS):
        dyadic_matrix = jnp.einsum('rhk,rhv->rhkv', key[:, position_number], value[:, position_number])
        result_vectors.append(jnp.einsum('tqe,tqeh->tqh', arriving_memories[:, position_number], memory_collection + subspace_reward_contribution[None, :, :, None] * dyadic_matrix))
        updated = decay[:, position_number][..., None] * memory_collection + dyadic_matrix
        memory_collection = jnp.where(live[:, position_number][:, None, None, None], updated, memory_collection)
    wkv = jnp.stack(result_vectors, axis=1)
    mean = lax.optimization_barrier(jnp.mean(wkv, axis=-1, keepdims=True))
    spread = lax.optimization_barrier(jnp.mean(jnp.square(wkv - mean), axis=-1, keepdims=True))
    grouped = ((wkv - mean) * lax.rsqrt(spread + EPS_GN)).reshape(count, EMBEDDING_DIM) * perspan_standardize_scale + perspan_standardize_shift
    gated = (grouped * jax.nn.silu(gate)).astype(jnp.bfloat16)
    stream = stream + jnp.dot(gated, timemix_emit_matrix.T, preferred_element_type=jnp.float32).reshape(REQUESTS, SLOTS, EMBEDDING_DIM)
    normed_two = layer_norm(stream, standardize_scales[1], standardize_shifts[1]).astype(jnp.bfloat16)
    mixed_two = shifted(normed_two, edges[1], feedforward_blend_factors).reshape(2, count, EMBEDDING_DIM)
    units = jnp.square(jax.nn.relu(jnp.dot(mixed_two[0], feedforward_lookup_matrix, preferred_element_type=jnp.float32))).astype(jnp.bfloat16)
    receive = jax.nn.sigmoid(jnp.dot(mixed_two[1], feedforward_accept_matrix, preferred_element_type=jnp.float32))
    values = jnp.dot(units, feedforward_emit_matrix.T, preferred_element_type=jnp.float32)
    result = stream + (receive * values).reshape(REQUESTS, SLOTS, EMBEDDING_DIM)
    hidden = jnp.where(live[..., None], result, jnp.float32(0.0))
    last = (alive_span_sizes - 1).astype(jnp.int32)[:, None, None]
    new_edges = jnp.stack([jnp.take_along_axis(normed, last, axis=1)[:, 0], jnp.take_along_axis(normed_two, last, axis=1)[:, 0]])
    return (hidden, new_edges, memory_collection.astype(jnp.bfloat16))
```

```python
import jax
import jax.numpy as jnp
from jax import lax
from jax.experimental import pallas as pl
from jax.experimental.pallas import tpu as pltpu
from jax.sharding import PartitionSpec as P

F32 = jnp.float32
BF16 = jnp.bfloat16
MESH = pl.DeviceIdType.MESH
EPS_LN = 1e-05
EPS_GN = 0.00064
NX, NY, NZ, NC = 4, 4, 8, 2
NQ = NY * NC
VM = pl.BlockSpec(memory_space=pltpu.VMEM)
ANY = pl.BlockSpec(memory_space=pl.ANY)
DMA = pltpu.SemaphoreType.DMA


def batch_of(y, z, c):
    return (y * NZ + z) * NC + c


def place():
    h = lax.axis_index("head")
    b = lax.axis_index("batch")
    c = lax.rem(b, NC)
    z = lax.rem(lax.div(b, NC), NZ)
    y = lax.div(b, NC * NZ)
    return h, b, y, z, c, y * NC + c


class Group:
    def __init__(self, kind):
        h, b, y, z, c, q = place()
        if kind == "z":
            self.me, self.n = z, NZ
            self.dev = lambda i: (h, batch_of(y, i, c))
        elif kind == "q":
            self.me, self.n = q, NQ
            self.dev = lambda i: (h, batch_of(lax.div(i, NC), z, lax.rem(i, NC)))
        elif kind == "x":
            self.me, self.n = h, NX
            self.dev = lambda i: (i, b)
        elif kind == "b":
            self.me, self.n = b, NY * NZ * NC
            self.dev = lambda i: (h, i)
        else:
            self.me, self.n = q * NX + h, NQ * NX

            def dev(i):
                k = lax.div(i, NX)
                return (lax.rem(i, NX), batch_of(lax.div(k, NC), z, lax.rem(k, NC)))

            self.dev = dev

    def each(self, body):
        def step(p, carry):
            body(p, lax.rem(self.me + p, self.n))
            return carry

        lax.fori_loop(1, self.n, step, 0)


def barrier(*groups):
    sem = pltpu.get_barrier_semaphore()
    for g in groups:
        g.each(
            lambda p, i: pl.semaphore_signal(
                sem, inc=1, device_id=g.dev(i), device_id_type=MESH
            )
        )
    pl.semaphore_wait(sem, sum(g.n - 1 for g in groups))


class Exchange:
    def __init__(self, group, src, dst, sems):
        self.g, self.src, self.dst, self.sems = group, src, dst, sems

    def copy(self, p, i):
        return pltpu.make_async_remote_copy(
            src_ref=self.src(i),
            dst_ref=self.dst(self.g.me),
            send_sem=self.sems.at[0, p],
            recv_sem=self.sems.at[1, p],
            device_id=self.g.dev(i),
            device_id_type=MESH,
        )

    def own(self):
        return pltpu.make_async_copy(
            self.src(self.g.me), self.dst(self.g.me), self.sems.at[0, 0]
        )

    def start(self):
        self.g.each(lambda p, i: self.copy(p, i).start())
        self.own().start()

    def arrive(self):
        self.own().wait()
        self.g.each(lambda p, i: self.copy(p, i).wait_recv())

    def drain(self):
        self.g.each(lambda p, i: self.copy(p, i).wait_send())

    @staticmethod
    def sem(n):
        return DMA((2, n))


def call(kernel, cid, outs, out_specs, in_specs, scratch, args):
    return pl.pallas_call(
        kernel,
        out_shape=[jax.ShapeDtypeStruct(s, d) for s, d in outs],
        in_specs=in_specs,
        out_specs=out_specs,
        scratch_shapes=scratch,
        compiler_params=pltpu.CompilerParams(collective_id=cid, has_side_effects=True),
        name="exchange_%d" % cid,
    )(*args)


def lanes(i, n):
    return pl.ds(pl.multiple_of(i, 128), n)


def chunk_start(i):
    return (7 * lax.div(i, 2) + 3 * lax.rem(i, 2)) * 128


def kernel_a(meta, state, params, low, maps, meta_o, state_o, params_o, low_o, maps_o, s0, s1, s2, s3, s4):
    gb, gq = Group("b"), Group("q")
    xs = [
        Exchange(gb, lambda i: meta, lambda m: meta_o.at[m], s0),
        Exchange(gq, lambda i: params, lambda m: params_o.at[m], s2),
        Exchange(gq, lambda i: low, lambda m: low_o.at[m], s3),
        Exchange(gq, lambda i: maps.at[:, :, lanes(i * 128, 128)], lambda m: maps_o.at[:, m], s4),
        Exchange(
            gb,
            lambda i: state.at[
                (lax.div(i, NC * NZ) * NC + lax.rem(i, NC)) * NZ + lax.rem(lax.div(i, NC), NZ)
            ],
            lambda m: state_o.at[m],
            s1,
        ),
    ]
    barrier(gb)
    for x in xs:
        x.start()
    for x in xs:
        x.arrive()
        x.drain()


def kernel_b(emb, edges, state, edges_o, state_o, stream_o, stats_o, xbuf, blk, st, s0, s1, s2, s3, s4):
    gb, gq, gx, gz = Group("b"), Group("q"), Group("x"), Group("z")
    ex = Exchange(gx, lambda i: emb, lambda m: xbuf.at[m], s0)
    ee = Exchange(
        gb, lambda i: edges.at[lax.rem(lax.div(i, NC), NZ)], lambda m: edges_o.at[m], s1
    )
    es = Exchange(gz, lambda i: state.at[i], lambda m: state_o.at[m], s2)
    barrier(gx, gb)
    ex.start()
    ee.start()
    es.start()
    ex.arrive()
    total = xbuf[0].astype(F32)
    for k in range(1, NX):
        total = total + xbuf[k].astype(F32)
    blk[...] = total.astype(BF16)
    mean = jnp.sum(total, axis=0, keepdims=True) * (1.0 / total.shape[0])
    dev = total - mean
    st[0:1, :] = mean
    st[1:2, :] = jnp.sum(dev * dev, axis=0, keepdims=True)
    eg = Exchange(gq, lambda i: blk, lambda m: stream_o.at[m], s3)
    et = Exchange(gb, lambda i: st, lambda m: stats_o.at[m], s4)
    eg.start()
    et.start()
    eg.arrive()
    et.arrive()
    ee.arrive()
    es.arrive()
    for x in (ex, ee, es, eg, et):
        x.drain()


def kernel_d(part, emit, look, acc, part_o, emit_o, look_o, acc_o, s0, s1, s2, s3):
    gq, gz = Group("q"), Group("z")
    h = lax.axis_index("head")
    xs = [
        Exchange(gz, lambda i: part.at[:, pl.ds(pl.multiple_of(i * 32, 32), 32)], lambda m: part_o.at[m], s0),
        Exchange(gq, lambda i: emit.at[:, lanes(i * 128, 128)], lambda m: emit_o.at[m], s1),
        Exchange(gq, lambda i: look.at[:, lanes(chunk_start(i), 512)], lambda m: look_o.at[m], s2),
        Exchange(
            gq,
            lambda i: acc.at[:, lanes((lax.div(i, NC) * NZ + 2 * h + lax.rem(i, NC)) * 128, 128)],
            lambda m: acc_o.at[m],
            s3,
        ),
    ]
    barrier(gz, gq)
    for x in xs:
        x.start()
    for x in xs:
        x.arrive()
        x.drain()


def kernel_e(gated, state, down, gated_o, state_o, down_o, s0, s1, s2):
    gq, gz = Group("q"), Group("z")
    xs = [
        Exchange(gz, lambda i: gated, lambda m: gated_o.at[m], s0),
        Exchange(gq, lambda i: state.at[i], lambda m: state_o.at[m], s1),
        Exchange(gq, lambda i: down.at[:, lanes(chunk_start(i), 512)], lambda m: down_o.at[m], s2),
    ]
    barrier(gz, gq)
    for x in xs:
        x.start()
    for x in xs:
        x.arrive()
        x.drain()


def kernel_f(part, stream, full_o, stats_o, rbuf, mine, st, s0, s1, s2):
    gg, gz = Group("g"), Group("z")
    er = Exchange(gg, lambda i: part.at[i], lambda m: rbuf.at[m], s0)
    barrier(gg, gz)
    er.start()
    er.arrive()
    mine[...] = stream[...] + jnp.sum(rbuf[...].astype(F32), axis=0)
    eg = Exchange(gg, lambda i: mine, lambda m: full_o.at[m], s1)
    eg.start()
    eg.arrive()
    n = gg.n * mine.shape[0]
    mean = jnp.sum(jnp.sum(full_o[...], axis=0), axis=0, keepdims=True) * (1.0 / n)
    dev = full_o[...] - mean[None]
    st[0:1, :] = mean
    st[1:2, :] = jnp.sum(jnp.sum(dev * dev, axis=0), axis=0, keepdims=True)
    es = Exchange(gz, lambda i: st, lambda m: stats_o.at[m], s2)
    es.start()
    es.arrive()
    for x in (er, eg, es):
        x.drain()


def kernel_i(part, rec, units_o, rec_o, rbuf, abuf, mine, sent, s0, s1, s2, s3):
    gz = Group("z")
    h, b, y, z, c, q = place()
    ep = Exchange(gz, lambda i: part.at[i], lambda m: rbuf.at[m], s0)
    ea = Exchange(gz, lambda i: rec.at[i], lambda m: abuf.at[m], s1)
    dest = (lax.rem(z, NX), batch_of(y, 2 * h + c, lax.div(z, NX)))
    source = (lax.div(z, 2), batch_of(y, c * NX + h, lax.rem(z, 2)))
    other = jnp.logical_or(dest[0] != h, dest[1] != b)

    def beyond(device):
        core = lax.rem(device[1], NC)
        return jnp.logical_or(device[0] != h, core != c)

    sem = pltpu.get_barrier_semaphore()
    gz.each(
        lambda p, i: pl.semaphore_signal(sem, inc=1, device_id=gz.dev(i), device_id_type=MESH)
    )

    @pl.when(beyond(source))
    def _():
        pl.semaphore_signal(sem, inc=1, device_id=source, device_id_type=MESH)

    pl.semaphore_wait(sem, gz.n - 1 + beyond(dest).astype(jnp.int32))

    ep.start()
    ea.start()
    ep.arrive()
    up = jnp.maximum(jnp.sum(rbuf[...].astype(F32), axis=0), 0.0)
    up = up * up
    lane = lax.broadcasted_iota(jnp.int32, up.shape, 1)
    mine[...] = jnp.where(jnp.logical_and(c == 1, lane < 128), 0.0, up).astype(BF16)
    eu = Exchange(gz, lambda i: mine, lambda m: units_o.at[m], s2)
    eu.start()
    ea.arrive()
    sent[...] = jax.nn.sigmoid(jnp.sum(abuf[...].astype(F32), axis=0))

    far = pltpu.make_async_remote_copy(
        src_ref=sent,
        dst_ref=rec_o,
        send_sem=s3.at[0],
        recv_sem=s3.at[1],
        device_id=dest,
        device_id_type=MESH,
    )

    @pl.when(other)
    def _():
        far.start()
        far.wait()

    @pl.when(jnp.logical_not(other))
    def _():
        near = pltpu.make_async_copy(sent, rec_o, s3.at[0])
        near.start()
        near.wait()

    eu.arrive()
    for x in (ep, ea, eu):
        x.drain()


def kernel_k(part, rec, stream, out, rbuf, mine, s0, s1):
    gg, gx = Group("g"), Group("x")
    er = Exchange(gg, lambda i: part.at[i], lambda m: rbuf.at[m], s0)
    barrier(gg)
    er.start()
    er.arrive()
    mine[...] = stream[...] + rec[...] * jnp.sum(rbuf[...].astype(F32), axis=0)
    eg = Exchange(gx, lambda i: mine, lambda m: out.at[m], s1)
    eg.start()
    eg.arrive()
    er.drain()
    eg.drain()


def join(stats, per, count):
    mean = jnp.mean(stats[:, 0], axis=0)
    spread = jnp.sum(stats[:, 1], axis=0) + per * jnp.sum(
        jnp.square(stats[:, 0] - mean[None]), axis=0
    )
    return mean, spread / count


def dot(a, b, ca, cb):
    return lax.dot_general(a, b, (((ca,), (cb,)), ((), ())), preferred_element_type=F32)


def local(
    query_symbol_numbers,
    alive_span_sizes,
    former_positions,
    previous_normed_vectors,
    memory_matrices,
    vocabulary_vectors,
    standardize_scales,
    standardize_shifts,
    timemix_blend_factors,
    timemix_linear_maps,
    forgetting_first_lowrank,
    forgetting_second_lowrank,
    forgetting_loglog_floor,
    current_reward_factor,
    perspan_standardize_scale,
    perspan_standardize_shift,
    timemix_emit_matrix,
    feedforward_blend_factors,
    feedforward_lookup_matrix,
    feedforward_accept_matrix,
    feedforward_emit_matrix,
):
    h, b, y, z, c, q = place()
    i32 = jnp.int32

    meta = jnp.concatenate(
        [query_symbol_numbers[0], alive_span_sizes, former_positions, jnp.zeros((122,), i32)]
    )[None]
    params = jnp.concatenate(
        [standardize_scales, standardize_shifts, timemix_blend_factors, feedforward_blend_factors]
    )
    params = jnp.pad(params, ((0, 5), (0, 64)))
    pieces = memory_matrices.reshape(64, 8, 128)
    S = Exchange.sem
    meta, pieces, params, low_w, maps = call(
        kernel_a,
        0,
        [
            ((64, 1, 128), i32),
            ((64, 8, 128), BF16),
            ((8, 16, 128), F32),
            ((8, 64, 128), BF16),
            ((4, 8, 64, 128), BF16),
        ],
        [VM, VM, VM, ANY, ANY],
        [VM, VM, VM, ANY, ANY],
        [S(64), S(64), S(8), S(8), S(8)],
        (meta, pieces, params, forgetting_first_lowrank, timemix_linear_maps),
    )
    meta = meta[:, 0]
    ids = meta[:, :4].reshape(NY, NZ, NC, 4).transpose(1, 3, 0, 2).reshape(256)
    lengths = meta[:, 4]
    owners = meta[:, 5].reshape(NY, NZ, NC).transpose(1, 0, 2).reshape(64)
    vocab_local = vocabulary_vectors.shape[1]
    offset = ids - h * vocab_local
    inside = (offset >= 0) & (offset < vocab_local)
    looked = jnp.take(vocabulary_vectors, jnp.clip(offset, 0, vocab_local - 1), axis=1)
    emb = jnp.where(inside[None], looked, jnp.zeros_like(looked))
    old = jnp.arange(64, dtype=i32)
    pick = owners[:, None] == old[None, :]
    pieces = dot(pick.astype(BF16), pieces.reshape(64, 1024), 1, 0).astype(BF16)
    params = params[:, :, :64].transpose(0, 2, 1).reshape(512, 16)
    scale, shift = params[:, 0:2], params[:, 2:4]
    mixes, mixes_two = params[:, 4:9], params[:, 9:11]

    edges = previous_normed_vectors.reshape(2, NY, NZ, 128).transpose(2, 0, 1, 3).reshape(NZ, 8, 128)
    edges, start, stream, stats = call(
        kernel_b,
        1,
        [((64, 8, 128), BF16), ((8, 8, 1024), BF16), ((8, 64, 256), BF16), ((64, 2, 256), F32)],
        [VM] * 4,
        [VM] * 3,
        [
            pltpu.VMEM((NX, 64, 256), BF16),
            pltpu.VMEM((64, 256), BF16),
            pltpu.VMEM((2, 256), F32),
            S(4),
            S(64),
            S(8),
            S(8),
            S(64),
        ],
        (emb, edges, pieces.reshape(8, 8, 1024)),
    )
    own_rows = lax.dynamic_slice(stream, (q, h * 16, 0), (1, 16, 256))[0].astype(F32)
    mean, var = join(stats, 64.0, 4096.0)
    tok_z = jnp.arange(256, dtype=i32) // 32
    tok_j = (jnp.arange(256, dtype=i32) // 8) % 4
    tok_q = jnp.arange(256, dtype=i32) % 8
    tok_r = (tok_q // 2 * 8 + tok_z) * 2 + tok_q % 2
    back = (
        (jnp.arange(256, dtype=i32)[:, None] + 8 == jnp.arange(256, dtype=i32)[None, :])
        & (tok_j[None, :] > 0)
    ).astype(BF16)
    owner_tok = jnp.broadcast_to(owners.reshape(8, 1, 8), (8, 4, 8)).reshape(256)
    first = ((old[:, None] == owner_tok[None, :]) & (tok_j[None, :] == 0)).astype(BF16)
    edges = edges.reshape(64, 2, 512)

    def normalize(x, mean, var, k):
        return (
            (x - mean[None]) * lax.rsqrt(var[None] + EPS_LN) * scale[:, k : k + 1]
            + shift[:, k : k + 1]
        ).astype(BF16)

    def shifted(normed, k, mixes):
        before = dot(normed, back, 1, 0) + dot(edges[:, k], first, 0, 0)
        now = normed.astype(F32)
        delta = before - now
        return [
            (now + delta * mixes[:, n : n + 1]).astype(BF16) for n in range(mixes.shape[1])
        ]

    normed = normalize(stream.reshape(512, 256).astype(F32), mean, var, 0)
    mixed = shifted(normed, 0, mixes)
    maps = maps.reshape(4, 512, 128)
    weights = [maps[n] for n in range(4)] + [low_w.reshape(512, 128)]
    part = jnp.stack([dot(m, w, 0, 0).astype(BF16) for m, w in zip(mixed, weights)])

    proj, emit, look, accept = call(
        kernel_d,
        2,
        [((8, 5, 32, 128), BF16), ((8, 64, 128), BF16), ((8, 64, 512), BF16), ((8, 64, 128), BF16)],
        [VM, ANY, ANY, ANY],
        [VM, ANY, ANY, ANY],
        [S(8)] * 4,
        (part, timemix_emit_matrix, feedforward_lookup_matrix, feedforward_accept_matrix),
    )
    proj = jnp.sum(proj.astype(F32), axis=0)
    low = jnp.tanh(proj[4]).astype(BF16)

    def mine(v):
        return lax.dynamic_slice_in_dim(v, q * 128, 128, v.ndim - 1)

    decay = jnp.exp(
        -jnp.exp(
            mine(forgetting_loglog_floor)[None]
            + jnp.dot(low, mine(forgetting_second_lowrank), preferred_element_type=F32)
        )
    )
    shape = (4, 8, 2, 64)
    rec, key, val = (proj[n].reshape(shape) for n in range(3))
    decay = decay.reshape(shape)
    bonus = mine(current_reward_factor).reshape(2, 64)
    lens_q = lax.dynamic_index_in_dim(lengths.reshape(NY, NZ, NC), z, 1, keepdims=False).reshape(8)
    state = (
        start.reshape(2, 4, 8, 16, 64).transpose(2, 0, 1, 3, 4).reshape(8, 2, 64, 64).astype(F32)
    )
    outs = []
    for j in range(4):
        r, k, v, d = rec[j], key[j], val[j], decay[j]
        within = jnp.sum(state * r[..., None], axis=2)
        within = within + jnp.sum(r * bonus[None] * k, axis=-1, keepdims=True) * v
        outs.append(within)
        alive = (j < lens_q)[:, None, None, None]
        state = jnp.where(alive, d[..., None] * state + k[..., None] * v[:, :, None, :], state)
    wkv = jnp.stack(outs)
    mu = jnp.mean(wkv, axis=-1, keepdims=True)
    spread = jnp.mean(jnp.square(wkv - mu), axis=-1, keepdims=True)
    grouped = ((wkv - mu) * lax.rsqrt(spread + EPS_GN)).reshape(32, 128)
    grouped = grouped * mine(perspan_standardize_scale)[None] + mine(perspan_standardize_shift)[None]
    gated = (grouped * jax.nn.silu(proj[3])).astype(BF16)

    gated, states, down = call(
        kernel_e,
        3,
        [((8, 32, 128), BF16), ((8, 64, 128), BF16), ((8, 64, 512), BF16)],
        [VM, VM, ANY],
        [VM, VM, ANY],
        [S(8)] * 3,
        (gated, state.astype(BF16).reshape(8, 64, 128), feedforward_emit_matrix),
    )
    new_states = states.reshape(1, 16, 64, 64)
    att = dot(emit.reshape(512, 128), gated.reshape(256, 128), 1, 1).astype(BF16)

    full, stats = call(
        kernel_f,
        4,
        [((32, 16, 256), F32), ((8, 2, 256), F32)],
        [VM] * 2,
        [VM] * 2,
        [
            pltpu.VMEM((32, 16, 256), BF16),
            pltpu.VMEM((16, 256), F32),
            pltpu.VMEM((2, 256), F32),
            S(32),
            S(32),
            S(8),
        ],
        (att.reshape(32, 16, 256), own_rows),
    )
    own_two = lax.dynamic_index_in_dim(full, q * 4 + h, 0, keepdims=False)
    mean, var = join(stats, 512.0, 4096.0)
    normed_two = normalize(full.reshape(512, 256), mean, var, 1)
    mixed_two = shifted(normed_two, 1, mixes_two)
    part = dot(mixed_two[0], look.reshape(512, 512), 0, 0).astype(BF16).reshape(8, 32, 512)
    recv = dot(accept.reshape(512, 128), mixed_two[1], 0, 0).astype(BF16).reshape(8, 16, 256)

    units, recv = call(
        kernel_i,
        5,
        [((8, 32, 512), BF16), ((16, 256), F32)],
        [VM] * 2,
        [VM] * 2,
        [
            pltpu.VMEM((8, 32, 512), BF16),
            pltpu.VMEM((8, 16, 256), BF16),
            pltpu.VMEM((32, 512), BF16),
            pltpu.VMEM((16, 256), F32),
            S(8),
            S(8),
            S(8),
            DMA((2,)),
        ],
        (part, recv),
    )
    values = dot(down.reshape(512, 512), units.reshape(256, 512), 1, 1).astype(BF16)

    (result,) = call(
        kernel_k,
        6,
        [((4, 16, 256), F32)],
        [VM],
        [VM] * 3,
        [pltpu.VMEM((32, 16, 256), BF16), pltpu.VMEM((16, 256), F32), S(32), S(4)],
        (values.reshape(32, 16, 256), recv, own_two),
    )
    result = result.reshape(64, NZ, 4, NY, NC).transpose(3, 1, 4, 2, 0).reshape(64, 4, 64)
    live = jnp.arange(4, dtype=i32)[None, :] < lengths[:, None]
    hidden = jnp.where(live[..., None], result, jnp.float32(0.0))
    last = ((tok_r[:, None] == old[None, :]) & (tok_j[:, None] == lengths[None, :] - 1)).astype(BF16)

    def last_of(normed):
        rows = lax.dynamic_slice_in_dim(normed, q * 64, 64, 0)
        return dot(last, rows, 0, 1).astype(BF16)

    new_edges = jnp.stack([last_of(normed), last_of(normed_two)])
    return (hidden, new_edges, new_states)


def solution(mesh):
    return jax.shard_map(
        local,
        mesh=mesh,
        in_specs=(
            P("batch", None),
            P("batch"),
            P("batch"),
            P(None, "batch", None),
            P("batch", "head", None, None),
            P("batch", "head"),
            P(None, "batch"),
            P(None, "batch"),
            P(None, "batch"),
            P(None, "batch", "head"),
            P("batch", None),
            P(None, "head"),
            P("head"),
            P("head"),
            P("head"),
            P("head"),
            P("batch", "head"),
            P(None, "batch"),
            P("batch", "head"),
            P("batch", None),
            P("batch", "head"),
        ),
        out_specs=(P(None, None, "batch"), P(None, None, "batch"), P("batch", "head", None, None)),
        check_vma=False,
    )
```

```python
import jax
import jax.numpy as jnp
from jax import lax
from jax.experimental import pallas as pl
from jax.experimental.pallas import tpu as pltpu
from jax.sharding import PartitionSpec as P

F32 = jnp.float32
BF16 = jnp.bfloat16
MESH = pl.DeviceIdType.MESH
EPS_LN = 1e-05
EPS_GN = 0.00064
NX, NY, NZ, NC = 4, 4, 8, 2
NQ = NY * NC
VM = pl.BlockSpec(memory_space=pltpu.VMEM)
ANY = pl.BlockSpec(memory_space=pl.ANY)
DMA = pltpu.SemaphoreType.DMA


def batch_of(y, z, c):
    return (y * NZ + z) * NC + c


def place():
    h = lax.axis_index("head")
    b = lax.axis_index("batch")
    c = lax.rem(b, NC)
    z = lax.rem(lax.div(b, NC), NZ)
    y = lax.div(b, NC * NZ)
    return h, b, y, z, c, y * NC + c


class Group:
    def __init__(self, kind):
        h, b, y, z, c, q = place()
        if kind == "z":
            self.me, self.n = z, NZ
            self.dev = lambda i: (h, batch_of(y, i, c))
        elif kind == "q":
            self.me, self.n = q, NQ
            self.dev = lambda i: (h, batch_of(lax.div(i, NC), z, lax.rem(i, NC)))
        elif kind == "x":
            self.me, self.n = h, NX
            self.dev = lambda i: (i, b)
        elif kind == "b":
            self.me, self.n = b, NY * NZ * NC
            self.dev = lambda i: (h, i)
        else:
            self.me, self.n = q * NX + h, NQ * NX

            def dev(i):
                k = lax.div(i, NX)
                return (lax.rem(i, NX), batch_of(lax.div(k, NC), z, lax.rem(k, NC)))

            self.dev = dev

    def each(self, body):
        def step(p, carry):
            body(p, lax.rem(self.me + p, self.n))
            return carry

        lax.fori_loop(1, self.n, step, 0)


def barrier(*groups):
    sem = pltpu.get_barrier_semaphore()
    for g in groups:
        g.each(
            lambda p, i: pl.semaphore_signal(
                sem, inc=1, device_id=g.dev(i), device_id_type=MESH
            )
        )
    pl.semaphore_wait(sem, sum(g.n - 1 for g in groups))


class Exchange:
    def __init__(self, group, src, dst, whole, sems):
        self.g, self.src, self.dst, self.whole, self.sems = group, src, dst, whole, sems

    def copy(self, i):
        return pltpu.make_async_remote_copy(
            src_ref=self.src(i),
            dst_ref=self.dst(self.g.me),
            send_sem=self.sems.at[0],
            recv_sem=self.sems.at[1],
            device_id=self.g.dev(i),
            device_id_type=MESH,
        )

    def start(self):
        self.g.each(lambda p, i: self.copy(i).start())
        pltpu.make_async_copy(self.src(self.g.me), self.dst(self.g.me), self.sems.at[1]).start()

    def arrive(self):
        pltpu.make_async_copy(self.whole, self.whole, self.sems.at[1]).wait()

    def drain(self):
        part = self.dst(0)
        for _ in range(1):
            self.g.each(
                lambda p, i: pltpu.make_async_copy(part, part, self.sems.at[0]).wait()
            )


def lanes(i, n):
    return pl.ds(pl.multiple_of(i, 128), n)


def rows(i, n):
    return pl.ds(pl.multiple_of(i, n), n)


def chunk_start(i):
    return (7 * lax.div(i, 2) + 3 * lax.rem(i, 2)) * 128


def iota(shape, axis):
    return lax.broadcasted_iota(jnp.int32, shape, axis)


def dot(a, b, cb=0):
    return lax.dot_general(a, b, (((1,), (cb,)), ((), ())), preferred_element_type=F32)


def head_sum(x):
    left = iota(x.shape, 1) < 64
    a = jnp.sum(jnp.where(left, x, 0.0), axis=1, keepdims=True)
    b = jnp.sum(jnp.where(left, 0.0, x), axis=1, keepdims=True)
    return jnp.where(left, a, b)


def split(x):
    high = x.astype(BF16)
    return high, (x - high.astype(F32)).astype(BF16)


def join(stats, per, count):
    blocks = stats[...]
    total = jnp.sum(blocks, axis=0)
    mean = total[0:1] * (1.0 / blocks.shape[0])
    dev = blocks - mean[None]
    between = jnp.sum(dev * dev, axis=0)[0:1]
    return mean, (total[1:2] + per * between) * (1.0 / count)


def block_stats(x, st):
    mean = jnp.sum(x, axis=0, keepdims=True) * (1.0 / x.shape[0])
    dev = x - mean
    st[0:1, :] = mean
    st[1:2, :] = jnp.sum(dev * dev, axis=0, keepdims=True)
    return dev


INPUTS = [
    "ids", "lens", "pos", "gains", "biases", "mixes", "mixes2", "edges", "state", "low", "maps",
    "emit", "look", "acc", "down", "vocab", "second", "floor", "bonus", "gn_gain", "gn_bias",
]
SPACES = ["S"] * 3 + ["V"] * 6 + ["A"] * 7 + ["V"] * 5
OUTPUTS = ["hidden", "new_edges", "states"]
SCRATCH = [
    ("meta_s", (1, 128), jnp.int32),
    ("meta_r", (64, 1, 128), jnp.int32),
    ("prm_s", (16, 128), F32),
    ("prm_r", (8, 16, 128), F32),
    ("edges_r", (64, 8, 128), BF16),
    ("edges_f", (64, 8, 128), F32),
    ("state_r", (64, 8, 128), BF16),
    ("state_s", (64, 8, 128), BF16),
    ("state_z", (8, 8, 8, 128), BF16),
    ("low_w", (8, 64, 128), BF16),
    ("maps_w", (4, 8, 64, 128), BF16),
    ("emit_w", (8, 64, 128), BF16),
    ("look_w", (8, 64, 512), BF16),
    ("acc_w", (8, 64, 128), BF16),
    ("down_w", (8, 64, 512), BF16),
    ("vocab_w", (64, 16384), BF16),
    ("table", (64, 128), F32),
    ("emb_s", (64, 256), BF16),
    ("emb_r", (NX, 64, 256), BF16),
    ("blk", (64, 256), BF16),
    ("st", (2, 256), F32),
    ("st_r", (64, 2, 256), F32),
    ("stream_r", (8, 64, 256), BF16),
    ("part_s", (5, 256, 128), BF16),
    ("part_r", (8, 5, 32, 128), BF16),
    ("bd", (8, 128, 128), BF16),
    ("gated_s", (32, 128), BF16),
    ("gated_r", (8, 32, 128), BF16),
    ("new_s", (8, 64, 128), BF16),
    ("att_s", (8, 64, 256), BF16),
    ("att_r", (8, 64, 256), BF16),
    ("attx_s", (64, 256), BF16),
    ("attx_r", (NX, 64, 256), BF16),
    ("two", (64, 256), F32),
    ("dev_s", (64, 256), BF16),
    ("st2", (2, 256), F32),
    ("st2_r", (64, 2, 256), F32),
    ("dev_r", (8, 64, 256), BF16),
    ("up_s", (8, 32, 512), BF16),
    ("up_r", (8, 32, 512), BF16),
    ("rec_s", (8, 16, 256), BF16),
    ("rec_r", (8, 16, 256), BF16),
    ("units_s", (32, 512), BF16),
    ("units_r", (8, 32, 512), BF16),
    ("sig_s", (16, 256), F32),
    ("sig_r", (4, 16, 256), F32),
    ("val_s", (8, 64, 256), BF16),
    ("val_r", (8, 64, 256), BF16),
    ("valx_s", (64, 256), BF16),
    ("valx_r", (NX, 64, 256), BF16),
    ("norm_t", (512, 256), F32),
]
SEMS = [
    "meta", "prm", "edges", "state", "zstate", "low", "maps", "emit", "look", "acc", "down", "emb",
    "stats", "stream", "part", "gated", "new", "att", "attx", "stats2", "dev2", "up", "rec",
    "units", "val", "valx",
]


class Refs:
    pass


def kernel(*refs):
    r, s = Refs(), Refs()
    names = INPUTS + OUTPUTS + [n for n, _, _ in SCRATCH]
    for name, ref in zip(names, refs):
        setattr(r, name + ("_o" if name in OUTPUTS else ""), ref)
    for name, ref in zip(SEMS + ["sig", "vocab", "smem"], refs[len(names) :]):
        setattr(s, name, ref)
    meta_m = refs[-1]
    h, b, y, z, c, q = place()
    gb, gq, gx, gz = Group("b"), Group("q"), Group("x"), Group("z")

    dest = lambda k: (k, batch_of(y, 2 * h + c, lax.div(z, NX)))
    source = lambda k: (lax.div(z, 2), batch_of(y, c * NX + k, lax.rem(z, 2)))
    dest_here = dest(0)[1] == b

    sem = pltpu.get_barrier_semaphore()
    for g in (gb, gx):
        g.each(
            lambda p, i: pl.semaphore_signal(sem, inc=1, device_id=g.dev(i), device_id_type=MESH)
        )
    for k in range(4):
        far = source(k)

        @pl.when(jnp.logical_and(far[0] != h, far[1] != b))
        def _():
            pl.semaphore_signal(sem, inc=1, device_id=far, device_id_type=MESH)

    vocab_in = pltpu.make_async_copy(r.vocab, r.vocab_w, s.vocab)
    vocab_in.start()
    lane = iota((1, 128), 1)
    meta = jnp.where(lane == 4, r.lens[0], jnp.where(lane == 5, r.pos[0], 0))
    for j in range(4):
        meta = jnp.where(lane == j, r.ids[0, j], meta)
    r.meta_s[...] = meta
    r.prm_s[...] = jnp.zeros((16, 128), F32)
    r.prm_s[0:2, 0:64] = r.gains[...]
    r.prm_s[2:4, 0:64] = r.biases[...]
    r.prm_s[4:9, 0:64] = r.mixes[...]
    r.prm_s[9:11, 0:64] = r.mixes2[...]
    prm = r.prm_s[...]
    r.prm_s[...] = jnp.where(c == 0, prm, pltpu.roll(prm, 64, 1))

    pl.semaphore_wait(sem, gb.n - 1 + gx.n - 1 + 3 * (1 - dest_here.astype(jnp.int32)))

    def same(ref):
        return lambda i: ref

    def slots(ref):
        return lambda m: ref.at[m]

    x_meta = Exchange(gb, same(r.meta_s), slots(r.meta_r), r.meta_r, s.meta)
    x_prm = Exchange(gq, same(r.prm_s), slots(r.prm_r), r.prm_r, s.prm)
    x_edges = Exchange(
        gb, lambda i: r.edges.at[lax.rem(lax.div(i, NC), NZ)], slots(r.edges_r), r.edges_r, s.edges
    )
    x_state = Exchange(
        gb,
        lambda i: r.state.at[
            (lax.div(i, NC * NZ) * NC + lax.rem(i, NC)) * NZ + lax.rem(lax.div(i, NC), NZ)
        ],
        slots(r.state_r),
        r.state_r,
        s.state,
    )
    x_low = Exchange(gq, same(r.low), slots(r.low_w), r.low_w, s.low)
    x_maps = Exchange(
        gq,
        lambda i: r.maps.at[:, :, lanes(i * 128, 128)],
        lambda m: r.maps_w.at[:, m],
        r.maps_w,
        s.maps,
    )
    x_emit = Exchange(gq, lambda i: r.emit.at[:, lanes(i * 128, 128)], slots(r.emit_w), r.emit_w, s.emit)
    x_look = Exchange(
        gq, lambda i: r.look.at[:, lanes(chunk_start(i), 512)], slots(r.look_w), r.look_w, s.look
    )
    x_acc = Exchange(
        gq,
        lambda i: r.acc.at[:, lanes((lax.div(i, NC) * NZ + 2 * h + lax.rem(i, NC)) * 128, 128)],
        slots(r.acc_w),
        r.acc_w,
        s.acc,
    )
    x_down = Exchange(
        gq, lambda i: r.down.at[:, lanes(chunk_start(i), 512)], slots(r.down_w), r.down_w, s.down
    )
    for x in (x_meta, x_prm, x_edges, x_state, x_maps, x_low, x_emit, x_look, x_acc, x_down):
        x.start()

    x_meta.arrive()
    to_smem = pltpu.make_async_copy(r.meta_r, meta_m, s.smem)
    to_smem.start()
    meta = r.meta_r[...].reshape(64, 128)
    high = lax.shift_right_logical(meta, 8)
    lowb = (meta - high * 256).astype(F32).astype(BF16)
    high = high.astype(F32).astype(BF16)

    def device_of(zz, qq):
        return (lax.shift_right_logical(qq, 1) * NZ + zz) * NC + (qq & 1)

    tok = iota((256, 64), 0)
    by_tok = device_of(lax.shift_right_logical(tok, 5), tok & 7) == iota((256, 64), 1)
    by_tok = jnp.where(by_tok, 1.0, 0.0).astype(BF16)
    cols = dot(by_tok, high) * 256.0 + dot(by_tok, lowb)
    req = iota((64, 64), 0)
    by_req = device_of(lax.shift_right_logical(req, 3), req & 7) == iota((64, 64), 1)
    by_req = jnp.where(by_req, 1.0, 0.0).astype(BF16)
    r.table[...] = dot(by_req, lowb)
    tok_rows = cols.T
    lane_t = iota((1, 256), 1)
    slot = lax.shift_right_logical(lane_t, 3) & 3
    ids = tok_rows[0:1]
    for j in range(1, 4):
        ids = jnp.where(slot == j, tok_rows[j : j + 1], ids)
    ids = ids.astype(jnp.int32) - h * 16384
    length = tok_rows[4:5].astype(jnp.int32)

    vocab_in.wait()
    step = 1024

    def look_up(k, acc):
        base = pl.multiple_of(k * step, step)
        hot = jnp.where(iota((step, 256), 0) == ids - base, 1.0, 0.0).astype(BF16)
        return acc + dot(r.vocab_w[:, pl.ds(base, step)], hot)

    emb = lax.fori_loop(0, 16384 // step, look_up, jnp.zeros((64, 256), F32))
    r.emb_s[...] = emb.astype(BF16)
    x_emb = Exchange(gx, same(r.emb_s), slots(r.emb_r), r.emb_r, s.emb)
    x_emb.start()

    x_edges.arrive()
    x_state.arrive()
    to_smem.wait()

    def reorder(n, carry):
        zz = lax.div(n, 8)
        qq = lax.rem(n, 8)
        old = meta_m[batch_of(lax.div(qq, 2), zz, lax.rem(qq, 2)), 0, 5]
        r.edges_f[n] = r.edges_r[old].astype(F32)
        r.state_s[n] = r.state_r[old]
        return carry

    lax.fori_loop(0, 64, reorder, 0)
    x_zstate = Exchange(gz, lambda i: r.state_s.at[rows(i * 8, 8)], slots(r.state_z), r.state_z, s.zstate)
    x_zstate.start()

    x_emb.arrive()
    own = jnp.sum(r.emb_r[...].astype(F32), axis=0)
    r.blk[...] = own.astype(BF16)
    x_stream = Exchange(gq, same(r.blk), slots(r.stream_r), r.stream_r, s.stream)
    x_stream.start()
    block_stats(own, r.st)
    x_stats = Exchange(gb, same(r.st), slots(r.st_r), r.st_r, s.stats)
    x_stats.start()

    x_prm.arrive()
    prm = jnp.concatenate([r.prm_r[2 * k] + r.prm_r[2 * k + 1] for k in range(NY)], axis=1)

    def shifted(normed, k, first):
        now = normed.astype(F32).reshape(8, 4, 8, 512)
        edge = jnp.concatenate([r.edges_f[:, k * 4 + i, :] for i in range(NY)], axis=1)
        before = jnp.concatenate([edge.reshape(8, 1, 8, 512), now[:, :3]], axis=1)
        delta = (before - now).reshape(256, 512)
        now = now.reshape(256, 512)
        return lambda n: (now + delta * prm[first + n : first + n + 1]).astype(BF16)

    last = jnp.logical_and(
        iota((64, 256), 0)
        == device_of(lax.shift_right_logical(lane_t, 5), lane_t & 7),
        slot == length - 1,
    )
    last = jnp.where(last, 1.0, 0.0).astype(BF16)

    def layer(x, k):
        normed = (x.T * prm[k : k + 1] + prm[2 + k : 3 + k]).astype(BF16)
        r.norm_t[...] = normed.astype(F32).T
        mine = r.norm_t[rows(q * 64, 64), :].astype(BF16)
        r.new_edges_o[k] = dot(last, mine, 1).astype(BF16)
        return normed

    x_stream.arrive()
    x_stats.arrive()
    mean, var = join(r.st_r, 64.0, 4096.0)
    scaled = (r.stream_r[...].astype(F32).reshape(512, 256) - mean) * lax.rsqrt(var + EPS_LN)
    mixed = shifted(layer(scaled, 0), 0, 4)
    x_maps.arrive()
    x_low.arrive()
    for n in range(5):
        w = r.maps_w[n] if n < 4 else r.low_w[...]
        r.part_s[n] = dot(mixed(n), w.reshape(512, 128)).astype(BF16)
    x_part = Exchange(gz, lambda i: r.part_s.at[:, rows(i * 32, 32)], slots(r.part_r), r.part_r, s.part)
    x_part.start()

    x_zstate.arrive()
    left = iota((32, 128), 1) < 64
    for n in range(8):
        tile = r.state_z[:, n].astype(F32).reshape(64, 128)
        turn = pltpu.roll(tile, 64, 1)
        blocks = [
            jnp.where(left, tile[0:32], 0.0),
            jnp.where(left, turn[0:32], 0.0),
            jnp.where(left, 0.0, turn[32:64]),
            jnp.where(left, 0.0, tile[32:64]),
        ]
        r.bd[n] = jnp.concatenate(blocks, axis=0).astype(BF16)
    lens8 = r.table[rows(z * 8, 8), :][:, 4:5].astype(jnp.int32)

    x_part.arrive()
    proj = jnp.sum(r.part_r[...].astype(F32), axis=0)
    low = jnp.tanh(proj[4]).astype(BF16)
    decay = jnp.exp(-jnp.exp(r.floor[pl.ds(q, 1), :] + dot(low, r.second[:, lanes(q * 128, 128)])))
    rec = [proj[0, 8 * j : 8 * j + 8] for j in range(4)]
    key = [proj[1, 8 * j : 8 * j + 8] for j in range(4)]
    val = [proj[2, 8 * j : 8 * j + 8] for j in range(4)]
    dec = [decay[8 * j : 8 * j + 8] for j in range(4)]
    bonus = r.bonus[pl.ds(q, 1), :]
    alive = [lens8 > j for j in range(4)]
    seen, inner = [], []
    for j in range(4):
        acc = head_sum(rec[j] * bonus * key[j]) * val[j]
        run = rec[j]
        for i in range(j - 1, -1, -1):
            acc = acc + head_sum(run * key[i]) * val[i]
            run = run * dec[i]
        seen.append(run)
        inner.append(acc)
    row_q = iota((32, 128), 0) & 7

    def spread(x):
        return jnp.concatenate([jnp.where(row_q == n, x, 0.0) for n in range(8)], axis=1)

    wide = spread(jnp.concatenate(seen, axis=0))
    high, rest = split(wide)
    bd = r.bd[...].reshape(1024, 128)
    wkv = dot(high, bd) + dot(rest, bd) + jnp.concatenate(inner, axis=0)
    mu = head_sum(wkv) * (1.0 / 64)
    dev = wkv - mu
    spr = head_sum(dev * dev) * (1.0 / 64)
    grouped = dev * lax.rsqrt(spr + EPS_GN) * r.gn_gain[pl.ds(q, 1), :] + r.gn_bias[pl.ds(q, 1), :]
    gate = proj[3]
    r.gated_s[...] = (grouped * (gate * jax.nn.sigmoid(gate))).astype(BF16)
    x_gated = Exchange(gz, same(r.gated_s), slots(r.gated_r), r.gated_r, s.gated)
    x_gated.start()

    tail, keys = jnp.ones((8, 128), F32), []
    for j in range(3, -1, -1):
        keys.append(jnp.where(alive[j], key[j] * tail, 0.0))
        tail = jnp.where(alive[j], tail * dec[j], tail)
    keys = spread(jnp.concatenate(keys[::-1], axis=0)).T
    vals = jnp.concatenate(val, axis=0)
    kh, kl = split(keys)
    vh, vl = split(vals)
    outer = dot(kh, vh) + dot(kl, vh) + dot(kh, vl)
    tail = tail.T
    for n in range(8):
        new = outer[n * 128 : n * 128 + 128] + tail[:, n : n + 1] * r.bd[n].astype(F32)
        turn = pltpu.roll(new, 64, 1)
        top = jnp.where(left, new[0:32], turn[32:64])
        bottom = jnp.where(left, turn[64:96], new[96:128])
        r.new_s[n] = jnp.concatenate([top, bottom], axis=0).astype(BF16)
    x_new = Exchange(gq, lambda i: r.new_s.at[i], lambda m: r.states_o.at[m], r.states_o, s.new)
    x_new.start()

    x_emit.arrive()
    x_gated.arrive()
    att = dot(r.emit_w[...].reshape(512, 128), r.gated_r[...].reshape(256, 128), 1)
    r.att_s[...] = att.astype(BF16).reshape(8, 64, 256)
    x_att = Exchange(gq, lambda i: r.att_s.at[i], slots(r.att_r), r.att_r, s.att)
    x_att.start()
    x_att.arrive()
    r.attx_s[...] = jnp.sum(r.att_r[...].astype(F32), axis=0).astype(BF16)
    x_attx = Exchange(gx, same(r.attx_s), slots(r.attx_r), r.attx_r, s.attx)
    x_attx.start()
    x_attx.arrive()
    two = r.blk[...].astype(F32) + jnp.sum(r.attx_r[...].astype(F32), axis=0)
    r.two[...] = two
    r.dev_s[...] = block_stats(two, r.st2).astype(BF16)
    x_dev = Exchange(gq, same(r.dev_s), slots(r.dev_r), r.dev_r, s.dev2)
    x_dev.start()
    x_stats2 = Exchange(gb, same(r.st2), slots(r.st2_r), r.st2_r, s.stats2)
    x_stats2.start()
    x_dev.arrive()
    x_stats2.arrive()
    mean, var = join(r.st2_r, 64.0, 4096.0)
    scale = lax.rsqrt(var + EPS_LN)
    blocks = []
    for n in range(8):
        off = r.st2_r[batch_of(n // 2, z, n % 2)][0:1] - mean
        blocks.append((r.dev_r[n].astype(F32) + off) * scale)
    mixed = shifted(layer(jnp.concatenate(blocks, axis=0), 1), 1, 9)

    x_look.arrive()
    x_acc.arrive()
    up = dot(mixed(0), r.look_w[...].reshape(512, 512))
    r.up_s[...] = up.astype(BF16).reshape(8, 32, 512)
    x_up = Exchange(gz, lambda i: r.up_s.at[i], slots(r.up_r), r.up_r, s.up)
    x_up.start()
    rec = dot(mixed(1), r.acc_w[...].reshape(512, 128)).T
    r.rec_s[...] = rec.astype(BF16).reshape(8, 16, 256)
    x_rec = Exchange(gz, lambda i: r.rec_s.at[i], slots(r.rec_r), r.rec_r, s.rec)
    x_rec.start()
    x_up.arrive()
    up = jnp.maximum(jnp.sum(r.up_r[...].astype(F32), axis=0), 0.0)
    up = jnp.where(jnp.logical_and(c == 1, iota(up.shape, 1) < 128), 0.0, up * up)
    r.units_s[...] = up.astype(BF16)
    x_units = Exchange(gz, same(r.units_s), slots(r.units_r), r.units_r, s.units)
    x_units.start()
    x_rec.arrive()
    r.sig_s[...] = jax.nn.sigmoid(jnp.sum(r.rec_r[...].astype(F32), axis=0))

    def far_copy(k):
        return pltpu.make_async_remote_copy(
            src_ref=r.sig_s,
            dst_ref=r.sig_r.at[lax.rem(z, NX)],
            send_sem=s.sig.at[0],
            recv_sem=s.sig.at[1],
            device_id=dest(k),
            device_id_type=MESH,
        )

    for k in range(4):
        here = jnp.logical_and(dest_here, h == k)

        @pl.when(jnp.logical_not(here))
        def _():
            far_copy(k).start()

        @pl.when(here)
        def _():
            pltpu.make_async_copy(r.sig_s, r.sig_r.at[lax.rem(z, NX)], s.sig.at[1]).start()

    x_down.arrive()
    x_units.arrive()
    val = dot(r.down_w[...].reshape(512, 512), r.units_r[...].reshape(256, 512), 1)
    r.val_s[...] = val.astype(BF16).reshape(8, 64, 256)
    x_val = Exchange(gq, lambda i: r.val_s.at[i], slots(r.val_r), r.val_r, s.val)
    x_val.start()
    x_val.arrive()
    r.valx_s[...] = jnp.sum(r.val_r[...].astype(F32), axis=0).astype(BF16)
    x_valx = Exchange(gx, same(r.valx_s), slots(r.valx_r), r.valx_r, s.valx)
    x_valx.start()
    pltpu.make_async_copy(r.sig_r, r.sig_r, s.sig.at[1]).wait()
    x_valx.arrive()
    value = jnp.sum(r.valx_r[...].astype(F32), axis=0)
    result = r.two[...] + r.sig_r[...].reshape(64, 256) * value
    r.hidden_o[...] = jnp.where(slot < length, result, 0.0).T

    x_new.arrive()
    for k in range(4):

        @pl.when(jnp.logical_not(jnp.logical_and(dest_here, h == k)))
        def _():
            far_copy(k).wait_send()

    for x in (
        x_meta, x_prm, x_edges, x_state, x_low, x_maps, x_emit, x_look, x_acc, x_down, x_emb, x_zstate, x_stream,
        x_stats, x_part, x_gated, x_new, x_att, x_attx, x_dev, x_stats2, x_up, x_rec, x_units, x_val, x_valx,
    ):
        x.drain()


def local(
    query_symbol_numbers,
    alive_span_sizes,
    former_positions,
    previous_normed_vectors,
    memory_matrices,
    vocabulary_vectors,
    standardize_scales,
    standardize_shifts,
    timemix_blend_factors,
    timemix_linear_maps,
    forgetting_first_lowrank,
    forgetting_second_lowrank,
    forgetting_loglog_floor,
    current_reward_factor,
    perspan_standardize_scale,
    perspan_standardize_shift,
    timemix_emit_matrix,
    feedforward_blend_factors,
    feedforward_lookup_matrix,
    feedforward_accept_matrix,
    feedforward_emit_matrix,
):
    edges = (
        previous_normed_vectors.reshape(2, NY, NZ, 128).transpose(2, 0, 1, 3).reshape(NZ, 8, 128)
    )
    state = memory_matrices.reshape(16, 2, 32, 64).transpose(0, 2, 1, 3).reshape(64, 8, 128)
    spaces = {
        "S": pl.BlockSpec(memory_space=pltpu.SMEM),
        "V": VM,
        "A": ANY,
    }
    hidden, new_edges, states = pl.pallas_call(
        kernel,
        out_shape=[
            jax.ShapeDtypeStruct((256, 64), F32),
            jax.ShapeDtypeStruct((2, 64, 64), BF16),
            jax.ShapeDtypeStruct((8, 64, 128), BF16),
        ],
        in_specs=[spaces[k] for k in SPACES],
        out_specs=[VM] * 3,
        scratch_shapes=[pltpu.VMEM(shape, dtype) for _, shape, dtype in SCRATCH]
        + [DMA((2,)) for _ in SEMS]
        + [DMA((2,)), DMA(()), DMA(()), pltpu.SMEM((64, 1, 128), jnp.int32)],
        compiler_params=pltpu.CompilerParams(
            collective_id=0, has_side_effects=True, vmem_limit_bytes=48 << 20
        ),
        name="layer",
    )(
        query_symbol_numbers,
        alive_span_sizes,
        former_positions,
        standardize_scales,
        standardize_shifts,
        timemix_blend_factors,
        feedforward_blend_factors,
        edges,
        state,
        forgetting_first_lowrank,
        timemix_linear_maps,
        timemix_emit_matrix,
        feedforward_lookup_matrix,
        feedforward_accept_matrix,
        feedforward_emit_matrix,
        vocabulary_vectors,
        forgetting_second_lowrank,
        forgetting_loglog_floor.reshape(8, 128),
        current_reward_factor.reshape(8, 128),
        perspan_standardize_scale.reshape(8, 128),
        perspan_standardize_shift.reshape(8, 128),
    )
    hidden = hidden.reshape(NZ, 4, NY, NC, 64).transpose(2, 0, 3, 1, 4).reshape(64, 4, 64)
    states = states.reshape(16, 32, 2, 64).transpose(0, 2, 1, 3).reshape(1, 16, 64, 64)
    return hidden, new_edges, states


def solution(mesh):
    return jax.shard_map(
        local,
        mesh=mesh,
        in_specs=(
            P("batch", None),
            P("batch"),
            P("batch"),
            P(None, "batch", None),
            P("batch", "head", None, None),
            P("batch", "head"),
            P(None, "batch"),
            P(None, "batch"),
            P(None, "batch"),
            P(None, "batch", "head"),
            P("batch", None),
            P(None, "head"),
            P("head"),
            P("head"),
            P("head"),
            P("head"),
            P("batch", "head"),
            P(None, "batch"),
            P("batch", "head"),
            P("batch", None),
            P("batch", "head"),
        ),
        out_specs=(P(None, None, "batch"), P(None, None, "batch"), P("batch", "head", None, None)),
        check_vma=False,
    )
```

```python
import jax
import jax.numpy as jnp
from jax import lax
from jax.experimental import pallas as pl
from jax.experimental.pallas import tpu as pltpu
from jax.sharding import PartitionSpec as P

F32 = jnp.float32
BF16 = jnp.bfloat16
MESH = pl.DeviceIdType.MESH
EPS_LN = 1e-05
EPS_GN = 0.00064
NX, NY, NZ, NC = 4, 4, 8, 2
NQ = NY * NC
VM = pl.BlockSpec(memory_space=pltpu.VMEM)
ANY = pl.BlockSpec(memory_space=pl.ANY)
DMA = pltpu.SemaphoreType.DMA


def batch_of(y, z, c):
    return (y * NZ + z) * NC + c


def place():
    h = lax.axis_index("head")
    b = lax.axis_index("batch")
    c = lax.rem(b, NC)
    z = lax.rem(lax.div(b, NC), NZ)
    y = lax.div(b, NC * NZ)
    return h, b, y, z, c, y * NC + c


class Group:
    def __init__(self, kind):
        h, b, y, z, c, q = place()
        if kind == "z":
            self.me, self.n = z, NZ
            self.dev = lambda i: (h, batch_of(y, i, c))
        elif kind == "q":
            self.me, self.n = q, NQ
            self.dev = lambda i: (h, batch_of(lax.div(i, NC), z, lax.rem(i, NC)))
        elif kind == "x":
            self.me, self.n = h, NX
            self.dev = lambda i: (i, b)
        elif kind == "b":
            self.me, self.n = b, NY * NZ * NC
            self.dev = lambda i: (h, i)
        else:
            self.me, self.n = q * NX + h, NQ * NX

            def dev(i):
                k = lax.div(i, NX)
                return (lax.rem(i, NX), batch_of(lax.div(k, NC), z, lax.rem(k, NC)))

            self.dev = dev

    def each(self, body):
        def step(p, carry):
            body(p, lax.rem(self.me + p, self.n))
            return carry

        lax.fori_loop(1, self.n, step, 0)


def barrier(*groups):
    sem = pltpu.get_barrier_semaphore()
    for g in groups:
        g.each(
            lambda p, i: pl.semaphore_signal(
                sem, inc=1, device_id=g.dev(i), device_id_type=MESH
            )
        )
    pl.semaphore_wait(sem, sum(g.n - 1 for g in groups))


class Exchange:
    def __init__(self, group, src, dst, whole, sems):
        self.g, self.src, self.dst, self.whole, self.sems = group, src, dst, whole, sems

    def copy(self, i):
        return pltpu.make_async_remote_copy(
            src_ref=self.src(i),
            dst_ref=self.dst(self.g.me),
            send_sem=self.sems.at[0],
            recv_sem=self.sems.at[1],
            device_id=self.g.dev(i),
            device_id_type=MESH,
        )

    def start(self):
        self.g.each(lambda p, i: self.copy(i).start())
        pltpu.make_async_copy(self.src(self.g.me), self.dst(self.g.me), self.sems.at[1]).start()

    def arrive(self):
        pltpu.make_async_copy(self.whole, self.whole, self.sems.at[1]).wait()

    def drain(self):
        part = self.dst(pl.ds(0, self.g.n - 1))
        pltpu.make_async_copy(part, part, self.sems.at[0]).wait()


def lanes(i, n):
    return pl.ds(pl.multiple_of(i, 128), n)


def rows(i, n):
    return pl.ds(pl.multiple_of(i, n), n)


def chunk_start(i):
    return (7 * lax.div(i, 2) + 3 * lax.rem(i, 2)) * 128


def iota(shape, axis):
    return lax.broadcasted_iota(jnp.int32, shape, axis)


def dot(a, b, cb=0):
    return lax.dot_general(a, b, (((1,), (cb,)), ((), ())), preferred_element_type=F32)


def head_sum(x):
    left = iota(x.shape, 1) < 64
    a = jnp.sum(jnp.where(left, x, 0.0), axis=1, keepdims=True)
    b = jnp.sum(jnp.where(left, 0.0, x), axis=1, keepdims=True)
    return jnp.where(left, a, b)


def split(x):
    high = x.astype(BF16)
    return high, (x - high.astype(F32)).astype(BF16)


def join(stats, per, count):
    blocks = stats[...]
    total = jnp.sum(blocks, axis=0)
    mean = total[0:1] * (1.0 / blocks.shape[0])
    dev = blocks - mean[None]
    between = jnp.sum(dev * dev, axis=0)[0:1]
    return mean, (total[1:2] + per * between) * (1.0 / count)


def block_stats(x, st):
    mean = jnp.sum(x, axis=0, keepdims=True) * (1.0 / x.shape[0])
    dev = x - mean
    st[0:1, :] = mean
    st[1:2, :] = jnp.sum(dev * dev, axis=0, keepdims=True)
    return dev


INPUTS = [
    "ids", "lens", "pos", "gains", "biases", "mixes", "mixes2", "edges", "state", "low", "maps",
    "emit", "look", "acc", "down", "vocab", "second", "floor", "bonus", "gn_gain", "gn_bias",
]
LOCAL = [
    "ids", "lens", "pos", "gains", "biases", "mixes", "mixes2", "edges", "state", "second",
    "floor", "bonus", "gn_gain", "gn_bias",
]
LOCAL_SHAPES = [
    ((1, 4), jnp.int32),
    ((1,), jnp.int32),
    ((1,), jnp.int32),
    ((2, 64), F32),
    ((2, 64), F32),
    ((5, 64), F32),
    ((2, 64), F32),
    ((2, 4096), BF16),
    ((16, 64, 64), BF16),
    ((128, 128), BF16),
    ((8, 128), F32),
    ((8, 128), F32),
    ((8, 128), F32),
    ((8, 128), F32),
]
OUTPUTS = ["hidden", "new_edges", "states"]
SCRATCH = [
    ("meta_s", (1, 128), jnp.int32),
    ("meta_r", (64, 1, 128), jnp.int32),
    ("prm_s", (16, 128), F32),
    ("prm_r", (8, 16, 128), F32),
    ("edges_s", (8, 8, 128), BF16),
    ("edges_r", (64, 8, 128), BF16),
    ("state_p", (64, 8, 128), BF16),
    ("state_n", (8, 64, 128), BF16),
    ("out", (256, 64), F32),
    ("edges_f", (64, 8, 128), F32),
    ("state_r", (64, 8, 128), BF16),
    ("state_s", (64, 8, 128), BF16),
    ("state_z", (8, 8, 8, 128), BF16),
    ("low_w", (8, 64, 128), BF16),
    ("maps_w", (4, 8, 64, 128), BF16),
    ("emit_w", (8, 64, 128), BF16),
    ("look_w", (8, 64, 512), BF16),
    ("acc_w", (8, 64, 128), BF16),
    ("down_w", (8, 64, 512), BF16),
    ("vocab_w", (64, 16384), BF16),
    ("table", (64, 128), F32),
    ("emb_s", (64, 256), BF16),
    ("emb_r", (NX, 64, 256), BF16),
    ("blk", (64, 256), BF16),
    ("st", (2, 256), F32),
    ("st_r", (64, 2, 256), F32),
    ("stream_r", (8, 64, 256), BF16),
    ("part_s", (5, 256, 128), BF16),
    ("part_r", (8, 5, 32, 128), BF16),
    ("bd", (8, 128, 128), BF16),
    ("gated_s", (32, 128), BF16),
    ("gated_r", (8, 32, 128), BF16),
    ("new_s", (8, 64, 128), BF16),
    ("att_s", (8, 64, 256), BF16),
    ("att_r", (8, 64, 256), BF16),
    ("attx_s", (64, 256), BF16),
    ("attx_r", (NX, 64, 256), BF16),
    ("two", (64, 256), F32),
    ("dev_s", (64, 256), BF16),
    ("st2", (2, 256), F32),
    ("st2_r", (64, 2, 256), F32),
    ("dev_r", (8, 64, 256), BF16),
    ("up_s", (8, 32, 512), BF16),
    ("up_r", (8, 32, 512), BF16),
    ("rec_s", (8, 16, 256), BF16),
    ("rec_r", (8, 16, 256), BF16),
    ("units_s", (32, 512), BF16),
    ("units_r", (8, 32, 512), BF16),
    ("sig_s", (16, 256), F32),
    ("sig_r", (4, 16, 256), F32),
    ("val_s", (8, 64, 256), BF16),
    ("val_r", (8, 64, 256), BF16),
    ("valx_s", (64, 256), BF16),
    ("valx_r", (NX, 64, 256), BF16),
    ("norm_t", (512, 256), F32),
]
SEMS = [
    "meta", "prm", "edges", "state", "zstate", "low", "maps", "emit", "look", "acc", "down", "emb",
    "stats", "stream", "part", "gated", "new", "att", "attx", "stats2", "dev2", "up", "rec",
    "units", "val", "valx",
]


class Refs:
    pass


def kernel(*refs):
    r, s = Refs(), Refs()
    names = INPUTS + OUTPUTS + [n for n, _, _ in SCRATCH]
    refs, meta_m = refs[:-1], refs[-1]
    refs, fetched = refs[: -len(LOCAL)], refs[-len(LOCAL) :]
    for name, ref in zip(names, refs):
        setattr(r, name + ("_o" if name in OUTPUTS else ""), ref)
    for name, ref in zip(SEMS + ["sig", "vocab", "smem", "local"], refs[len(names) :]):
        setattr(s, name, ref)
    h, b, y, z, c, q = place()
    gb, gq, gx, gz = Group("b"), Group("q"), Group("x"), Group("z")

    dest = lambda k: (k, batch_of(y, 2 * h + c, lax.div(z, NX)))
    source = lambda k: (lax.div(z, 2), batch_of(y, c * NX + k, lax.rem(z, 2)))
    dest_here = dest(0)[1] == b

    sem = pltpu.get_barrier_semaphore()
    for g in (gb, gx):
        g.each(
            lambda p, i: pl.semaphore_signal(sem, inc=1, device_id=g.dev(i), device_id_type=MESH)
        )
    for k in range(4):
        far = source(k)

        @pl.when(jnp.logical_and(far[0] != h, far[1] != b))
        def _():
            pl.semaphore_signal(sem, inc=1, device_id=far, device_id_type=MESH)

    fetch = {}
    for n, (name, ref) in enumerate(zip(LOCAL, fetched)):
        whole = getattr(r, name)
        if name == "second":
            whole = whole.at[:, lanes(q * 128, 128)]
        fetch[name] = pltpu.make_async_copy(whole, ref, s.local.at[n])
        fetch[name].start()
        setattr(r, name, ref)
    vocab_in = pltpu.make_async_copy(r.vocab, r.vocab_w, s.vocab)
    vocab_in.start()
    for name in LOCAL[:7]:
        fetch[name].wait()
    lane = iota((1, 128), 1)
    meta = jnp.where(lane == 4, r.lens[0], jnp.where(lane == 5, r.pos[0], 0))
    for j in range(4):
        meta = jnp.where(lane == j, r.ids[0, j], meta)
    r.meta_s[...] = meta
    r.prm_s[...] = jnp.zeros((16, 128), F32)
    r.prm_s[0:2, 0:64] = r.gains[...]
    r.prm_s[2:4, 0:64] = r.biases[...]
    r.prm_s[4:9, 0:64] = r.mixes[...]
    r.prm_s[9:11, 0:64] = r.mixes2[...]
    prm = r.prm_s[...]
    r.prm_s[...] = jnp.where(c == 0, prm, pltpu.roll(prm, 64, 1))

    fetch["edges"].wait()
    old = r.edges[...].astype(F32)
    for k in range(NZ):
        tiles = [old[:, (i * NZ + k) * 128 : (i * NZ + k) * 128 + 128] for i in range(NY)]
        r.edges_s[k] = jnp.concatenate(tiles, axis=0).astype(BF16)
    fetch["state"].wait()
    for k in range(16):
        tile = r.state[k].astype(F32)
        tile = jnp.concatenate([tile[0:32], tile[32:64]], axis=1).astype(BF16)
        for i in range(4):
            r.state_p[k * 4 + i] = tile[i * 8 : i * 8 + 8]

    pl.semaphore_wait(sem, gb.n - 1 + gx.n - 1 + 3 * (1 - dest_here.astype(jnp.int32)))

    def same(ref):
        return lambda i: ref

    def slots(ref):
        return lambda m: ref.at[m]

    x_meta = Exchange(gb, same(r.meta_s), slots(r.meta_r), r.meta_r, s.meta)
    x_prm = Exchange(gq, same(r.prm_s), slots(r.prm_r), r.prm_r, s.prm)
    x_edges = Exchange(
        gb, lambda i: r.edges_s.at[lax.rem(lax.div(i, NC), NZ)], slots(r.edges_r), r.edges_r, s.edges
    )
    x_state = Exchange(
        gb,
        lambda i: r.state_p.at[
            (lax.div(i, NC * NZ) * NC + lax.rem(i, NC)) * NZ + lax.rem(lax.div(i, NC), NZ)
        ],
        slots(r.state_r),
        r.state_r,
        s.state,
    )
    x_low = Exchange(gq, same(r.low), slots(r.low_w), r.low_w, s.low)
    x_maps = Exchange(
        gq,
        lambda i: r.maps.at[:, :, lanes(i * 128, 128)],
        lambda m: r.maps_w.at[:, m],
        r.maps_w,
        s.maps,
    )
    x_emit = Exchange(gq, lambda i: r.emit.at[:, lanes(i * 128, 128)], slots(r.emit_w), r.emit_w, s.emit)
    x_look = Exchange(
        gq, lambda i: r.look.at[:, lanes(chunk_start(i), 512)], slots(r.look_w), r.look_w, s.look
    )
    x_acc = Exchange(
        gq,
        lambda i: r.acc.at[:, lanes((lax.div(i, NC) * NZ + 2 * h + lax.rem(i, NC)) * 128, 128)],
        slots(r.acc_w),
        r.acc_w,
        s.acc,
    )
    x_down = Exchange(
        gq, lambda i: r.down.at[:, lanes(chunk_start(i), 512)], slots(r.down_w), r.down_w, s.down
    )
    for x in (x_meta, x_maps, x_low, x_prm, x_edges):
        x.start()

    x_meta.arrive()
    to_smem = pltpu.make_async_copy(r.meta_r, meta_m, s.smem)
    to_smem.start()
    meta = r.meta_r[...].reshape(64, 128)
    high = lax.shift_right_logical(meta, 8)
    lowb = (meta - high * 256).astype(F32).astype(BF16)
    high = high.astype(F32).astype(BF16)

    def device_of(zz, qq):
        return (lax.shift_right_logical(qq, 1) * NZ + zz) * NC + (qq & 1)

    tok = iota((256, 64), 0)
    by_tok = device_of(lax.shift_right_logical(tok, 5), tok & 7) == iota((256, 64), 1)
    by_tok = jnp.where(by_tok, 1.0, 0.0).astype(BF16)
    cols = dot(by_tok, high) * 256.0 + dot(by_tok, lowb)
    req = iota((64, 64), 0)
    by_req = device_of(lax.shift_right_logical(req, 3), req & 7) == iota((64, 64), 1)
    by_req = jnp.where(by_req, 1.0, 0.0).astype(BF16)
    r.table[...] = dot(by_req, lowb)
    tok_rows = cols.T
    lane_t = iota((1, 256), 1)
    slot = lax.shift_right_logical(lane_t, 3) & 3
    ids = tok_rows[0:1]
    for j in range(1, 4):
        ids = jnp.where(slot == j, tok_rows[j : j + 1], ids)
    ids = ids.astype(jnp.int32) - h * 16384
    length = tok_rows[4:5].astype(jnp.int32)

    vocab_in.wait()
    step = 4096

    def look_up(k, acc):
        base = pl.multiple_of(k * step, step)
        hot = jnp.where(iota((step, 256), 0) == ids - base, 1.0, 0.0).astype(BF16)
        return acc + dot(r.vocab_w[:, pl.ds(base, step)], hot)

    emb = lax.fori_loop(0, 16384 // step, look_up, jnp.zeros((64, 256), F32))
    r.emb_s[...] = emb.astype(BF16)
    x_emb = Exchange(gx, same(r.emb_s), slots(r.emb_r), r.emb_r, s.emb)
    x_emb.start()
    x_state.start()

    x_emb.arrive()
    own = jnp.sum(r.emb_r[...].astype(F32), axis=0)
    r.blk[...] = own.astype(BF16)
    x_stream = Exchange(gq, same(r.blk), slots(r.stream_r), r.stream_r, s.stream)
    x_stream.start()
    block_stats(own, r.st)
    x_stats = Exchange(gb, same(r.st), slots(r.st_r), r.st_r, s.stats)
    x_stats.start()

    x_edges.arrive()
    x_state.arrive()
    to_smem.wait()

    def reorder(n, carry):
        zz = lax.div(n, 8)
        qq = lax.rem(n, 8)
        old = meta_m[batch_of(lax.div(qq, 2), zz, lax.rem(qq, 2)), 0, 5]
        r.edges_f[n] = r.edges_r[old].astype(F32)
        r.state_s[n] = r.state_r[old]
        return carry

    lax.fori_loop(0, 64, reorder, 0)
    x_zstate = Exchange(gz, lambda i: r.state_s.at[rows(i * 8, 8)], slots(r.state_z), r.state_z, s.zstate)
    x_zstate.start()

    x_prm.arrive()
    prm = jnp.concatenate([r.prm_r[2 * k] + r.prm_r[2 * k + 1] for k in range(NY)], axis=1)

    def shifted(normed, k, first):
        now = normed.astype(F32).reshape(8, 4, 8, 512)
        edge = jnp.concatenate([r.edges_f[:, i * 2 + k, :] for i in range(NY)], axis=1)
        before = jnp.concatenate([edge.reshape(8, 1, 8, 512), now[:, :3]], axis=1)
        delta = (before - now).reshape(256, 512)
        now = now.reshape(256, 512)
        return lambda n: (now + delta * prm[first + n : first + n + 1]).astype(BF16)

    last = jnp.logical_and(
        iota((64, 256), 0)
        == device_of(lax.shift_right_logical(lane_t, 5), lane_t & 7),
        slot == length - 1,
    )
    last = jnp.where(last, 1.0, 0.0).astype(BF16)

    def layer(x, k):
        normed = (x.T * prm[k : k + 1] + prm[2 + k : 3 + k]).astype(BF16)
        r.norm_t[...] = normed.astype(F32).T
        mine = r.norm_t[rows(q * 64, 64), :].astype(BF16)
        r.new_edges_o[k] = dot(last, mine, 1).astype(BF16)
        return normed

    x_stream.arrive()
    x_stats.arrive()
    mean, var = join(r.st_r, 64.0, 4096.0)
    scaled = (r.stream_r[...].astype(F32).reshape(512, 256) - mean) * lax.rsqrt(var + EPS_LN)
    mixed = shifted(layer(scaled, 0), 0, 4)
    x_maps.arrive()
    x_low.arrive()
    for n in range(5):
        w = r.maps_w[n] if n < 4 else r.low_w[...]
        r.part_s[n] = dot(mixed(n), w.reshape(512, 128)).astype(BF16)
    x_part = Exchange(gz, lambda i: r.part_s.at[:, rows(i * 32, 32)], slots(r.part_r), r.part_r, s.part)
    x_part.start()
    for x in (x_emit, x_look, x_acc, x_down):
        x.start()

    x_zstate.arrive()
    left = iota((32, 128), 1) < 64
    for n in range(8):
        tile = r.state_z[:, n].astype(F32).reshape(64, 128)
        turn = pltpu.roll(tile, 64, 1)
        blocks = [
            jnp.where(left, tile[0:32], 0.0),
            jnp.where(left, turn[0:32], 0.0),
            jnp.where(left, 0.0, turn[32:64]),
            jnp.where(left, 0.0, tile[32:64]),
        ]
        r.bd[n] = jnp.concatenate(blocks, axis=0).astype(BF16)
    lens8 = r.table[rows(z * 8, 8), :][:, 4:5].astype(jnp.int32)

    x_part.arrive()
    proj = jnp.sum(r.part_r[...].astype(F32), axis=0)
    for name in LOCAL[9:]:
        fetch[name].wait()
    low = jnp.tanh(proj[4]).astype(BF16)
    decay = jnp.exp(-jnp.exp(r.floor[pl.ds(q, 1), :] + dot(low, r.second[...])))
    rec = [proj[0, 8 * j : 8 * j + 8] for j in range(4)]
    key = [proj[1, 8 * j : 8 * j + 8] for j in range(4)]
    val = [proj[2, 8 * j : 8 * j + 8] for j in range(4)]
    dec = [decay[8 * j : 8 * j + 8] for j in range(4)]
    bonus = r.bonus[pl.ds(q, 1), :]
    alive = [lens8 > j for j in range(4)]
    seen, inner = [], []
    for j in range(4):
        acc = head_sum(rec[j] * bonus * key[j]) * val[j]
        run = rec[j]
        for i in range(j - 1, -1, -1):
            acc = acc + head_sum(run * key[i]) * val[i]
            run = run * dec[i]
        seen.append(run)
        inner.append(acc)
    row_q = iota((32, 128), 0) & 7

    def spread(x):
        return jnp.concatenate([jnp.where(row_q == n, x, 0.0) for n in range(8)], axis=1)

    wide = spread(jnp.concatenate(seen, axis=0))
    high, rest = split(wide)
    bd = r.bd[...].reshape(1024, 128)
    wkv = dot(high, bd) + dot(rest, bd) + jnp.concatenate(inner, axis=0)
    mu = head_sum(wkv) * (1.0 / 64)
    dev = wkv - mu
    spr = head_sum(dev * dev) * (1.0 / 64)
    grouped = dev * lax.rsqrt(spr + EPS_GN) * r.gn_gain[pl.ds(q, 1), :] + r.gn_bias[pl.ds(q, 1), :]
    gate = proj[3]
    r.gated_s[...] = (grouped * (gate * jax.nn.sigmoid(gate))).astype(BF16)
    x_gated = Exchange(gz, same(r.gated_s), slots(r.gated_r), r.gated_r, s.gated)
    x_gated.start()

    tail, keys = jnp.ones((8, 128), F32), []
    for j in range(3, -1, -1):
        keys.append(jnp.where(alive[j], key[j] * tail, 0.0))
        tail = jnp.where(alive[j], tail * dec[j], tail)
    keys = spread(jnp.concatenate(keys[::-1], axis=0)).T
    vals = jnp.concatenate(val, axis=0)
    kh, kl = split(keys)
    vh, vl = split(vals)
    outer = dot(kh, vh) + dot(kl, vh) + dot(kh, vl)
    tail = tail.T
    for n in range(8):
        new = outer[n * 128 : n * 128 + 128] + tail[:, n : n + 1] * r.bd[n].astype(F32)
        turn = pltpu.roll(new, 64, 1)
        top = jnp.where(left, new[0:32], turn[32:64])
        bottom = jnp.where(left, turn[64:96], new[96:128])
        r.new_s[n] = jnp.concatenate([top, bottom], axis=0).astype(BF16)
    x_new = Exchange(gq, lambda i: r.new_s.at[i], lambda m: r.state_n.at[m], r.state_n, s.new)
    x_new.start()

    x_emit.arrive()
    x_gated.arrive()
    att = dot(r.emit_w[...].reshape(512, 128), r.gated_r[...].reshape(256, 128), 1)
    r.att_s[...] = att.astype(BF16).reshape(8, 64, 256)
    x_att = Exchange(gq, lambda i: r.att_s.at[i], slots(r.att_r), r.att_r, s.att)
    x_att.start()
    x_att.arrive()
    r.attx_s[...] = jnp.sum(r.att_r[...].astype(F32), axis=0).astype(BF16)
    x_attx = Exchange(gx, same(r.attx_s), slots(r.attx_r), r.attx_r, s.attx)
    x_attx.start()
    x_attx.arrive()
    two = r.blk[...].astype(F32) + jnp.sum(r.attx_r[...].astype(F32), axis=0)
    r.two[...] = two
    r.dev_s[...] = block_stats(two, r.st2).astype(BF16)
    x_dev = Exchange(gq, same(r.dev_s), slots(r.dev_r), r.dev_r, s.dev2)
    x_dev.start()
    x_stats2 = Exchange(gb, same(r.st2), slots(r.st2_r), r.st2_r, s.stats2)
    x_stats2.start()
    x_dev.arrive()
    x_stats2.arrive()
    mean, var = join(r.st2_r, 64.0, 4096.0)
    scale = lax.rsqrt(var + EPS_LN)
    blocks = []
    for n in range(8):
        off = r.st2_r[batch_of(n // 2, z, n % 2)][0:1] - mean
        blocks.append((r.dev_r[n].astype(F32) + off) * scale)
    mixed = shifted(layer(jnp.concatenate(blocks, axis=0), 1), 1, 9)

    x_look.arrive()
    x_acc.arrive()
    up = dot(mixed(0), r.look_w[...].reshape(512, 512))
    r.up_s[...] = up.astype(BF16).reshape(8, 32, 512)
    x_up = Exchange(gz, lambda i: r.up_s.at[i], slots(r.up_r), r.up_r, s.up)
    x_up.start()
    rec = dot(mixed(1), r.acc_w[...].reshape(512, 128)).T
    r.rec_s[...] = rec.astype(BF16).reshape(8, 16, 256)
    x_rec = Exchange(gz, lambda i: r.rec_s.at[i], slots(r.rec_r), r.rec_r, s.rec)
    x_rec.start()
    x_up.arrive()
    up = jnp.maximum(jnp.sum(r.up_r[...].astype(F32), axis=0), 0.0)
    up = jnp.where(jnp.logical_and(c == 1, iota(up.shape, 1) < 128), 0.0, up * up)
    r.units_s[...] = up.astype(BF16)
    x_units = Exchange(gz, same(r.units_s), slots(r.units_r), r.units_r, s.units)
    x_units.start()
    x_rec.arrive()
    r.sig_s[...] = jax.nn.sigmoid(jnp.sum(r.rec_r[...].astype(F32), axis=0))

    def far_copy(k):
        return pltpu.make_async_remote_copy(
            src_ref=r.sig_s,
            dst_ref=r.sig_r.at[lax.rem(z, NX)],
            send_sem=s.sig.at[0],
            recv_sem=s.sig.at[1],
            device_id=dest(k),
            device_id_type=MESH,
        )

    for k in range(4):
        here = jnp.logical_and(dest_here, h == k)

        @pl.when(jnp.logical_not(here))
        def _():
            far_copy(k).start()

        @pl.when(here)
        def _():
            pltpu.make_async_copy(r.sig_s, r.sig_r.at[lax.rem(z, NX)], s.sig.at[1]).start()

    x_down.arrive()
    x_units.arrive()
    val = dot(r.down_w[...].reshape(512, 512), r.units_r[...].reshape(256, 512), 1)
    r.val_s[...] = val.astype(BF16).reshape(8, 64, 256)
    x_val = Exchange(gq, lambda i: r.val_s.at[i], slots(r.val_r), r.val_r, s.val)
    x_val.start()
    x_new.arrive()
    for k in range(16):
        tile = r.state_n[k // 2].astype(F32)[(k % 2) * 32 : (k % 2) * 32 + 32]
        r.states_o[k, 0:32] = tile[:, 0:64].astype(BF16)
        r.states_o[k, 32:64] = tile[:, 64:128].astype(BF16)
    x_val.arrive()
    r.valx_s[...] = jnp.sum(r.val_r[...].astype(F32), axis=0).astype(BF16)
    x_valx = Exchange(gx, same(r.valx_s), slots(r.valx_r), r.valx_r, s.valx)
    x_valx.start()
    pltpu.make_async_copy(r.sig_r, r.sig_r, s.sig.at[1]).wait()
    x_valx.arrive()
    value = jnp.sum(r.valx_r[...].astype(F32), axis=0)
    result = r.two[...] + r.sig_r[...].reshape(64, 256) * value
    r.out[...] = jnp.where(slot < length, result, 0.0).T
    for k in range(64):
        first = (k // 2 % NZ) * 32 + (k // 16) * 2 + k % 2
        r.hidden_o[k] = r.out[pl.ds(first, 4, stride=8), :]

    for k in range(4):

        @pl.when(jnp.logical_not(jnp.logical_and(dest_here, h == k)))
        def _():
            far_copy(k).wait_send()

    for x in (
        x_meta, x_prm, x_edges, x_state, x_low, x_maps, x_emit, x_look, x_acc, x_down, x_emb, x_zstate, x_stream,
        x_stats, x_part, x_gated, x_new, x_att, x_attx, x_dev, x_stats2, x_up, x_rec, x_units, x_val, x_valx,
    ):
        x.drain()


def local(
    query_symbol_numbers,
    alive_span_sizes,
    former_positions,
    previous_normed_vectors,
    memory_matrices,
    vocabulary_vectors,
    standardize_scales,
    standardize_shifts,
    timemix_blend_factors,
    timemix_linear_maps,
    forgetting_first_lowrank,
    forgetting_second_lowrank,
    forgetting_loglog_floor,
    current_reward_factor,
    perspan_standardize_scale,
    perspan_standardize_shift,
    timemix_emit_matrix,
    feedforward_blend_factors,
    feedforward_lookup_matrix,
    feedforward_accept_matrix,
    feedforward_emit_matrix,
):
    hidden, new_edges, states = pl.pallas_call(
        kernel,
        out_shape=[
            jax.ShapeDtypeStruct((64, 4, 64), F32),
            jax.ShapeDtypeStruct((2, 64, 64), BF16),
            jax.ShapeDtypeStruct((16, 64, 64), BF16),
        ],
        in_specs=[ANY] * len(INPUTS),
        out_specs=[VM] * 3,
        scratch_shapes=[pltpu.VMEM(shape, dtype) for _, shape, dtype in SCRATCH]
        + [DMA((2,)) for _ in SEMS]
        + [DMA((2,)), DMA(()), DMA(()), DMA((len(LOCAL),))]
        + [
            (pltpu.SMEM if n < 3 else pltpu.VMEM)(shape, dtype)
            for n, (shape, dtype) in enumerate(LOCAL_SHAPES)
        ]
        + [pltpu.SMEM((64, 1, 128), jnp.int32)],
        compiler_params=pltpu.CompilerParams(
            collective_id=0, has_side_effects=True, vmem_limit_bytes=67043328
        ),
        name="layer",
    )(
        query_symbol_numbers,
        alive_span_sizes,
        former_positions,
        standardize_scales,
        standardize_shifts,
        timemix_blend_factors,
        feedforward_blend_factors,
        previous_normed_vectors.reshape(2, 4096),
        memory_matrices.reshape(16, 64, 64),
        forgetting_first_lowrank,
        timemix_linear_maps,
        timemix_emit_matrix,
        feedforward_lookup_matrix,
        feedforward_accept_matrix,
        feedforward_emit_matrix,
        vocabulary_vectors,
        forgetting_second_lowrank,
        forgetting_loglog_floor.reshape(8, 128),
        current_reward_factor.reshape(8, 128),
        perspan_standardize_scale.reshape(8, 128),
        perspan_standardize_shift.reshape(8, 128),
    )
    return hidden, new_edges, states.reshape(1, 16, 64, 64)


def solution(mesh):
    return jax.shard_map(
        local,
        mesh=mesh,
        in_specs=(
            P("batch", None),
            P("batch"),
            P("batch"),
            P(None, "batch", None),
            P("batch", "head", None, None),
            P("batch", "head"),
            P(None, "batch"),
            P(None, "batch"),
            P(None, "batch"),
            P(None, "batch", "head"),
            P("batch", None),
            P(None, "head"),
            P("head"),
            P("head"),
            P("head"),
            P("head"),
            P("batch", "head"),
            P(None, "batch"),
            P("batch", "head"),
            P("batch", None),
            P("batch", "head"),
        ),
        out_specs=(P(None, None, "batch"), P(None, None, "batch"), P("batch", "head", None, None)),
        check_vma=False,
    )
```

```python
import jax
import jax.numpy as jnp
from jax import lax
from jax.experimental import pallas as pl
from jax.experimental.pallas import tpu as pltpu
from jax.sharding import PartitionSpec as P

F32 = jnp.float32
BF16 = jnp.bfloat16
MESH = pl.DeviceIdType.MESH
EPS_LN = 1e-05
EPS_GN = 0.00064
NX, NY, NZ, NC = 4, 4, 8, 2
NQ = NY * NC
VM = pl.BlockSpec(memory_space=pltpu.VMEM)
ANY = pl.BlockSpec(memory_space=pl.ANY)
DMA = pltpu.SemaphoreType.DMA


def batch_of(y, z, c):
    return (y * NZ + z) * NC + c


def place():
    h = lax.axis_index("head")
    b = lax.axis_index("batch")
    c = lax.rem(b, NC)
    z = lax.rem(lax.div(b, NC), NZ)
    y = lax.div(b, NC * NZ)
    return h, b, y, z, c, y * NC + c


class Group:
    def __init__(self, kind):
        h, b, y, z, c, q = place()
        if kind == "z":
            self.me, self.n = z, NZ
            self.dev = lambda i: (h, batch_of(y, i, c))
        elif kind == "q":
            self.me, self.n = q, NQ
            self.dev = lambda i: (h, batch_of(lax.div(i, NC), z, lax.rem(i, NC)))
        elif kind == "x":
            self.me, self.n = h, NX
            self.dev = lambda i: (i, b)
        elif kind == "b":
            self.me, self.n = b, NY * NZ * NC
            self.dev = lambda i: (h, i)
        else:
            self.me, self.n = q * NX + h, NQ * NX

            def dev(i):
                k = lax.div(i, NX)
                return (lax.rem(i, NX), batch_of(lax.div(k, NC), z, lax.rem(k, NC)))

            self.dev = dev

    def each(self, body):
        def step(p, carry):
            body(p, lax.rem(self.me + p, self.n))
            return carry

        lax.fori_loop(1, self.n, step, 0)


def barrier(*groups):
    sem = pltpu.get_barrier_semaphore()
    for g in groups:
        g.each(
            lambda p, i: pl.semaphore_signal(
                sem, inc=1, device_id=g.dev(i), device_id_type=MESH
            )
        )
    pl.semaphore_wait(sem, sum(g.n - 1 for g in groups))


class Exchange:
    def __init__(self, group, src, dst, whole, sems):
        self.g, self.src, self.dst, self.whole, self.sems = group, src, dst, whole, sems

    def copy(self, i):
        return pltpu.make_async_remote_copy(
            src_ref=self.src(i),
            dst_ref=self.dst(self.g.me),
            send_sem=self.sems.at[0],
            recv_sem=self.sems.at[1],
            device_id=self.g.dev(i),
            device_id_type=MESH,
        )

    def start(self):
        self.g.each(lambda p, i: self.copy(i).start())
        pltpu.make_async_copy(self.src(self.g.me), self.dst(self.g.me), self.sems.at[1]).start()

    def arrive(self):
        pltpu.make_async_copy(self.whole, self.whole, self.sems.at[1]).wait()

    def drain(self):
        part = self.dst(pl.ds(0, self.g.n - 1))
        pltpu.make_async_copy(part, part, self.sems.at[0]).wait()


def lanes(i, n):
    return pl.ds(pl.multiple_of(i, 128), n)


def rows(i, n):
    return pl.ds(pl.multiple_of(i, n), n)


def chunk_start(i):
    return (7 * lax.div(i, 2) + 3 * lax.rem(i, 2)) * 128


def iota(shape, axis):
    return lax.broadcasted_iota(jnp.int32, shape, axis)


def dot(a, b, cb=0):
    return lax.dot_general(a, b, (((1,), (cb,)), ((), ())), preferred_element_type=F32)


def head_sum(x):
    left = iota(x.shape, 1) < 64
    a = jnp.sum(jnp.where(left, x, 0.0), axis=1, keepdims=True)
    b = jnp.sum(jnp.where(left, 0.0, x), axis=1, keepdims=True)
    return jnp.where(left, a, b)


def split(x):
    high = x.astype(BF16)
    return high, (x - high.astype(F32)).astype(BF16)


def join(stats, per, count):
    blocks = stats[...]
    total = jnp.sum(blocks, axis=0)
    mean = total[0:1] * (1.0 / blocks.shape[0])
    dev = blocks - mean[None]
    between = jnp.sum(dev * dev, axis=0)[0:1]
    return mean, (total[1:2] + per * between) * (1.0 / count)


def block_stats(x, st):
    mean = jnp.sum(x, axis=0, keepdims=True) * (1.0 / x.shape[0])
    dev = x - mean
    st[0:1, :] = mean
    st[1:2, :] = jnp.sum(dev * dev, axis=0, keepdims=True)
    return dev


INPUTS = [
    "ids", "lens", "pos", "gains", "biases", "mixes", "mixes2", "edges", "state", "low", "maps",
    "emit", "look", "acc", "down", "vocab", "second", "floor", "bonus", "gn_gain", "gn_bias",
]
LOCAL = [
    "ids", "lens", "pos", "gains", "biases", "mixes", "mixes2", "edges", "state", "second",
    "floor", "bonus", "gn_gain", "gn_bias",
]
LOCAL_SHAPES = [
    ((1, 4), jnp.int32),
    ((1,), jnp.int32),
    ((1,), jnp.int32),
    ((2, 64), F32),
    ((2, 64), F32),
    ((5, 64), F32),
    ((2, 64), F32),
    ((2, 4096), BF16),
    ((16, 64, 64), BF16),
    ((128, 128), BF16),
    ((8, 128), F32),
    ((8, 128), F32),
    ((8, 128), F32),
    ((8, 128), F32),
]
OUTPUTS = ["hidden", "new_edges", "states"]
SCRATCH = [
    ("meta_s", (1, 128), jnp.int32),
    ("meta_r", (64, 1, 128), jnp.int32),
    ("prm_s", (16, 128), F32),
    ("prm_r", (8, 16, 128), F32),
    ("edges_s", (8, 8, 128), BF16),
    ("edges_r", (64, 8, 128), BF16),
    ("state_p", (64, 8, 128), BF16),
    ("state_n", (8, 64, 128), BF16),
    ("out", (256, 64), F32),
    ("edges_f", (64, 8, 128), F32),
    ("state_r", (64, 8, 128), BF16),
    ("state_s", (64, 8, 128), BF16),
    ("state_z", (8, 8, 8, 128), BF16),
    ("low_w", (8, 64, 128), BF16),
    ("maps_w", (4, 8, 64, 128), BF16),
    ("emit_w", (8, 64, 128), BF16),
    ("look_w", (8, 64, 512), BF16),
    ("acc_w", (8, 64, 128), BF16),
    ("down_w", (8, 64, 512), BF16),
    ("vocab_w", (64, 16384), BF16),
    ("table", (64, 128), F32),
    ("emb_s", (64, 256), BF16),
    ("emb_r", (NX, 64, 256), BF16),
    ("blk", (64, 256), BF16),
    ("st", (2, 256), F32),
    ("st_r", (64, 2, 256), F32),
    ("stream_r", (8, 64, 256), BF16),
    ("part_s", (2, 5, 128, 128), BF16),
    ("part_r", (2, 8, 5, 16, 128), BF16),
    ("bd", (8, 128, 128), BF16),
    ("gated_s", (2, 16, 128), BF16),
    ("gated_r", (2, 8, 16, 128), BF16),
    ("new_s", (8, 64, 128), BF16),
    ("att_s", (2, 8, 64, 128), BF16),
    ("att_r", (2, 8, 64, 128), BF16),
    ("attx_s", (2, 64, 128), BF16),
    ("attx_r", (2, NX, 64, 128), BF16),
    ("two", (64, 256), F32),
    ("dev_s", (64, 256), BF16),
    ("st2", (2, 256), F32),
    ("st2_r", (64, 2, 256), F32),
    ("dev_r", (8, 64, 256), BF16),
    ("up_s", (2, 8, 16, 512), BF16),
    ("up_r", (2, 8, 16, 512), BF16),
    ("rec_s", (8, 16, 256), BF16),
    ("rec_r", (8, 16, 256), BF16),
    ("units_s", (2, 16, 512), BF16),
    ("units_r", (2, 8, 16, 512), BF16),
    ("sig_s", (16, 256), F32),
    ("sig_r", (4, 16, 256), F32),
    ("val_s", (2, 8, 64, 128), BF16),
    ("val_r", (2, 8, 64, 128), BF16),
    ("valx_s", (2, 64, 128), BF16),
    ("valx_r", (2, NX, 64, 128), BF16),
    ("norm_t", (512, 256), F32),
]
SEMS = [
    "meta", "prm", "edges", "state", "zstate", "low", "maps", "emit", "look", "acc", "down", "emb",
    "stats", "stream", "new", "stats2", "dev2", "rec",
]
HALVES = ["part", "gated", "att", "attx", "up", "units", "val", "valx"]


class Refs:
    pass


def kernel(*refs):
    r, s = Refs(), Refs()
    names = INPUTS + OUTPUTS + [n for n, _, _ in SCRATCH]
    refs, meta_m = refs[:-1], refs[-1]
    refs, fetched = refs[: -len(LOCAL)], refs[-len(LOCAL) :]
    for name, ref in zip(names, refs):
        setattr(r, name + ("_o" if name in OUTPUTS else ""), ref)
    for name, ref in zip(SEMS + HALVES + ["sig", "vocab", "smem", "local"], refs[len(names) :]):
        setattr(s, name, ref)
    h, b, y, z, c, q = place()
    gb, gq, gx, gz = Group("b"), Group("q"), Group("x"), Group("z")

    dest = lambda k: (k, batch_of(y, 2 * h + c, lax.div(z, NX)))
    source = lambda k: (lax.div(z, 2), batch_of(y, c * NX + k, lax.rem(z, 2)))
    dest_here = dest(0)[1] == b

    sem = pltpu.get_barrier_semaphore()
    for g in (gb, gx):
        g.each(
            lambda p, i: pl.semaphore_signal(sem, inc=1, device_id=g.dev(i), device_id_type=MESH)
        )
    for k in range(4):
        far = source(k)

        @pl.when(jnp.logical_and(far[0] != h, far[1] != b))
        def _():
            pl.semaphore_signal(sem, inc=1, device_id=far, device_id_type=MESH)

    fetch = {}
    for n, (name, ref) in enumerate(zip(LOCAL, fetched)):
        whole = getattr(r, name)
        if name == "second":
            whole = whole.at[:, lanes(q * 128, 128)]
        fetch[name] = pltpu.make_async_copy(whole, ref, s.local.at[n])
        fetch[name].start()
        setattr(r, name, ref)
    vocab_in = pltpu.make_async_copy(r.vocab, r.vocab_w, s.vocab)
    vocab_in.start()
    for name in LOCAL[:7]:
        fetch[name].wait()
    lane = iota((1, 128), 1)
    meta = jnp.where(lane == 4, r.lens[0], jnp.where(lane == 5, r.pos[0], 0))
    for j in range(4):
        meta = jnp.where(lane == j, r.ids[0, j], meta)
    r.meta_s[...] = meta
    r.prm_s[...] = jnp.zeros((16, 128), F32)
    r.prm_s[0:2, 0:64] = r.gains[...]
    r.prm_s[2:4, 0:64] = r.biases[...]
    r.prm_s[4:9, 0:64] = r.mixes[...]
    r.prm_s[9:11, 0:64] = r.mixes2[...]
    prm = r.prm_s[...]
    r.prm_s[...] = jnp.where(c == 0, prm, pltpu.roll(prm, 64, 1))

    fetch["edges"].wait()
    old = r.edges[...].astype(F32)
    for k in range(NZ):
        tiles = [old[:, (i * NZ + k) * 128 : (i * NZ + k) * 128 + 128] for i in range(NY)]
        r.edges_s[k] = jnp.concatenate(tiles, axis=0).astype(BF16)
    fetch["state"].wait()
    for k in range(16):
        tile = r.state[k].astype(F32)
        tile = jnp.concatenate([tile[0:32], tile[32:64]], axis=1).astype(BF16)
        for i in range(4):
            r.state_p[k * 4 + i] = tile[i * 8 : i * 8 + 8]

    pl.semaphore_wait(sem, gb.n - 1 + gx.n - 1 + 3 * (1 - dest_here.astype(jnp.int32)))

    def same(ref):
        return lambda i: ref

    def slots(ref):
        return lambda m: ref.at[m]

    x_meta = Exchange(gb, same(r.meta_s), slots(r.meta_r), r.meta_r, s.meta)
    x_prm = Exchange(gq, same(r.prm_s), slots(r.prm_r), r.prm_r, s.prm)
    x_edges = Exchange(
        gb, lambda i: r.edges_s.at[lax.rem(lax.div(i, NC), NZ)], slots(r.edges_r), r.edges_r, s.edges
    )
    x_state = Exchange(
        gb,
        lambda i: r.state_p.at[
            (lax.div(i, NC * NZ) * NC + lax.rem(i, NC)) * NZ + lax.rem(lax.div(i, NC), NZ)
        ],
        slots(r.state_r),
        r.state_r,
        s.state,
    )
    x_low = Exchange(gq, same(r.low), slots(r.low_w), r.low_w, s.low)
    x_maps = Exchange(
        gq,
        lambda i: r.maps.at[:, :, lanes(i * 128, 128)],
        lambda m: r.maps_w.at[:, m],
        r.maps_w,
        s.maps,
    )
    x_emit = Exchange(gq, lambda i: r.emit.at[:, lanes(i * 128, 128)], slots(r.emit_w), r.emit_w, s.emit)
    x_look = Exchange(
        gq, lambda i: r.look.at[:, lanes(chunk_start(i), 512)], slots(r.look_w), r.look_w, s.look
    )
    x_acc = Exchange(
        gq,
        lambda i: r.acc.at[:, lanes((lax.div(i, NC) * NZ + 2 * h + lax.rem(i, NC)) * 128, 128)],
        slots(r.acc_w),
        r.acc_w,
        s.acc,
    )
    x_down = Exchange(
        gq, lambda i: r.down.at[:, lanes(chunk_start(i), 512)], slots(r.down_w), r.down_w, s.down
    )
    for x in (x_meta, x_maps, x_low, x_prm, x_edges):
        x.start()

    x_meta.arrive()
    to_smem = pltpu.make_async_copy(r.meta_r, meta_m, s.smem)
    to_smem.start()
    meta = r.meta_r[...].reshape(64, 128)
    high = lax.shift_right_logical(meta, 8)
    lowb = (meta - high * 256).astype(F32).astype(BF16)
    high = high.astype(F32).astype(BF16)

    def device_of(zz, qq):
        return (lax.shift_right_logical(qq, 1) * NZ + zz) * NC + (qq & 1)

    tok = iota((256, 64), 0)
    by_tok = device_of(lax.shift_right_logical(tok, 4) & 7, tok & 7) == iota((256, 64), 1)
    by_tok = jnp.where(by_tok, 1.0, 0.0).astype(BF16)
    cols = dot(by_tok, high) * 256.0 + dot(by_tok, lowb)
    req = iota((64, 64), 0)
    by_req = device_of(lax.shift_right_logical(req, 3), req & 7) == iota((64, 64), 1)
    by_req = jnp.where(by_req, 1.0, 0.0).astype(BF16)
    r.table[...] = dot(by_req, lowb)
    tok_rows = cols.T
    lane_t = iota((1, 256), 1)
    slot = lax.shift_right_logical(lane_t, 7) * 2 + (lax.shift_right_logical(lane_t, 3) & 1)
    ids = tok_rows[0:1]
    for j in range(1, 4):
        ids = jnp.where(slot == j, tok_rows[j : j + 1], ids)
    ids = ids.astype(jnp.int32) - h * 16384
    length = tok_rows[4:5].astype(jnp.int32)

    vocab_in.wait()
    step = 4096

    def look_up(k, acc):
        base = pl.multiple_of(k * step, step)
        hot = jnp.where(iota((step, 256), 0) == ids - base, 1.0, 0.0).astype(BF16)
        return acc + dot(r.vocab_w[:, pl.ds(base, step)], hot)

    emb = lax.fori_loop(0, 16384 // step, look_up, jnp.zeros((64, 256), F32))
    r.emb_s[...] = emb.astype(BF16)
    x_emb = Exchange(gx, same(r.emb_s), slots(r.emb_r), r.emb_r, s.emb)
    x_emb.start()
    x_state.start()

    x_emb.arrive()
    own = jnp.sum(r.emb_r[...].astype(F32), axis=0)
    r.blk[...] = own.astype(BF16)
    x_stream = Exchange(gq, same(r.blk), slots(r.stream_r), r.stream_r, s.stream)
    x_stream.start()
    block_stats(own, r.st)
    x_stats = Exchange(gb, same(r.st), slots(r.st_r), r.st_r, s.stats)
    x_stats.start()

    x_edges.arrive()
    x_state.arrive()
    to_smem.wait()

    def reorder(n, carry):
        zz = lax.div(n, 8)
        qq = lax.rem(n, 8)
        old = meta_m[batch_of(lax.div(qq, 2), zz, lax.rem(qq, 2)), 0, 5]
        r.edges_f[n] = r.edges_r[old].astype(F32)
        r.state_s[n] = r.state_r[old]
        return carry

    lax.fori_loop(0, 64, reorder, 0)
    x_zstate = Exchange(gz, lambda i: r.state_s.at[rows(i * 8, 8)], slots(r.state_z), r.state_z, s.zstate)
    x_zstate.start()

    x_prm.arrive()
    prm = jnp.concatenate([r.prm_r[2 * k] + r.prm_r[2 * k + 1] for k in range(NY)], axis=1)

    def shifted(normed, k, first):
        now = normed.astype(F32).reshape(2, 8, 2, 8, 512)
        edge = jnp.concatenate([r.edges_f[:, i * 2 + k, :] for i in range(NY)], axis=1)
        before = [
            jnp.concatenate([edge.reshape(8, 1, 8, 512), now[0, :, :1]], axis=1).reshape(128, 512),
            jnp.concatenate([now[0, :, 1:], now[1, :, :1]], axis=1).reshape(128, 512),
        ]
        now = [now[k].reshape(128, 512) for k in range(2)]
        delta = [before[k] - now[k] for k in range(2)]
        return lambda n, k: (now[k] + delta[k] * prm[first + n : first + n + 1]).astype(BF16)

    def halves(group, name, src):
        got, sems = getattr(r, name + "_r"), getattr(s, name)
        return [
            Exchange(
                group,
                lambda i, k=k: src(k, i),
                lambda m, k=k: got.at[k, m],
                got.at[k],
                sems.at[k],
            )
            for k in range(2)
        ]

    last = jnp.logical_and(
        iota((64, 256), 0)
        == device_of(lax.shift_right_logical(lane_t, 4) & 7, lane_t & 7),
        slot == length - 1,
    )
    last = jnp.where(last, 1.0, 0.0).astype(BF16)

    def layer(x, k):
        normed = (x.T * prm[k : k + 1] + prm[2 + k : 3 + k]).astype(BF16)
        r.norm_t[...] = normed.astype(F32).T
        mine = r.norm_t[rows(q * 64, 64), :].astype(BF16)
        r.new_edges_o[k] = dot(last, mine, 1).astype(BF16)
        return normed

    x_stream.arrive()
    x_stats.arrive()
    mean, var = join(r.st_r, 64.0, 4096.0)
    scaled = (r.stream_r[...].astype(F32).reshape(512, 256) - mean) * lax.rsqrt(var + EPS_LN)
    mixed = shifted(layer(scaled, 0), 0, 4)
    x_maps.arrive()
    x_low.arrive()
    x_part = halves(gz, "part", lambda k, i: r.part_s.at[k, :, rows(i * 16, 16)])
    for k in range(2):
        for n in range(5):
            w = r.maps_w[n] if n < 4 else r.low_w[...]
            r.part_s[k, n] = dot(mixed(n, k), w.reshape(512, 128)).astype(BF16)
        x_part[k].start()
    for x in (x_emit, x_look, x_acc, x_down):
        x.start()

    x_zstate.arrive()
    left = iota((32, 128), 1) < 64
    for n in range(8):
        tile = r.state_z[:, n].astype(F32).reshape(64, 128)
        turn = pltpu.roll(tile, 64, 1)
        blocks = [
            jnp.where(left, tile[0:32], 0.0),
            jnp.where(left, turn[0:32], 0.0),
            jnp.where(left, 0.0, turn[32:64]),
            jnp.where(left, 0.0, tile[32:64]),
        ]
        r.bd[n] = jnp.concatenate(blocks, axis=0).astype(BF16)
    lens8 = r.table[rows(z * 8, 8), :][:, 4:5].astype(jnp.int32)

    for name in LOCAL[9:]:
        fetch[name].wait()
    floor, bonus, gn_gain, gn_bias = (
        ref[pl.ds(q, 1), :] for ref in (r.floor, r.bonus, r.gn_gain, r.gn_bias)
    )
    alive = [lens8 > j for j in range(4)]

    def spread(x):
        row_q = iota(x.shape, 0) & 7
        return jnp.concatenate([jnp.where(row_q == n, x, 0.0) for n in range(8)], axis=1)

    bd = r.bd[...].reshape(1024, 128)
    rec, key, val, dec = [], [], [], []
    x_gated = halves(gz, "gated", lambda k, i: r.gated_s.at[k])
    for k in range(2):
        x_part[k].arrive()
        proj = jnp.sum(r.part_r[k].astype(F32), axis=0)
        low = jnp.tanh(proj[4]).astype(BF16)
        decay = jnp.exp(-jnp.exp(floor + dot(low, r.second[...])))
        for j in range(2):
            rec.append(proj[0, 8 * j : 8 * j + 8])
            key.append(proj[1, 8 * j : 8 * j + 8])
            val.append(proj[2, 8 * j : 8 * j + 8])
            dec.append(decay[8 * j : 8 * j + 8])
        seen, inner = [], []
        for j in range(2 * k, 2 * k + 2):
            acc = head_sum(rec[j] * bonus * key[j]) * val[j]
            run = rec[j]
            for i in range(j - 1, -1, -1):
                acc = acc + head_sum(run * key[i]) * val[i]
                run = run * dec[i]
            seen.append(run)
            inner.append(acc)
        high, rest = split(spread(jnp.concatenate(seen, axis=0)))
        wkv = dot(high, bd) + dot(rest, bd) + jnp.concatenate(inner, axis=0)
        mu = head_sum(wkv) * (1.0 / 64)
        dev = wkv - mu
        spr = head_sum(dev * dev) * (1.0 / 64)
        grouped = dev * lax.rsqrt(spr + EPS_GN) * gn_gain + gn_bias
        gate = proj[3]
        r.gated_s[k] = (grouped * (gate * jax.nn.sigmoid(gate))).astype(BF16)
        x_gated[k].start()

    tail, keys = jnp.ones((8, 128), F32), []
    for j in range(3, -1, -1):
        keys.append(jnp.where(alive[j], key[j] * tail, 0.0))
        tail = jnp.where(alive[j], tail * dec[j], tail)
    keys = spread(jnp.concatenate(keys[::-1], axis=0)).T
    vals = jnp.concatenate(val, axis=0)
    kh, kl = split(keys)
    vh, vl = split(vals)
    outer = dot(kh, vh) + dot(kl, vh) + dot(kh, vl)
    tail = tail.T
    for n in range(8):
        new = outer[n * 128 : n * 128 + 128] + tail[:, n : n + 1] * r.bd[n].astype(F32)
        turn = pltpu.roll(new, 64, 1)
        top = jnp.where(left, new[0:32], turn[32:64])
        bottom = jnp.where(left, turn[64:96], new[96:128])
        r.new_s[n] = jnp.concatenate([top, bottom], axis=0).astype(BF16)
    x_new = Exchange(gq, lambda i: r.new_s.at[i], lambda m: r.state_n.at[m], r.state_n, s.new)
    x_new.start()

    x_emit.arrive()
    x_att = halves(gq, "att", lambda k, i: r.att_s.at[k, i])
    x_attx = halves(gx, "attx", lambda k, i: r.attx_s.at[k])
    for k in range(2):
        x_gated[k].arrive()
        att = dot(r.emit_w[...].reshape(512, 128), r.gated_r[k].reshape(128, 128), 1)
        r.att_s[k] = att.astype(BF16).reshape(8, 64, 128)
        x_att[k].start()
    for k in range(2):
        x_att[k].arrive()
        r.attx_s[k] = jnp.sum(r.att_r[k].astype(F32), axis=0).astype(BF16)
        x_attx[k].start()
    added = []
    for k in range(2):
        x_attx[k].arrive()
        added.append(jnp.sum(r.attx_r[k].astype(F32), axis=0))
    two = r.blk[...].astype(F32) + jnp.concatenate(added, axis=1)
    r.two[...] = two
    r.dev_s[...] = block_stats(two, r.st2).astype(BF16)
    x_dev = Exchange(gq, same(r.dev_s), slots(r.dev_r), r.dev_r, s.dev2)
    x_dev.start()
    x_stats2 = Exchange(gb, same(r.st2), slots(r.st2_r), r.st2_r, s.stats2)
    x_stats2.start()
    x_dev.arrive()
    x_stats2.arrive()
    mean, var = join(r.st2_r, 64.0, 4096.0)
    scale = lax.rsqrt(var + EPS_LN)
    blocks = []
    for n in range(8):
        off = r.st2_r[batch_of(n // 2, z, n % 2)][0:1] - mean
        blocks.append((r.dev_r[n].astype(F32) + off) * scale)
    mixed = shifted(layer(jnp.concatenate(blocks, axis=0), 1), 1, 9)

    x_look.arrive()
    x_acc.arrive()
    x_up = halves(gz, "up", lambda k, i: r.up_s.at[k, i])
    x_units = halves(gz, "units", lambda k, i: r.units_s.at[k])
    x_val = halves(gq, "val", lambda k, i: r.val_s.at[k, i])
    x_valx = halves(gx, "valx", lambda k, i: r.valx_s.at[k])
    for k in range(2):
        up = dot(mixed(0, k), r.look_w[...].reshape(512, 512))
        r.up_s[k] = up.astype(BF16).reshape(8, 16, 512)
        x_up[k].start()
    for k in range(2):
        x_up[k].arrive()
        up = jnp.maximum(jnp.sum(r.up_r[k].astype(F32), axis=0), 0.0)
        up = jnp.where(jnp.logical_and(c == 1, iota(up.shape, 1) < 128), 0.0, up * up)
        r.units_s[k] = up.astype(BF16)
        x_units[k].start()
    take = [dot(mixed(1, k), r.acc_w[...].reshape(512, 128)) for k in range(2)]
    take = jnp.concatenate(take, axis=0).T
    r.rec_s[...] = take.astype(BF16).reshape(8, 16, 256)
    x_rec = Exchange(gz, lambda i: r.rec_s.at[i], slots(r.rec_r), r.rec_r, s.rec)
    x_rec.start()
    x_down.arrive()
    for k in range(2):
        x_units[k].arrive()
        value = dot(r.down_w[...].reshape(512, 512), r.units_r[k].reshape(128, 512), 1)
        r.val_s[k] = value.astype(BF16).reshape(8, 64, 128)
        x_val[k].start()
    x_rec.arrive()
    r.sig_s[...] = jax.nn.sigmoid(jnp.sum(r.rec_r[...].astype(F32), axis=0))

    def far_copy(k):
        return pltpu.make_async_remote_copy(
            src_ref=r.sig_s,
            dst_ref=r.sig_r.at[lax.rem(z, NX)],
            send_sem=s.sig.at[0],
            recv_sem=s.sig.at[1],
            device_id=dest(k),
            device_id_type=MESH,
        )

    for k in range(4):
        here = jnp.logical_and(dest_here, h == k)

        @pl.when(jnp.logical_not(here))
        def _():
            far_copy(k).start()

        @pl.when(here)
        def _():
            pltpu.make_async_copy(r.sig_s, r.sig_r.at[lax.rem(z, NX)], s.sig.at[1]).start()

    x_new.arrive()
    for k in range(16):
        tile = r.state_n[k // 2].astype(F32)[(k % 2) * 32 : (k % 2) * 32 + 32]
        r.states_o[k, 0:32] = tile[:, 0:64].astype(BF16)
        r.states_o[k, 32:64] = tile[:, 64:128].astype(BF16)
    for k in range(2):
        x_val[k].arrive()
        r.valx_s[k] = jnp.sum(r.val_r[k].astype(F32), axis=0).astype(BF16)
        x_valx[k].start()
    pltpu.make_async_copy(r.sig_r, r.sig_r, s.sig.at[1]).wait()
    value = []
    for k in range(2):
        x_valx[k].arrive()
        value.append(jnp.sum(r.valx_r[k].astype(F32), axis=0))
    value = jnp.concatenate(value, axis=1)
    result = r.two[...] + r.sig_r[...].reshape(64, 256) * value
    r.out[...] = jnp.where(slot < length, result, 0.0).T
    for k in range(64):
        first = (k // 2 % NZ) * 16 + (k // 16) * 2 + k % 2
        r.hidden_o[k, 0:2] = r.out[pl.ds(first, 2, stride=8), :]
        r.hidden_o[k, 2:4] = r.out[pl.ds(first + 128, 2, stride=8), :]

    for k in range(4):

        @pl.when(jnp.logical_not(jnp.logical_and(dest_here, h == k)))
        def _():
            far_copy(k).wait_send()

    for x in (
        x_meta, x_prm, x_edges, x_state, x_low, x_maps, x_emit, x_look, x_acc, x_down, x_emb,
        x_zstate, x_stream, x_stats, x_new, x_dev, x_stats2, x_rec, *x_part, *x_gated, *x_att,
        *x_attx, *x_up, *x_units, *x_val, *x_valx,
    ):
        x.drain()


def local(
    query_symbol_numbers,
    alive_span_sizes,
    former_positions,
    previous_normed_vectors,
    memory_matrices,
    vocabulary_vectors,
    standardize_scales,
    standardize_shifts,
    timemix_blend_factors,
    timemix_linear_maps,
    forgetting_first_lowrank,
    forgetting_second_lowrank,
    forgetting_loglog_floor,
    current_reward_factor,
    perspan_standardize_scale,
    perspan_standardize_shift,
    timemix_emit_matrix,
    feedforward_blend_factors,
    feedforward_lookup_matrix,
    feedforward_accept_matrix,
    feedforward_emit_matrix,
):
    hidden, new_edges, states = pl.pallas_call(
        kernel,
        out_shape=[
            jax.ShapeDtypeStruct((64, 4, 64), F32),
            jax.ShapeDtypeStruct((2, 64, 64), BF16),
            jax.ShapeDtypeStruct((16, 64, 64), BF16),
        ],
        in_specs=[ANY] * len(INPUTS),
        out_specs=[VM] * 3,
        scratch_shapes=[pltpu.VMEM(shape, dtype) for _, shape, dtype in SCRATCH]
        + [DMA((2,)) for _ in SEMS]
        + [DMA((2, 2)) for _ in HALVES]
        + [DMA((2,)), DMA(()), DMA(()), DMA((len(LOCAL),))]
        + [
            (pltpu.SMEM if n < 3 else pltpu.VMEM)(shape, dtype)
            for n, (shape, dtype) in enumerate(LOCAL_SHAPES)
        ]
        + [pltpu.SMEM((64, 1, 128), jnp.int32)],
        compiler_params=pltpu.CompilerParams(
            collective_id=0, has_side_effects=True, vmem_limit_bytes=67043328
        ),
        name="layer",
    )(
        query_symbol_numbers,
        alive_span_sizes,
        former_positions,
        standardize_scales,
        standardize_shifts,
        timemix_blend_factors,
        feedforward_blend_factors,
        previous_normed_vectors.reshape(2, 4096),
        memory_matrices.reshape(16, 64, 64),
        forgetting_first_lowrank,
        timemix_linear_maps,
        timemix_emit_matrix,
        feedforward_lookup_matrix,
        feedforward_accept_matrix,
        feedforward_emit_matrix,
        vocabulary_vectors,
        forgetting_second_lowrank,
        forgetting_loglog_floor.reshape(8, 128),
        current_reward_factor.reshape(8, 128),
        perspan_standardize_scale.reshape(8, 128),
        perspan_standardize_shift.reshape(8, 128),
    )
    return hidden, new_edges, states.reshape(1, 16, 64, 64)


def solution(mesh):
    return jax.shard_map(
        local,
        mesh=mesh,
        in_specs=(
            P("batch", None),
            P("batch"),
            P("batch"),
            P(None, "batch", None),
            P("batch", "head", None, None),
            P("batch", "head"),
            P(None, "batch"),
            P(None, "batch"),
            P(None, "batch"),
            P(None, "batch", "head"),
            P("batch", None),
            P(None, "head"),
            P("head"),
            P("head"),
            P("head"),
            P("head"),
            P("batch", "head"),
            P(None, "batch"),
            P("batch", "head"),
            P("batch", None),
            P("batch", "head"),
        ),
        out_specs=(P(None, None, "batch"), P(None, None, "batch"), P("batch", "head", None, None)),
        check_vma=False,
    )
```

```python
import jax
import jax.numpy as jnp
from jax import lax
from jax.experimental import pallas as pl
from jax.experimental.pallas import tpu as pltpu
from jax.sharding import PartitionSpec as P

F32 = jnp.float32
BF16 = jnp.bfloat16
MESH = pl.DeviceIdType.MESH
EPS_LN = 1e-05
EPS_GN = 0.00064
NX, NY, NZ, NC = 4, 4, 8, 2
NQ = NY * NC
VM = pl.BlockSpec(memory_space=pltpu.VMEM)
ANY = pl.BlockSpec(memory_space=pl.ANY)
DMA = pltpu.SemaphoreType.DMA


def batch_of(y, z, c):
    return (y * NZ + z) * NC + c


def place():
    h = lax.axis_index("head")
    b = lax.axis_index("batch")
    c = lax.rem(b, NC)
    z = lax.rem(lax.div(b, NC), NZ)
    y = lax.div(b, NC * NZ)
    return h, b, y, z, c, y * NC + c


class Group:
    def __init__(self, kind):
        h, b, y, z, c, q = place()
        if kind == "z":
            self.me, self.n = z, NZ
            self.dev = lambda i: (h, batch_of(y, i, c))
        elif kind == "q":
            self.me, self.n = q, NQ
            self.dev = lambda i: (h, batch_of(lax.div(i, NC), z, lax.rem(i, NC)))
        elif kind == "x":
            self.me, self.n = h, NX
            self.dev = lambda i: (i, b)
        elif kind == "b":
            self.me, self.n = b, NY * NZ * NC
            self.dev = lambda i: (h, i)
        else:
            self.me, self.n = q * NX + h, NQ * NX

            def dev(i):
                k = lax.div(i, NX)
                return (lax.rem(i, NX), batch_of(lax.div(k, NC), z, lax.rem(k, NC)))

            self.dev = dev

    def each(self, body):
        def step(p, carry):
            body(p, lax.rem(self.me + p, self.n))
            return carry

        lax.fori_loop(1, self.n, step, 0)


def barrier(*groups):
    sem = pltpu.get_barrier_semaphore()
    for g in groups:
        g.each(
            lambda p, i: pl.semaphore_signal(
                sem, inc=1, device_id=g.dev(i), device_id_type=MESH
            )
        )
    pl.semaphore_wait(sem, sum(g.n - 1 for g in groups))


class Exchange:
    def __init__(self, group, src, dst, whole, sems):
        self.g, self.src, self.dst, self.whole, self.sems = group, src, dst, whole, sems

    def copy(self, i):
        return pltpu.make_async_remote_copy(
            src_ref=self.src(i),
            dst_ref=self.dst(self.g.me),
            send_sem=self.sems.at[0],
            recv_sem=self.sems.at[1],
            device_id=self.g.dev(i),
            device_id_type=MESH,
        )

    def start(self):
        self.g.each(lambda p, i: self.copy(i).start())
        pltpu.make_async_copy(self.src(self.g.me), self.dst(self.g.me), self.sems.at[1]).start()

    def arrive(self):
        pltpu.make_async_copy(self.whole, self.whole, self.sems.at[1]).wait()

    def drain(self):
        part = self.dst(pl.ds(0, self.g.n - 1))
        pltpu.make_async_copy(part, part, self.sems.at[0]).wait()


def lanes(i, n):
    return pl.ds(pl.multiple_of(i, 128), n)


def rows(i, n):
    return pl.ds(pl.multiple_of(i, n), n)


def chunk_start(i):
    return (7 * lax.div(i, 2) + 3 * lax.rem(i, 2)) * 128


def iota(shape, axis):
    return lax.broadcasted_iota(jnp.int32, shape, axis)


def dot(a, b, cb=0):
    return lax.dot_general(a, b, (((1,), (cb,)), ((), ())), preferred_element_type=F32)


def head_sum(x):
    left = iota(x.shape, 1) < 64
    a = jnp.sum(jnp.where(left, x, 0.0), axis=1, keepdims=True)
    b = jnp.sum(jnp.where(left, 0.0, x), axis=1, keepdims=True)
    return jnp.where(left, a, b)


def split(x):
    high = x.astype(BF16)
    return high, (x - high.astype(F32)).astype(BF16)


def join(stats, per, count):
    blocks = stats[...]
    total = jnp.sum(blocks, axis=0)
    mean = total[0:1] * (1.0 / blocks.shape[0])
    dev = blocks - mean[None]
    between = jnp.sum(dev * dev, axis=0)[0:1]
    return mean, (total[1:2] + per * between) * (1.0 / count)


def block_stats(x, st):
    mean = jnp.sum(x, axis=0, keepdims=True) * (1.0 / x.shape[0])
    dev = x - mean
    st[0:1, :] = mean
    st[1:2, :] = jnp.sum(dev * dev, axis=0, keepdims=True)
    return dev


INPUTS = [
    "ids", "lens", "pos", "gains", "biases", "mixes", "mixes2", "edges", "state", "low", "maps",
    "emit", "look", "acc", "down", "vocab", "second", "floor", "bonus", "gn_gain", "gn_bias",
]
LOCAL = [
    "ids", "lens", "pos", "gains", "biases", "mixes", "mixes2", "edges", "state", "second",
    "floor", "bonus", "gn_gain", "gn_bias",
]
LOCAL_SHAPES = [
    ((1, 4), jnp.int32),
    ((1,), jnp.int32),
    ((1,), jnp.int32),
    ((2, 64), F32),
    ((2, 64), F32),
    ((5, 64), F32),
    ((2, 64), F32),
    ((2, 4096), BF16),
    ((16, 64, 64), BF16),
    ((128, 128), BF16),
    ((8, 128), F32),
    ((8, 128), F32),
    ((8, 128), F32),
    ((8, 128), F32),
]
OUTPUTS = ["hidden", "new_edges", "states"]
SCRATCH = [
    ("meta_s", (1, 128), jnp.int32),
    ("meta_r", (64, 1, 128), jnp.int32),
    ("prm_s", (16, 128), F32),
    ("prm_r", (8, 16, 128), F32),
    ("edges_s", (8, 8, 128), BF16),
    ("edges_r", (64, 8, 128), BF16),
    ("state_p", (64, 8, 128), BF16),
    ("state_n", (8, 64, 128), BF16),
    ("out", (256, 64), F32),
    ("edges_f", (64, 8, 128), F32),
    ("state_r", (64, 8, 128), BF16),
    ("state_s", (64, 8, 128), BF16),
    ("state_z", (8, 8, 8, 128), BF16),
    ("low_w", (8, 64, 128), BF16),
    ("maps_w", (4, 8, 64, 128), BF16),
    ("emit_w", (8, 64, 128), BF16),
    ("look_w", (8, 64, 512), BF16),
    ("acc_w", (8, 64, 128), BF16),
    ("down_w", (8, 64, 512), BF16),
    ("vocab_w", (64, 16384), BF16),
    ("table", (64, 128), F32),
    ("emb_s", (64, 256), BF16),
    ("emb_r", (NX, 64, 256), BF16),
    ("blk", (64, 256), BF16),
    ("st", (2, 256), F32),
    ("st_r", (64, 2, 256), F32),
    ("stream_r", (8, 64, 256), BF16),
    ("part_s", (2, 5, 128, 128), BF16),
    ("part_r", (2, 8, 5, 16, 128), BF16),
    ("bd", (8, 128, 128), BF16),
    ("gated_s", (2, 16, 128), BF16),
    ("gated_r", (2, 8, 16, 128), BF16),
    ("new_s", (8, 64, 128), BF16),
    ("att_s", (2, 8, 64, 128), BF16),
    ("att_r", (2, 8, 64, 128), BF16),
    ("attx_s", (2, 64, 128), BF16),
    ("attx_r", (2, NX, 64, 128), BF16),
    ("two", (64, 256), F32),
    ("dev2_s", (2, 64, 128), BF16),
    ("stats2_s", (2, 2, 128), F32),
    ("stats2_r", (2, 64, 2, 128), F32),
    ("dev2_r", (2, 8, 64, 128), BF16),
    ("up_s", (2, 8, 16, 512), BF16),
    ("up_r", (2, 8, 16, 512), BF16),
    ("rec_s", (8, 16, 256), BF16),
    ("rec_r", (8, 16, 256), BF16),
    ("units_s", (2, 16, 512), BF16),
    ("units_r", (2, 8, 16, 512), BF16),
    ("sig_s", (16, 256), F32),
    ("sig_r", (4, 16, 256), F32),
    ("val_s", (2, 8, 64, 128), BF16),
    ("val_r", (2, 8, 64, 128), BF16),
    ("valx_s", (2, 64, 128), BF16),
    ("valx_r", (2, NX, 64, 128), BF16),
    ("norm_t", (512, 256), F32),
]
SEMS = [
    "meta", "prm", "edges", "state", "zstate", "low", "maps", "emit", "look", "acc", "down", "emb",
    "stats", "stream", "new", "rec",
]
HALVES = [
    "part", "gated", "att", "attx", "dev2", "stats2", "up", "units", "val", "valx",
]


class Refs:
    pass


def kernel(*refs):
    r, s = Refs(), Refs()
    names = INPUTS + OUTPUTS + [n for n, _, _ in SCRATCH]
    refs, meta_m = refs[:-1], refs[-1]
    refs, fetched = refs[: -len(LOCAL)], refs[-len(LOCAL) :]
    for name, ref in zip(names, refs):
        setattr(r, name + ("_o" if name in OUTPUTS else ""), ref)
    for name, ref in zip(SEMS + HALVES + ["sig", "vocab", "smem", "local"], refs[len(names) :]):
        setattr(s, name, ref)
    h, b, y, z, c, q = place()
    gb, gq, gx, gz = Group("b"), Group("q"), Group("x"), Group("z")

    dest = lambda k: (k, batch_of(y, 2 * h + c, lax.div(z, NX)))
    source = lambda k: (lax.div(z, 2), batch_of(y, c * NX + k, lax.rem(z, 2)))
    dest_here = dest(0)[1] == b

    sem = pltpu.get_barrier_semaphore()
    for g in (gb, gx):
        g.each(
            lambda p, i: pl.semaphore_signal(sem, inc=1, device_id=g.dev(i), device_id_type=MESH)
        )
    for k in range(4):
        far = source(k)

        @pl.when(jnp.logical_and(far[0] != h, far[1] != b))
        def _():
            pl.semaphore_signal(sem, inc=1, device_id=far, device_id_type=MESH)

    fetch = {}
    for n, (name, ref) in enumerate(zip(LOCAL, fetched)):
        whole = getattr(r, name)
        if name == "second":
            whole = whole.at[:, lanes(q * 128, 128)]
        fetch[name] = pltpu.make_async_copy(whole, ref, s.local.at[n])
        fetch[name].start()
        setattr(r, name, ref)
    vocab_in = pltpu.make_async_copy(r.vocab, r.vocab_w, s.vocab)
    vocab_in.start()
    for name in LOCAL[:7]:
        fetch[name].wait()
    lane = iota((1, 128), 1)
    meta = jnp.where(lane == 4, r.lens[0], jnp.where(lane == 5, r.pos[0], 0))
    for j in range(4):
        meta = jnp.where(lane == j, r.ids[0, j], meta)
    r.meta_s[...] = meta
    r.prm_s[...] = jnp.zeros((16, 128), F32)
    r.prm_s[0:2, 0:64] = r.gains[...]
    r.prm_s[2:4, 0:64] = r.biases[...]
    r.prm_s[4:9, 0:64] = r.mixes[...]
    r.prm_s[9:11, 0:64] = r.mixes2[...]
    prm = r.prm_s[...]
    r.prm_s[...] = jnp.where(c == 0, prm, pltpu.roll(prm, 64, 1))

    fetch["edges"].wait()
    old = r.edges[...].astype(F32)
    for k in range(NZ):
        tiles = [old[:, (i * NZ + k) * 128 : (i * NZ + k) * 128 + 128] for i in range(NY)]
        r.edges_s[k] = jnp.concatenate(tiles, axis=0).astype(BF16)
    fetch["state"].wait()
    for k in range(16):
        tile = r.state[k].astype(F32)
        tile = jnp.concatenate([tile[0:32], tile[32:64]], axis=1).astype(BF16)
        for i in range(4):
            r.state_p[k * 4 + i] = tile[i * 8 : i * 8 + 8]

    pl.semaphore_wait(sem, gb.n - 1 + gx.n - 1 + 3 * (1 - dest_here.astype(jnp.int32)))

    def same(ref):
        return lambda i: ref

    def slots(ref):
        return lambda m: ref.at[m]

    x_meta = Exchange(gb, same(r.meta_s), slots(r.meta_r), r.meta_r, s.meta)
    x_prm = Exchange(gq, same(r.prm_s), slots(r.prm_r), r.prm_r, s.prm)
    x_edges = Exchange(
        gb, lambda i: r.edges_s.at[lax.rem(lax.div(i, NC), NZ)], slots(r.edges_r), r.edges_r, s.edges
    )
    x_state = Exchange(
        gb,
        lambda i: r.state_p.at[
            (lax.div(i, NC * NZ) * NC + lax.rem(i, NC)) * NZ + lax.rem(lax.div(i, NC), NZ)
        ],
        slots(r.state_r),
        r.state_r,
        s.state,
    )
    x_low = Exchange(gq, same(r.low), slots(r.low_w), r.low_w, s.low)
    x_maps = Exchange(
        gq,
        lambda i: r.maps.at[:, :, lanes(i * 128, 128)],
        lambda m: r.maps_w.at[:, m],
        r.maps_w,
        s.maps,
    )
    x_emit = Exchange(gq, lambda i: r.emit.at[:, lanes(i * 128, 128)], slots(r.emit_w), r.emit_w, s.emit)
    x_look = Exchange(
        gq, lambda i: r.look.at[:, lanes(chunk_start(i), 512)], slots(r.look_w), r.look_w, s.look
    )
    x_acc = Exchange(
        gq,
        lambda i: r.acc.at[:, lanes((lax.div(i, NC) * NZ + 2 * h + lax.rem(i, NC)) * 128, 128)],
        slots(r.acc_w),
        r.acc_w,
        s.acc,
    )
    x_down = Exchange(
        gq, lambda i: r.down.at[:, lanes(chunk_start(i), 512)], slots(r.down_w), r.down_w, s.down
    )
    for x in (x_meta, x_maps, x_low, x_prm, x_edges):
        x.start()

    x_meta.arrive()
    to_smem = pltpu.make_async_copy(r.meta_r, meta_m, s.smem)
    to_smem.start()
    meta = r.meta_r[...].reshape(64, 128)
    high = lax.shift_right_logical(meta, 8)
    lowb = (meta - high * 256).astype(F32).astype(BF16)
    high = high.astype(F32).astype(BF16)

    def device_of(zz, qq):
        return (lax.shift_right_logical(qq, 1) * NZ + zz) * NC + (qq & 1)

    tok = iota((256, 64), 0)
    by_tok = device_of(lax.shift_right_logical(tok, 4) & 7, tok & 7) == iota((256, 64), 1)
    by_tok = jnp.where(by_tok, 1.0, 0.0).astype(BF16)
    cols = dot(by_tok, high) * 256.0 + dot(by_tok, lowb)
    req = iota((64, 64), 0)
    by_req = device_of(lax.shift_right_logical(req, 3), req & 7) == iota((64, 64), 1)
    by_req = jnp.where(by_req, 1.0, 0.0).astype(BF16)
    r.table[...] = dot(by_req, lowb)
    tok_rows = cols.T
    lane_t = iota((1, 256), 1)
    slot = lax.shift_right_logical(lane_t, 7) * 2 + (lax.shift_right_logical(lane_t, 3) & 1)
    ids = tok_rows[0:1]
    for j in range(1, 4):
        ids = jnp.where(slot == j, tok_rows[j : j + 1], ids)
    ids = ids.astype(jnp.int32) - h * 16384
    length = tok_rows[4:5].astype(jnp.int32)

    vocab_in.wait()
    step = 4096

    def look_up(k, acc):
        base = pl.multiple_of(k * step, step)
        hot = jnp.where(iota((step, 256), 0) == ids - base, 1.0, 0.0).astype(BF16)
        return acc + dot(r.vocab_w[:, pl.ds(base, step)], hot)

    emb = lax.fori_loop(0, 16384 // step, look_up, jnp.zeros((64, 256), F32))
    r.emb_s[...] = emb.astype(BF16)
    x_emb = Exchange(gx, same(r.emb_s), slots(r.emb_r), r.emb_r, s.emb)
    x_emb.start()
    x_state.start()

    x_emb.arrive()
    own = jnp.sum(r.emb_r[...].astype(F32), axis=0)
    r.blk[...] = own.astype(BF16)
    x_stream = Exchange(gq, same(r.blk), slots(r.stream_r), r.stream_r, s.stream)
    x_stream.start()
    block_stats(own, r.st)
    x_stats = Exchange(gb, same(r.st), slots(r.st_r), r.st_r, s.stats)
    x_stats.start()

    x_edges.arrive()
    x_state.arrive()
    to_smem.wait()

    def reorder(n, carry):
        zz = lax.div(n, 8)
        qq = lax.rem(n, 8)
        old = meta_m[batch_of(lax.div(qq, 2), zz, lax.rem(qq, 2)), 0, 5]
        r.edges_f[n] = r.edges_r[old].astype(F32)
        r.state_s[n] = r.state_r[old]
        return carry

    lax.fori_loop(0, 64, reorder, 0)
    x_zstate = Exchange(gz, lambda i: r.state_s.at[rows(i * 8, 8)], slots(r.state_z), r.state_z, s.zstate)
    x_zstate.start()

    x_prm.arrive()
    prm = jnp.concatenate([r.prm_r[2 * k] + r.prm_r[2 * k + 1] for k in range(NY)], axis=1)

    def edge_rows(k):
        return jnp.concatenate([r.edges_f[:, i * 2 + k, :] for i in range(NY)], axis=1)

    def shifted(normed, k, first):
        now = normed.astype(F32).reshape(2, 8, 2, 8, 512)
        edge = edge_rows(k)
        before = [
            jnp.concatenate([edge.reshape(8, 1, 8, 512), now[0, :, :1]], axis=1).reshape(128, 512),
            jnp.concatenate([now[0, :, 1:], now[1, :, :1]], axis=1).reshape(128, 512),
        ]
        now = [now[k].reshape(128, 512) for k in range(2)]
        delta = [before[k] - now[k] for k in range(2)]
        return lambda n, k: (now[k] + delta[k] * prm[first + n : first + n + 1]).astype(BF16)

    def halves(group, name, src):
        got, sems = getattr(r, name + "_r"), getattr(s, name)
        return [
            Exchange(
                group,
                lambda i, k=k: src(k, i),
                lambda m, k=k: got.at[k, m],
                got.at[k],
                sems.at[k],
            )
            for k in range(2)
        ]

    last = jnp.logical_and(
        iota((64, 256), 0)
        == device_of(lax.shift_right_logical(lane_t, 4) & 7, lane_t & 7),
        slot == length - 1,
    )
    last = jnp.where(last, 1.0, 0.0).astype(BF16)

    def layer(x, k):
        normed = (x.T * prm[k : k + 1] + prm[2 + k : 3 + k]).astype(BF16)
        r.norm_t[...] = normed.astype(F32).T
        mine = r.norm_t[rows(q * 64, 64), :].astype(BF16)
        r.new_edges_o[k] = dot(last, mine, 1).astype(BF16)
        return normed

    x_stream.arrive()
    x_stats.arrive()
    mean, var = join(r.st_r, 64.0, 4096.0)
    scaled = (r.stream_r[...].astype(F32).reshape(512, 256) - mean) * lax.rsqrt(var + EPS_LN)
    mixed = shifted(layer(scaled, 0), 0, 4)
    x_maps.arrive()
    x_low.arrive()
    x_part = halves(gz, "part", lambda k, i: r.part_s.at[k, :, rows(i * 16, 16)])
    for k in range(2):
        for n in range(5):
            w = r.maps_w[n] if n < 4 else r.low_w[...]
            r.part_s[k, n] = dot(mixed(n, k), w.reshape(512, 128)).astype(BF16)
        x_part[k].start()
    for x in (x_emit, x_look, x_acc, x_down):
        x.start()

    x_zstate.arrive()
    left = iota((32, 128), 1) < 64
    for n in range(8):
        tile = r.state_z[:, n].astype(F32).reshape(64, 128)
        turn = pltpu.roll(tile, 64, 1)
        blocks = [
            jnp.where(left, tile[0:32], 0.0),
            jnp.where(left, turn[0:32], 0.0),
            jnp.where(left, 0.0, turn[32:64]),
            jnp.where(left, 0.0, tile[32:64]),
        ]
        r.bd[n] = jnp.concatenate(blocks, axis=0).astype(BF16)
    lens8 = r.table[rows(z * 8, 8), :][:, 4:5].astype(jnp.int32)

    for name in LOCAL[9:]:
        fetch[name].wait()
    floor, bonus, gn_gain, gn_bias = (
        ref[pl.ds(q, 1), :] for ref in (r.floor, r.bonus, r.gn_gain, r.gn_bias)
    )
    alive = [lens8 > j for j in range(4)]

    def spread(x):
        row_q = iota(x.shape, 0) & 7
        return jnp.concatenate([jnp.where(row_q == n, x, 0.0) for n in range(8)], axis=1)

    bd = r.bd[...].reshape(1024, 128)
    rec, key, val, dec = [], [], [], []
    x_gated = halves(gz, "gated", lambda k, i: r.gated_s.at[k])
    for k in range(2):
        x_part[k].arrive()
        proj = jnp.sum(r.part_r[k].astype(F32), axis=0)
        low = jnp.tanh(proj[4]).astype(BF16)
        decay = jnp.exp(-jnp.exp(floor + dot(low, r.second[...])))
        for j in range(2):
            rec.append(proj[0, 8 * j : 8 * j + 8])
            key.append(proj[1, 8 * j : 8 * j + 8])
            val.append(proj[2, 8 * j : 8 * j + 8])
            dec.append(decay[8 * j : 8 * j + 8])
        seen, inner = [], []
        for j in range(2 * k, 2 * k + 2):
            acc = head_sum(rec[j] * bonus * key[j]) * val[j]
            run = rec[j]
            for i in range(j - 1, -1, -1):
                acc = acc + head_sum(run * key[i]) * val[i]
                run = run * dec[i]
            seen.append(run)
            inner.append(acc)
        high, rest = split(spread(jnp.concatenate(seen, axis=0)))
        wkv = dot(high, bd) + dot(rest, bd) + jnp.concatenate(inner, axis=0)
        mu = head_sum(wkv) * (1.0 / 64)
        dev = wkv - mu
        spr = head_sum(dev * dev) * (1.0 / 64)
        grouped = dev * lax.rsqrt(spr + EPS_GN) * gn_gain + gn_bias
        gate = proj[3]
        r.gated_s[k] = (grouped * (gate * jax.nn.sigmoid(gate))).astype(BF16)
        x_gated[k].start()

    tail, keys = jnp.ones((8, 128), F32), []
    for j in range(3, -1, -1):
        keys.append(jnp.where(alive[j], key[j] * tail, 0.0))
        tail = jnp.where(alive[j], tail * dec[j], tail)
    keys = spread(jnp.concatenate(keys[::-1], axis=0)).T
    vals = jnp.concatenate(val, axis=0)
    kh, kl = split(keys)
    vh, vl = split(vals)
    outer = dot(kh, vh) + dot(kl, vh) + dot(kh, vl)
    tail = tail.T
    for n in range(8):
        new = outer[n * 128 : n * 128 + 128] + tail[:, n : n + 1] * r.bd[n].astype(F32)
        turn = pltpu.roll(new, 64, 1)
        top = jnp.where(left, new[0:32], turn[32:64])
        bottom = jnp.where(left, turn[64:96], new[96:128])
        r.new_s[n] = jnp.concatenate([top, bottom], axis=0).astype(BF16)
    x_new = Exchange(gq, lambda i: r.new_s.at[i], lambda m: r.state_n.at[m], r.state_n, s.new)
    x_new.start()

    x_emit.arrive()
    x_att = halves(gq, "att", lambda k, i: r.att_s.at[k, i])
    x_attx = halves(gx, "attx", lambda k, i: r.attx_s.at[k])
    for k in range(2):
        x_gated[k].arrive()
        att = dot(r.emit_w[...].reshape(512, 128), r.gated_r[k].reshape(128, 128), 1)
        r.att_s[k] = att.astype(BF16).reshape(8, 64, 128)
        x_att[k].start()
    for k in range(2):
        x_att[k].arrive()
        r.attx_s[k] = jnp.sum(r.att_r[k].astype(F32), axis=0).astype(BF16)
        x_attx[k].start()
    x_dev = halves(gq, "dev2", lambda k, i: r.dev2_s.at[k])
    x_stats2 = halves(gb, "stats2", lambda k, i: r.stats2_s.at[k])
    for k in range(2):
        x_attx[k].arrive()
        part = slice(k * 128, k * 128 + 128)
        two = r.blk[:, part].astype(F32) + jnp.sum(r.attx_r[k].astype(F32), axis=0)
        r.two[:, part] = two
        r.dev2_s[k] = block_stats(two, r.stats2_s.at[k]).astype(BF16)
        x_dev[k].start()
        x_stats2[k].start()
    edge = edge_rows(1).reshape(8, 1, 8, 512)
    now, delta = [], []

    def second(k):
        x_dev[k].arrive()
        x_stats2[k].arrive()
        mean, var = join(r.stats2_r.at[k], 64.0, 4096.0)
        scale = lax.rsqrt(var + EPS_LN)
        blocks = []
        for n in range(8):
            off = r.stats2_r[k, batch_of(n // 2, z, n % 2)][0:1] - mean
            blocks.append((r.dev2_r[k, n].astype(F32) + off) * scale)
        normed = jnp.concatenate(blocks, axis=0).T * prm[1:2] + prm[3:4]
        normed = normed.astype(BF16).astype(F32)
        r.norm_t[:, k * 128 : k * 128 + 128] = normed.T
        now.append(normed)
        split_now = [n.reshape(8, 2, 8, 512) for n in now]
        ahead = edge if k == 0 else split_now[0][:, 1:]
        before = jnp.concatenate([ahead, split_now[k][:, :1]], axis=1).reshape(128, 512)
        delta.append(before - normed)

    def mixed(n, k):
        return (now[k] + delta[k] * prm[9 + n : 10 + n]).astype(BF16)

    x_look.arrive()
    x_acc.arrive()
    x_up = halves(gz, "up", lambda k, i: r.up_s.at[k, i])
    x_units = halves(gz, "units", lambda k, i: r.units_s.at[k])
    x_val = halves(gq, "val", lambda k, i: r.val_s.at[k, i])
    x_valx = halves(gx, "valx", lambda k, i: r.valx_s.at[k])
    for k in range(2):
        second(k)
        up = dot(mixed(0, k), r.look_w[...].reshape(512, 512))
        r.up_s[k] = up.astype(BF16).reshape(8, 16, 512)
        x_up[k].start()
    for k in range(2):
        x_up[k].arrive()
        up = jnp.maximum(jnp.sum(r.up_r[k].astype(F32), axis=0), 0.0)
        up = jnp.where(jnp.logical_and(c == 1, iota(up.shape, 1) < 128), 0.0, up * up)
        r.units_s[k] = up.astype(BF16)
        x_units[k].start()
    mine = r.norm_t[rows(q * 64, 64), :].astype(BF16)
    r.new_edges_o[1] = dot(last, mine, 1).astype(BF16)
    take = [dot(mixed(1, k), r.acc_w[...].reshape(512, 128)) for k in range(2)]
    take = jnp.concatenate(take, axis=0).T
    r.rec_s[...] = take.astype(BF16).reshape(8, 16, 256)
    x_rec = Exchange(gz, lambda i: r.rec_s.at[i], slots(r.rec_r), r.rec_r, s.rec)
    x_rec.start()
    x_down.arrive()
    for k in range(2):
        x_units[k].arrive()
        value = dot(r.down_w[...].reshape(512, 512), r.units_r[k].reshape(128, 512), 1)
        r.val_s[k] = value.astype(BF16).reshape(8, 64, 128)
        x_val[k].start()
    x_rec.arrive()
    r.sig_s[...] = jax.nn.sigmoid(jnp.sum(r.rec_r[...].astype(F32), axis=0))

    def far_copy(k):
        return pltpu.make_async_remote_copy(
            src_ref=r.sig_s,
            dst_ref=r.sig_r.at[lax.rem(z, NX)],
            send_sem=s.sig.at[0],
            recv_sem=s.sig.at[1],
            device_id=dest(k),
            device_id_type=MESH,
        )

    for k in range(4):
        here = jnp.logical_and(dest_here, h == k)

        @pl.when(jnp.logical_not(here))
        def _():
            far_copy(k).start()

        @pl.when(here)
        def _():
            pltpu.make_async_copy(r.sig_s, r.sig_r.at[lax.rem(z, NX)], s.sig.at[1]).start()

    x_new.arrive()
    for k in range(16):
        tile = r.state_n[k // 2].astype(F32)[(k % 2) * 32 : (k % 2) * 32 + 32]
        r.states_o[k, 0:32] = tile[:, 0:64].astype(BF16)
        r.states_o[k, 32:64] = tile[:, 64:128].astype(BF16)
    for k in range(2):
        x_val[k].arrive()
        r.valx_s[k] = jnp.sum(r.val_r[k].astype(F32), axis=0).astype(BF16)
        x_valx[k].start()
    pltpu.make_async_copy(r.sig_r, r.sig_r, s.sig.at[1]).wait()
    value = []
    for k in range(2):
        x_valx[k].arrive()
        value.append(jnp.sum(r.valx_r[k].astype(F32), axis=0))
    value = jnp.concatenate(value, axis=1)
    result = r.two[...] + r.sig_r[...].reshape(64, 256) * value
    r.out[...] = jnp.where(slot < length, result, 0.0).T
    for k in range(64):
        first = (k // 2 % NZ) * 16 + (k // 16) * 2 + k % 2
        r.hidden_o[k, 0:2] = r.out[pl.ds(first, 2, stride=8), :]
        r.hidden_o[k, 2:4] = r.out[pl.ds(first + 128, 2, stride=8), :]

    for k in range(4):

        @pl.when(jnp.logical_not(jnp.logical_and(dest_here, h == k)))
        def _():
            far_copy(k).wait_send()

    for x in (
        x_meta, x_prm, x_edges, x_state, x_low, x_maps, x_emit, x_look, x_acc, x_down, x_emb,
        x_zstate, x_stream, x_stats, x_new, x_rec, *x_dev, *x_stats2, *x_part, *x_gated, *x_att,
        *x_attx, *x_up, *x_units, *x_val, *x_valx,
    ):
        x.drain()


def local(
    query_symbol_numbers,
    alive_span_sizes,
    former_positions,
    previous_normed_vectors,
    memory_matrices,
    vocabulary_vectors,
    standardize_scales,
    standardize_shifts,
    timemix_blend_factors,
    timemix_linear_maps,
    forgetting_first_lowrank,
    forgetting_second_lowrank,
    forgetting_loglog_floor,
    current_reward_factor,
    perspan_standardize_scale,
    perspan_standardize_shift,
    timemix_emit_matrix,
    feedforward_blend_factors,
    feedforward_lookup_matrix,
    feedforward_accept_matrix,
    feedforward_emit_matrix,
):
    hidden, new_edges, states = pl.pallas_call(
        kernel,
        out_shape=[
            jax.ShapeDtypeStruct((64, 4, 64), F32),
            jax.ShapeDtypeStruct((2, 64, 64), BF16),
            jax.ShapeDtypeStruct((16, 64, 64), BF16),
        ],
        in_specs=[ANY] * len(INPUTS),
        out_specs=[VM] * 3,
        scratch_shapes=[pltpu.VMEM(shape, dtype) for _, shape, dtype in SCRATCH]
        + [DMA((2,)) for _ in SEMS]
        + [DMA((2, 2)) for _ in HALVES]
        + [DMA((2,)), DMA(()), DMA(()), DMA((len(LOCAL),))]
        + [
            (pltpu.SMEM if n < 3 else pltpu.VMEM)(shape, dtype)
            for n, (shape, dtype) in enumerate(LOCAL_SHAPES)
        ]
        + [pltpu.SMEM((64, 1, 128), jnp.int32)],
        compiler_params=pltpu.CompilerParams(
            collective_id=0, has_side_effects=True, vmem_limit_bytes=67043328
        ),
        name="layer",
    )(
        query_symbol_numbers,
        alive_span_sizes,
        former_positions,
        standardize_scales,
        standardize_shifts,
        timemix_blend_factors,
        feedforward_blend_factors,
        previous_normed_vectors.reshape(2, 4096),
        memory_matrices.reshape(16, 64, 64),
        forgetting_first_lowrank,
        timemix_linear_maps,
        timemix_emit_matrix,
        feedforward_lookup_matrix,
        feedforward_accept_matrix,
        feedforward_emit_matrix,
        vocabulary_vectors,
        forgetting_second_lowrank,
        forgetting_loglog_floor.reshape(8, 128),
        current_reward_factor.reshape(8, 128),
        perspan_standardize_scale.reshape(8, 128),
        perspan_standardize_shift.reshape(8, 128),
    )
    return hidden, new_edges, states.reshape(1, 16, 64, 64)


def solution(mesh):
    return jax.shard_map(
        local,
        mesh=mesh,
        in_specs=(
            P("batch", None),
            P("batch"),
            P("batch"),
            P(None, "batch", None),
            P("batch", "head", None, None),
            P("batch", "head"),
            P(None, "batch"),
            P(None, "batch"),
            P(None, "batch"),
            P(None, "batch", "head"),
            P("batch", None),
            P(None, "head"),
            P("head"),
            P("head"),
            P("head"),
            P("head"),
            P("batch", "head"),
            P(None, "batch"),
            P("batch", "head"),
            P("batch", None),
            P("batch", "head"),
        ),
        out_specs=(P(None, None, "batch"), P(None, None, "batch"), P("batch", "head", None, None)),
        check_vma=False,
    )
```

```python
import jax
import jax.numpy as jnp
from jax import lax
from jax.experimental import pallas as pl
from jax.experimental.pallas import tpu as pltpu
from jax.sharding import PartitionSpec as P

F32 = jnp.float32
BF16 = jnp.bfloat16
MESH = pl.DeviceIdType.MESH
EPS_LN = 1e-05
EPS_GN = 0.00064
NX, NY, NZ, NC = 4, 4, 8, 2
NQ = NY * NC
VM = pl.BlockSpec(memory_space=pltpu.VMEM)
ANY = pl.BlockSpec(memory_space=pl.ANY)
DMA = pltpu.SemaphoreType.DMA


def batch_of(y, z, c):
    return (y * NZ + z) * NC + c


def place():
    h = lax.axis_index("head")
    b = lax.axis_index("batch")
    c = lax.rem(b, NC)
    z = lax.rem(lax.div(b, NC), NZ)
    y = lax.div(b, NC * NZ)
    return h, b, y, z, c, y * NC + c


class Group:
    def __init__(self, kind):
        h, b, y, z, c, q = place()
        if kind == "z":
            self.me, self.n = z, NZ
            self.dev = lambda i: (h, batch_of(y, i, c))
        elif kind == "q":
            self.me, self.n = q, NQ
            self.dev = lambda i: (h, batch_of(lax.div(i, NC), z, lax.rem(i, NC)))
        elif kind == "x":
            self.me, self.n = h, NX
            self.dev = lambda i: (i, b)
        elif kind == "b":
            self.me, self.n = b, NY * NZ * NC
            self.dev = lambda i: (h, i)
        else:
            self.me, self.n = q * NX + h, NQ * NX

            def dev(i):
                k = lax.div(i, NX)
                return (lax.rem(i, NX), batch_of(lax.div(k, NC), z, lax.rem(k, NC)))

            self.dev = dev

    def each(self, body):
        def step(p, carry):
            body(p, lax.rem(self.me + p, self.n))
            return carry

        lax.fori_loop(1, self.n, step, 0)


def barrier(*groups):
    sem = pltpu.get_barrier_semaphore()
    for g in groups:
        g.each(
            lambda p, i: pl.semaphore_signal(
                sem, inc=1, device_id=g.dev(i), device_id_type=MESH
            )
        )
    pl.semaphore_wait(sem, sum(g.n - 1 for g in groups))


class Exchange:
    def __init__(self, group, src, dst, whole, sems):
        self.g, self.src, self.dst, self.whole, self.sems = group, src, dst, whole, sems

    def copy(self, i):
        return pltpu.make_async_remote_copy(
            src_ref=self.src(i),
            dst_ref=self.dst(self.g.me),
            send_sem=self.sems.at[0],
            recv_sem=self.sems.at[1],
            device_id=self.g.dev(i),
            device_id_type=MESH,
        )

    def start(self):
        self.g.each(lambda p, i: self.copy(i).start())
        pltpu.make_async_copy(self.src(self.g.me), self.dst(self.g.me), self.sems.at[1]).start()

    def arrive(self):
        pltpu.make_async_copy(self.whole, self.whole, self.sems.at[1]).wait()

    def drain(self):
        part = self.dst(pl.ds(0, self.g.n - 1))
        pltpu.make_async_copy(part, part, self.sems.at[0]).wait()


def lanes(i, n):
    return pl.ds(pl.multiple_of(i, 128), n)


def rows(i, n):
    return pl.ds(pl.multiple_of(i, n), n)


def chunk_start(i):
    return (7 * lax.div(i, 2) + 3 * lax.rem(i, 2)) * 128


def iota(shape, axis):
    return lax.broadcasted_iota(jnp.int32, shape, axis)


def dot(a, b, cb=0):
    return lax.dot_general(a, b, (((1,), (cb,)), ((), ())), preferred_element_type=F32)


def head_sum(x):
    left = iota(x.shape, 1) < 64
    a = jnp.sum(jnp.where(left, x, 0.0), axis=1, keepdims=True)
    b = jnp.sum(jnp.where(left, 0.0, x), axis=1, keepdims=True)
    return jnp.where(left, a, b)


def split(x):
    high = x.astype(BF16)
    return high, (x - high.astype(F32)).astype(BF16)


def join(stats, per, count):
    blocks = stats[...]
    total = jnp.sum(blocks, axis=0)
    mean = total[0:1] * (1.0 / blocks.shape[0])
    dev = blocks - mean[None]
    between = jnp.sum(dev * dev, axis=0)[0:1]
    return mean, (total[1:2] + per * between) * (1.0 / count)


def block_stats(x, st):
    mean = jnp.sum(x, axis=0, keepdims=True) * (1.0 / x.shape[0])
    dev = x - mean
    st[0:1, :] = mean
    st[1:2, :] = jnp.sum(dev * dev, axis=0, keepdims=True)
    return dev


INPUTS = [
    "ids", "lens", "pos", "gains", "biases", "mixes", "mixes2", "edges", "state", "low", "maps",
    "emit", "look", "acc", "down", "vocab", "second", "floor", "bonus", "gn_gain", "gn_bias",
]
LOCAL = [
    "ids", "lens", "pos", "gains", "biases", "mixes", "mixes2", "edges", "state", "second",
    "floor", "bonus", "gn_gain", "gn_bias",
]
LOCAL_SHAPES = [
    ((1, 4), jnp.int32),
    ((1,), jnp.int32),
    ((1,), jnp.int32),
    ((2, 64), F32),
    ((2, 64), F32),
    ((5, 64), F32),
    ((2, 64), F32),
    ((2, 4096), BF16),
    ((16, 64, 64), BF16),
    ((128, 128), BF16),
    ((8, 128), F32),
    ((8, 128), F32),
    ((8, 128), F32),
    ((8, 128), F32),
]
OUTPUTS = ["hidden", "new_edges", "states"]
SCRATCH = [
    ("meta_s", (1, 128), jnp.int32),
    ("meta_r", (64, 1, 128), jnp.int32),
    ("prm_s", (16, 128), F32),
    ("prm_r", (8, 16, 128), F32),
    ("edges_s", (8, 8, 128), BF16),
    ("edges_r", (64, 8, 128), BF16),
    ("state_p", (64, 8, 128), BF16),
    ("state_n", (8, 64, 128), BF16),
    ("out", (256, 64), F32),
    ("edges_f", (64, 8, 128), F32),
    ("state_r", (64, 8, 128), BF16),
    ("state_s", (64, 8, 128), BF16),
    ("state_z", (8, 8, 8, 128), BF16),
    ("low_w", (8, 64, 128), BF16),
    ("maps_w", (4, 8, 64, 128), BF16),
    ("emit_w", (8, 64, 128), BF16),
    ("look_w", (8, 64, 512), BF16),
    ("acc_w", (8, 64, 128), BF16),
    ("down_w", (8, 64, 512), BF16),
    ("vocab_w", (64, 16384), BF16),
    ("table", (64, 128), F32),
    ("emb_s", (64, 256), BF16),
    ("emb_r", (NX, 64, 256), BF16),
    ("blk", (64, 256), BF16),
    ("st", (2, 256), F32),
    ("st_r", (64, 2, 256), F32),
    ("stream_r", (8, 64, 256), BF16),
    ("part_s", (2, 5, 128, 128), BF16),
    ("part_r", (2, 8, 5, 16, 128), BF16),
    ("bd", (8, 128, 128), BF16),
    ("gated_s", (2, 16, 128), BF16),
    ("gated_r", (2, 8, 16, 128), BF16),
    ("new_s", (8, 64, 128), BF16),
    ("att_s", (2, 8, 64, 128), BF16),
    ("att_r", (2, 8, 64, 128), BF16),
    ("attx_s", (2, 64, 128), BF16),
    ("attx_r", (2, NX, 64, 128), BF16),
    ("two", (64, 256), F32),
    ("dev2_s", (2, 64, 128), BF16),
    ("stats2_s", (2, 2, 128), F32),
    ("stats2_r", (2, 64, 2, 128), F32),
    ("dev2_r", (2, 8, 64, 128), BF16),
    ("up_s", (2, 8, 16, 512), BF16),
    ("up_r", (2, 8, 16, 512), BF16),
    ("rec_s", (8, 16, 256), BF16),
    ("rec_r", (8, 16, 256), BF16),
    ("units_s", (2, 16, 512), BF16),
    ("units_r", (2, 8, 16, 512), BF16),
    ("sig_s", (16, 256), F32),
    ("sig_r", (4, 16, 256), F32),
    ("val_s", (2, 8, 64, 128), BF16),
    ("val_r", (2, 8, 64, 128), BF16),
    ("valx_s", (2, 64, 128), BF16),
    ("valx_r", (2, NX, 64, 128), BF16),
    ("norm_t", (512, 256), F32),
]
SEMS = [
    "meta", "prm", "edges", "state", "zstate", "low", "maps", "emit", "look", "acc", "down", "emb",
    "stats", "stream", "new", "rec",
]
HALVES = [
    "part", "gated", "att", "attx", "dev2", "stats2", "up", "units", "val", "valx",
]


class Refs:
    pass


def kernel(*refs):
    r, s = Refs(), Refs()
    names = INPUTS + OUTPUTS + [n for n, _, _ in SCRATCH]
    refs, meta_m = refs[:-1], refs[-1]
    refs, fetched = refs[: -len(LOCAL)], refs[-len(LOCAL) :]
    for name, ref in zip(names, refs):
        setattr(r, name + ("_o" if name in OUTPUTS else ""), ref)
    for name, ref in zip(SEMS + HALVES + ["sig", "vocab", "smem", "local"], refs[len(names) :]):
        setattr(s, name, ref)
    h, b, y, z, c, q = place()
    gb, gq, gx, gz = Group("b"), Group("q"), Group("x"), Group("z")

    dest = lambda k: (k, batch_of(y, 2 * h + c, lax.div(z, NX)))
    source = lambda k: (lax.div(z, 2), batch_of(y, c * NX + k, lax.rem(z, 2)))
    dest_here = dest(0)[1] == b

    sem = pltpu.get_barrier_semaphore()
    for g in (gb, gx):
        g.each(
            lambda p, i: pl.semaphore_signal(sem, inc=1, device_id=g.dev(i), device_id_type=MESH)
        )
    for k in range(4):
        far = source(k)

        @pl.when(jnp.logical_and(far[0] != h, far[1] != b))
        def _():
            pl.semaphore_signal(sem, inc=1, device_id=far, device_id_type=MESH)

    fetch = {}
    for n, (name, ref) in enumerate(zip(LOCAL, fetched)):
        whole = getattr(r, name)
        if name == "second":
            whole = whole.at[:, lanes(q * 128, 128)]
        fetch[name] = pltpu.make_async_copy(whole, ref, s.local.at[n])
        fetch[name].start()
        setattr(r, name, ref)
    vocab_in = pltpu.make_async_copy(r.vocab, r.vocab_w, s.vocab)
    vocab_in.start()
    for name in LOCAL[:7]:
        fetch[name].wait()
    lane = iota((1, 128), 1)
    meta = jnp.where(lane == 4, r.lens[0], jnp.where(lane == 5, r.pos[0], 0))
    for j in range(4):
        meta = jnp.where(lane == j, r.ids[0, j], meta)
    r.meta_s[...] = meta
    r.prm_s[...] = jnp.zeros((16, 128), F32)
    r.prm_s[0:2, 0:64] = r.gains[...]
    r.prm_s[2:4, 0:64] = r.biases[...]
    r.prm_s[4:9, 0:64] = r.mixes[...]
    r.prm_s[9:11, 0:64] = r.mixes2[...]
    prm = r.prm_s[...]
    r.prm_s[...] = jnp.where(c == 0, prm, pltpu.roll(prm, 64, 1))

    fetch["edges"].wait()
    old = r.edges[...].astype(F32)
    for k in range(NZ):
        tiles = [old[:, (i * NZ + k) * 128 : (i * NZ + k) * 128 + 128] for i in range(NY)]
        r.edges_s[k] = jnp.concatenate(tiles, axis=0).astype(BF16)
    fetch["state"].wait()
    for k in range(16):
        tile = r.state[k].astype(F32)
        tile = jnp.concatenate([tile[0:32], tile[32:64]], axis=1).astype(BF16)
        for i in range(4):
            r.state_p[k * 4 + i] = tile[i * 8 : i * 8 + 8]

    pl.semaphore_wait(sem, gb.n - 1 + gx.n - 1 + 3 * (1 - dest_here.astype(jnp.int32)))

    def same(ref):
        return lambda i: ref

    def slots(ref):
        return lambda m: ref.at[m]

    x_meta = Exchange(gb, same(r.meta_s), slots(r.meta_r), r.meta_r, s.meta)
    x_prm = Exchange(gq, same(r.prm_s), slots(r.prm_r), r.prm_r, s.prm)
    x_edges = Exchange(
        gb, lambda i: r.edges_s.at[lax.rem(lax.div(i, NC), NZ)], slots(r.edges_r), r.edges_r, s.edges
    )
    x_state = Exchange(
        gb,
        lambda i: r.state_p.at[
            (lax.div(i, NC * NZ) * NC + lax.rem(i, NC)) * NZ + lax.rem(lax.div(i, NC), NZ)
        ],
        slots(r.state_r),
        r.state_r,
        s.state,
    )
    x_low = Exchange(gq, same(r.low), slots(r.low_w), r.low_w, s.low)
    x_maps = Exchange(
        gq,
        lambda i: r.maps.at[:, :, lanes(i * 128, 128)],
        lambda m: r.maps_w.at[:, m],
        r.maps_w,
        s.maps,
    )
    x_emit = Exchange(gq, lambda i: r.emit.at[:, lanes(i * 128, 128)], slots(r.emit_w), r.emit_w, s.emit)
    x_look = Exchange(
        gq, lambda i: r.look.at[:, lanes(chunk_start(i), 512)], slots(r.look_w), r.look_w, s.look
    )
    x_acc = Exchange(
        gq,
        lambda i: r.acc.at[:, lanes((lax.div(i, NC) * NZ + 2 * h + lax.rem(i, NC)) * 128, 128)],
        slots(r.acc_w),
        r.acc_w,
        s.acc,
    )
    x_down = Exchange(
        gq, lambda i: r.down.at[:, lanes(chunk_start(i), 512)], slots(r.down_w), r.down_w, s.down
    )
    for x in (x_meta, x_maps, x_low, x_prm, x_edges):
        x.start()

    x_meta.arrive()
    to_smem = pltpu.make_async_copy(r.meta_r, meta_m, s.smem)
    to_smem.start()
    meta = r.meta_r[...].reshape(64, 128)
    high = lax.shift_right_logical(meta, 8)
    lowb = (meta - high * 256).astype(F32).astype(BF16)
    high = high.astype(F32).astype(BF16)

    def device_of(zz, qq):
        return (lax.shift_right_logical(qq, 1) * NZ + zz) * NC + (qq & 1)

    tok = iota((256, 64), 0)
    by_tok = device_of(lax.shift_right_logical(tok, 4) & 7, tok & 7) == iota((256, 64), 1)
    by_tok = jnp.where(by_tok, 1.0, 0.0).astype(BF16)
    cols = dot(by_tok, high) * 256.0 + dot(by_tok, lowb)
    req = iota((64, 64), 0)
    by_req = device_of(lax.shift_right_logical(req, 3), req & 7) == iota((64, 64), 1)
    by_req = jnp.where(by_req, 1.0, 0.0).astype(BF16)
    r.table[...] = dot(by_req, lowb)
    tok_rows = cols.T
    lane_t = iota((1, 256), 1)
    slot = lax.shift_right_logical(lane_t, 7) * 2 + (lax.shift_right_logical(lane_t, 3) & 1)
    ids = tok_rows[0:1]
    for j in range(1, 4):
        ids = jnp.where(slot == j, tok_rows[j : j + 1], ids)
    ids = ids.astype(jnp.int32) - h * 16384
    length = tok_rows[4:5].astype(jnp.int32)

    vocab_in.wait()
    step = 8192

    def look_up(k, acc):
        base = pl.multiple_of(k * step, step)
        hot = jnp.where(iota((step, 256), 0) == ids - base, 1.0, 0.0).astype(BF16)
        return acc + dot(r.vocab_w[:, pl.ds(base, step)], hot)

    emb = lax.fori_loop(0, 16384 // step, look_up, jnp.zeros((64, 256), F32))
    r.emb_s[...] = emb.astype(BF16)
    x_emb = Exchange(gx, same(r.emb_s), slots(r.emb_r), r.emb_r, s.emb)
    x_emb.start()
    x_state.start()

    x_emb.arrive()
    own = jnp.sum(r.emb_r[...].astype(F32), axis=0)
    r.blk[...] = own.astype(BF16)
    x_stream = Exchange(gq, same(r.blk), slots(r.stream_r), r.stream_r, s.stream)
    x_stream.start()
    block_stats(own, r.st)
    x_stats = Exchange(gb, same(r.st), slots(r.st_r), r.st_r, s.stats)
    x_stats.start()

    x_edges.arrive()
    x_state.arrive()
    to_smem.wait()

    def reorder(n, carry):
        zz = lax.div(n, 8)
        qq = lax.rem(n, 8)
        old = meta_m[batch_of(lax.div(qq, 2), zz, lax.rem(qq, 2)), 0, 5]
        r.edges_f[n] = r.edges_r[old].astype(F32)
        r.state_s[n] = r.state_r[old]
        return carry

    lax.fori_loop(0, 64, reorder, 0)
    x_zstate = Exchange(gz, lambda i: r.state_s.at[rows(i * 8, 8)], slots(r.state_z), r.state_z, s.zstate)
    x_zstate.start()

    x_prm.arrive()
    prm = jnp.concatenate([r.prm_r[2 * k] + r.prm_r[2 * k + 1] for k in range(NY)], axis=1)

    def edge_rows(k):
        return jnp.concatenate([r.edges_f[:, i * 2 + k, :] for i in range(NY)], axis=1)

    def shifted(normed, k, first):
        now = normed.astype(F32).reshape(2, 8, 2, 8, 512)
        edge = edge_rows(k)
        before = [
            jnp.concatenate([edge.reshape(8, 1, 8, 512), now[0, :, :1]], axis=1).reshape(128, 512),
            jnp.concatenate([now[0, :, 1:], now[1, :, :1]], axis=1).reshape(128, 512),
        ]
        now = [now[k].reshape(128, 512) for k in range(2)]
        delta = [before[k] - now[k] for k in range(2)]
        return lambda n, k: (now[k] + delta[k] * prm[first + n : first + n + 1]).astype(BF16)

    def halves(group, name, src):
        got, sems = getattr(r, name + "_r"), getattr(s, name)
        return [
            Exchange(
                group,
                lambda i, k=k: src(k, i),
                lambda m, k=k: got.at[k, m],
                got.at[k],
                sems.at[k],
            )
            for k in range(2)
        ]

    last = jnp.logical_and(
        iota((64, 256), 0)
        == device_of(lax.shift_right_logical(lane_t, 4) & 7, lane_t & 7),
        slot == length - 1,
    )
    last = jnp.where(last, 1.0, 0.0).astype(BF16)

    def layer(x, k):
        normed = (x.T * prm[k : k + 1] + prm[2 + k : 3 + k]).astype(BF16)
        return normed

    x_stream.arrive()
    x_stats.arrive()
    mean, var = join(r.st_r, 64.0, 4096.0)
    scaled = (r.stream_r[...].astype(F32).reshape(512, 256) - mean) * lax.rsqrt(var + EPS_LN)
    normed = layer(scaled, 0)
    mixed = shifted(normed, 0, 4)
    x_maps.arrive()
    x_low.arrive()
    x_part = halves(gz, "part", lambda k, i: r.part_s.at[k, :, rows(i * 16, 16)])
    for k in range(2):
        for n in range(5):
            w = r.maps_w[n] if n < 4 else r.low_w[...]
            r.part_s[k, n] = dot(mixed(n, k), w.reshape(512, 128)).astype(BF16)
        x_part[k].start()
    for x in (x_emit, x_look, x_acc, x_down):
        x.start()

    r.norm_t[...] = normed.astype(F32).T
    mine = r.norm_t[rows(q * 64, 64), :].astype(BF16)
    r.new_edges_o[0] = dot(last, mine, 1).astype(BF16)

    x_zstate.arrive()
    left = iota((32, 128), 1) < 64
    for n in range(8):
        tile = r.state_z[:, n].astype(F32).reshape(64, 128)
        turn = pltpu.roll(tile, 64, 1)
        blocks = [
            jnp.where(left, tile[0:32], 0.0),
            jnp.where(left, turn[0:32], 0.0),
            jnp.where(left, 0.0, turn[32:64]),
            jnp.where(left, 0.0, tile[32:64]),
        ]
        r.bd[n] = jnp.concatenate(blocks, axis=0).astype(BF16)
    lens8 = r.table[rows(z * 8, 8), :][:, 4:5].astype(jnp.int32)

    for name in LOCAL[9:]:
        fetch[name].wait()
    floor, bonus, gn_gain, gn_bias = (
        ref[pl.ds(q, 1), :] for ref in (r.floor, r.bonus, r.gn_gain, r.gn_bias)
    )
    alive = [lens8 > j for j in range(4)]

    def spread(x):
        row_q = iota(x.shape, 0) & 7
        return jnp.concatenate([jnp.where(row_q == n, x, 0.0) for n in range(8)], axis=1)

    bd = r.bd[...].reshape(1024, 128)
    rec, key, val, dec = [], [], [], []
    x_gated = halves(gz, "gated", lambda k, i: r.gated_s.at[k])
    for k in range(2):
        x_part[k].arrive()
        proj = jnp.sum(r.part_r[k].astype(F32), axis=0)
        low = jnp.tanh(proj[4]).astype(BF16)
        decay = jnp.exp(-jnp.exp(floor + dot(low, r.second[...])))
        for j in range(2):
            rec.append(proj[0, 8 * j : 8 * j + 8])
            key.append(proj[1, 8 * j : 8 * j + 8])
            val.append(proj[2, 8 * j : 8 * j + 8])
            dec.append(decay[8 * j : 8 * j + 8])
        seen, inner = [], []
        for j in range(2 * k, 2 * k + 2):
            acc = head_sum(rec[j] * bonus * key[j]) * val[j]
            run = rec[j]
            for i in range(j - 1, -1, -1):
                acc = acc + head_sum(run * key[i]) * val[i]
                run = run * dec[i]
            seen.append(run)
            inner.append(acc)
        high, rest = split(spread(jnp.concatenate(seen, axis=0)))
        wkv = dot(high, bd) + dot(rest, bd) + jnp.concatenate(inner, axis=0)
        mu = head_sum(wkv) * (1.0 / 64)
        dev = wkv - mu
        spr = head_sum(dev * dev) * (1.0 / 64)
        grouped = dev * lax.rsqrt(spr + EPS_GN) * gn_gain + gn_bias
        gate = proj[3]
        r.gated_s[k] = (grouped * (gate * jax.nn.sigmoid(gate))).astype(BF16)
        x_gated[k].start()

    x_emit.arrive()
    x_att = halves(gq, "att", lambda k, i: r.att_s.at[k, i])
    x_attx = halves(gx, "attx", lambda k, i: r.attx_s.at[k])
    for k in range(2):
        x_gated[k].arrive()
        att = dot(r.emit_w[...].reshape(512, 128), r.gated_r[k].reshape(128, 128), 1)
        r.att_s[k] = att.astype(BF16).reshape(8, 64, 128)
        x_att[k].start()
    tail, keys = jnp.ones((8, 128), F32), []
    for j in range(3, -1, -1):
        keys.append(jnp.where(alive[j], key[j] * tail, 0.0))
        tail = jnp.where(alive[j], tail * dec[j], tail)
    keys = spread(jnp.concatenate(keys[::-1], axis=0)).T
    vals = jnp.concatenate(val, axis=0)
    kh, kl = split(keys)
    vh, vl = split(vals)
    outer = dot(kh, vh) + dot(kl, vh) + dot(kh, vl)
    tail = tail.T
    for n in range(8):
        new = outer[n * 128 : n * 128 + 128] + tail[:, n : n + 1] * r.bd[n].astype(F32)
        turn = pltpu.roll(new, 64, 1)
        top = jnp.where(left, new[0:32], turn[32:64])
        bottom = jnp.where(left, turn[64:96], new[96:128])
        r.new_s[n] = jnp.concatenate([top, bottom], axis=0).astype(BF16)
    x_new = Exchange(gq, lambda i: r.new_s.at[i], lambda m: r.state_n.at[m], r.state_n, s.new)
    x_new.start()

    for k in range(2):
        x_att[k].arrive()
        r.attx_s[k] = jnp.sum(r.att_r[k].astype(F32), axis=0).astype(BF16)
        x_attx[k].start()
    x_dev = halves(gq, "dev2", lambda k, i: r.dev2_s.at[k])
    x_stats2 = halves(gb, "stats2", lambda k, i: r.stats2_s.at[k])
    for k in range(2):
        x_attx[k].arrive()
        part = slice(k * 128, k * 128 + 128)
        two = r.blk[:, part].astype(F32) + jnp.sum(r.attx_r[k].astype(F32), axis=0)
        r.two[:, part] = two
        r.dev2_s[k] = block_stats(two, r.stats2_s.at[k]).astype(BF16)
        x_dev[k].start()
        x_stats2[k].start()
    edge = edge_rows(1).reshape(8, 1, 8, 512)
    now, delta = [], []

    def second(k):
        x_dev[k].arrive()
        x_stats2[k].arrive()
        mean, var = join(r.stats2_r.at[k], 64.0, 4096.0)
        scale = lax.rsqrt(var + EPS_LN)
        blocks = []
        for n in range(8):
            off = r.stats2_r[k, batch_of(n // 2, z, n % 2)][0:1] - mean
            blocks.append((r.dev2_r[k, n].astype(F32) + off) * scale)
        normed = jnp.concatenate(blocks, axis=0).T * prm[1:2] + prm[3:4]
        normed = normed.astype(BF16).astype(F32)
        r.norm_t[:, k * 128 : k * 128 + 128] = normed.T
        now.append(normed)
        split_now = [n.reshape(8, 2, 8, 512) for n in now]
        ahead = edge if k == 0 else split_now[0][:, 1:]
        before = jnp.concatenate([ahead, split_now[k][:, :1]], axis=1).reshape(128, 512)
        delta.append(before - normed)

    def mixed(n, k):
        return (now[k] + delta[k] * prm[9 + n : 10 + n]).astype(BF16)

    x_look.arrive()
    x_acc.arrive()
    x_up = halves(gz, "up", lambda k, i: r.up_s.at[k, i])
    x_units = halves(gz, "units", lambda k, i: r.units_s.at[k])
    x_val = halves(gq, "val", lambda k, i: r.val_s.at[k, i])
    x_valx = halves(gx, "valx", lambda k, i: r.valx_s.at[k])
    for k in range(2):
        second(k)
        up = dot(mixed(0, k), r.look_w[...].reshape(512, 512))
        r.up_s[k] = up.astype(BF16).reshape(8, 16, 512)
        x_up[k].start()
    for k in range(2):
        x_up[k].arrive()
        up = jnp.maximum(jnp.sum(r.up_r[k].astype(F32), axis=0), 0.0)
        up = jnp.where(jnp.logical_and(c == 1, iota(up.shape, 1) < 128), 0.0, up * up)
        r.units_s[k] = up.astype(BF16)
        x_units[k].start()
    mine = r.norm_t[rows(q * 64, 64), :].astype(BF16)
    r.new_edges_o[1] = dot(last, mine, 1).astype(BF16)
    take = [dot(mixed(1, k), r.acc_w[...].reshape(512, 128)) for k in range(2)]
    take = jnp.concatenate(take, axis=0).T
    r.rec_s[...] = take.astype(BF16).reshape(8, 16, 256)
    x_rec = Exchange(gz, lambda i: r.rec_s.at[i], slots(r.rec_r), r.rec_r, s.rec)
    x_rec.start()
    x_down.arrive()
    for k in range(2):
        x_units[k].arrive()
        value = dot(r.down_w[...].reshape(512, 512), r.units_r[k].reshape(128, 512), 1)
        r.val_s[k] = value.astype(BF16).reshape(8, 64, 128)
        x_val[k].start()
    x_rec.arrive()
    r.sig_s[...] = jax.nn.sigmoid(jnp.sum(r.rec_r[...].astype(F32), axis=0))

    def far_copy(k):
        return pltpu.make_async_remote_copy(
            src_ref=r.sig_s,
            dst_ref=r.sig_r.at[lax.rem(z, NX)],
            send_sem=s.sig.at[0],
            recv_sem=s.sig.at[1],
            device_id=dest(k),
            device_id_type=MESH,
        )

    for k in range(4):
        here = jnp.logical_and(dest_here, h == k)

        @pl.when(jnp.logical_not(here))
        def _():
            far_copy(k).start()

        @pl.when(here)
        def _():
            pltpu.make_async_copy(r.sig_s, r.sig_r.at[lax.rem(z, NX)], s.sig.at[1]).start()

    x_new.arrive()
    for k in range(16):
        tile = r.state_n[k // 2].astype(F32)[(k % 2) * 32 : (k % 2) * 32 + 32]
        r.states_o[k, 0:32] = tile[:, 0:64].astype(BF16)
        r.states_o[k, 32:64] = tile[:, 64:128].astype(BF16)
    for k in range(2):
        x_val[k].arrive()
        r.valx_s[k] = jnp.sum(r.val_r[k].astype(F32), axis=0).astype(BF16)
        x_valx[k].start()
    pltpu.make_async_copy(r.sig_r, r.sig_r, s.sig.at[1]).wait()
    value = []
    for k in range(2):
        x_valx[k].arrive()
        value.append(jnp.sum(r.valx_r[k].astype(F32), axis=0))
    value = jnp.concatenate(value, axis=1)
    result = r.two[...] + r.sig_r[...].reshape(64, 256) * value
    r.out[...] = jnp.where(slot < length, result, 0.0).T
    for k in range(64):
        first = (k // 2 % NZ) * 16 + (k // 16) * 2 + k % 2
        r.hidden_o[k, 0:2] = r.out[pl.ds(first, 2, stride=8), :]
        r.hidden_o[k, 2:4] = r.out[pl.ds(first + 128, 2, stride=8), :]

    for k in range(4):

        @pl.when(jnp.logical_not(jnp.logical_and(dest_here, h == k)))
        def _():
            far_copy(k).wait_send()

    for x in (
        x_meta, x_prm, x_edges, x_state, x_low, x_maps, x_emit, x_look, x_acc, x_down, x_emb,
        x_zstate, x_stream, x_stats, x_new, x_rec, *x_dev, *x_stats2, *x_part, *x_gated, *x_att,
        *x_attx, *x_up, *x_units, *x_val, *x_valx,
    ):
        x.drain()


def local(
    query_symbol_numbers,
    alive_span_sizes,
    former_positions,
    previous_normed_vectors,
    memory_matrices,
    vocabulary_vectors,
    standardize_scales,
    standardize_shifts,
    timemix_blend_factors,
    timemix_linear_maps,
    forgetting_first_lowrank,
    forgetting_second_lowrank,
    forgetting_loglog_floor,
    current_reward_factor,
    perspan_standardize_scale,
    perspan_standardize_shift,
    timemix_emit_matrix,
    feedforward_blend_factors,
    feedforward_lookup_matrix,
    feedforward_accept_matrix,
    feedforward_emit_matrix,
):
    hidden, new_edges, states = pl.pallas_call(
        kernel,
        out_shape=[
            jax.ShapeDtypeStruct((64, 4, 64), F32),
            jax.ShapeDtypeStruct((2, 64, 64), BF16),
            jax.ShapeDtypeStruct((16, 64, 64), BF16),
        ],
        in_specs=[ANY] * len(INPUTS),
        out_specs=[VM] * 3,
        scratch_shapes=[pltpu.VMEM(shape, dtype) for _, shape, dtype in SCRATCH]
        + [DMA((2,)) for _ in SEMS]
        + [DMA((2, 2)) for _ in HALVES]
        + [DMA((2,)), DMA(()), DMA(()), DMA((len(LOCAL),))]
        + [
            (pltpu.SMEM if n < 3 else pltpu.VMEM)(shape, dtype)
            for n, (shape, dtype) in enumerate(LOCAL_SHAPES)
        ]
        + [pltpu.SMEM((64, 1, 128), jnp.int32)],
        compiler_params=pltpu.CompilerParams(
            collective_id=0, has_side_effects=True, vmem_limit_bytes=67043328
        ),
        name="layer",
    )(
        query_symbol_numbers,
        alive_span_sizes,
        former_positions,
        standardize_scales,
        standardize_shifts,
        timemix_blend_factors,
        feedforward_blend_factors,
        previous_normed_vectors.reshape(2, 4096),
        memory_matrices.reshape(16, 64, 64),
        forgetting_first_lowrank,
        timemix_linear_maps,
        timemix_emit_matrix,
        feedforward_lookup_matrix,
        feedforward_accept_matrix,
        feedforward_emit_matrix,
        vocabulary_vectors,
        forgetting_second_lowrank,
        forgetting_loglog_floor.reshape(8, 128),
        current_reward_factor.reshape(8, 128),
        perspan_standardize_scale.reshape(8, 128),
        perspan_standardize_shift.reshape(8, 128),
    )
    return hidden, new_edges, states.reshape(1, 16, 64, 64)


def solution(mesh):
    return jax.shard_map(
        local,
        mesh=mesh,
        in_specs=(
            P("batch", None),
            P("batch"),
            P("batch"),
            P(None, "batch", None),
            P("batch", "head", None, None),
            P("batch", "head"),
            P(None, "batch"),
            P(None, "batch"),
            P(None, "batch"),
            P(None, "batch", "head"),
            P("batch", None),
            P(None, "head"),
            P("head"),
            P("head"),
            P("head"),
            P("head"),
            P("batch", "head"),
            P(None, "batch"),
            P("batch", "head"),
            P("batch", None),
            P("batch", "head"),
        ),
        out_specs=(P(None, None, "batch"), P(None, None, "batch"), P("batch", "head", None, None)),
        check_vma=False,
    )
```

```python
import jax
import jax.numpy as jnp
from jax import lax
from jax.experimental import pallas as pl
from jax.experimental.pallas import tpu as pltpu
from jax.sharding import PartitionSpec as P

F32 = jnp.float32
BF16 = jnp.bfloat16
MESH = pl.DeviceIdType.MESH
EPS_LN = 1e-05
EPS_GN = 0.00064
NX, NY, NZ, NC = 4, 4, 8, 2
NQ = NY * NC
VM = pl.BlockSpec(memory_space=pltpu.VMEM)
ANY = pl.BlockSpec(memory_space=pl.ANY)
DMA = pltpu.SemaphoreType.DMA


def batch_of(y, z, c):
    return (y * NZ + z) * NC + c


def place():
    h = lax.axis_index("head")
    b = lax.axis_index("batch")
    c = lax.rem(b, NC)
    z = lax.rem(lax.div(b, NC), NZ)
    y = lax.div(b, NC * NZ)
    return h, b, y, z, c, y * NC + c


class Group:
    def __init__(self, kind):
        h, b, y, z, c, q = place()
        if kind == "z":
            self.me, self.n = z, NZ
            self.dev = lambda i: (h, batch_of(y, i, c))
        elif kind == "q":
            self.me, self.n = q, NQ
            self.dev = lambda i: (h, batch_of(lax.div(i, NC), z, lax.rem(i, NC)))
        elif kind == "x":
            self.me, self.n = h, NX
            self.dev = lambda i: (i, b)
        elif kind == "b":
            self.me, self.n = b, NY * NZ * NC
            self.dev = lambda i: (h, i)
        else:
            self.me, self.n = q * NX + h, NQ * NX

            def dev(i):
                k = lax.div(i, NX)
                return (lax.rem(i, NX), batch_of(lax.div(k, NC), z, lax.rem(k, NC)))

            self.dev = dev

    def each(self, body):
        def step(p, carry):
            body(p, lax.rem(self.me + p, self.n))
            return carry

        lax.fori_loop(1, self.n, step, 0)


def barrier(*groups):
    sem = pltpu.get_barrier_semaphore()
    for g in groups:
        g.each(
            lambda p, i: pl.semaphore_signal(
                sem, inc=1, device_id=g.dev(i), device_id_type=MESH
            )
        )
    pl.semaphore_wait(sem, sum(g.n - 1 for g in groups))


class Exchange:
    def __init__(self, group, src, dst, whole, sems):
        self.g, self.src, self.dst, self.whole, self.sems = group, src, dst, whole, sems

    def copy(self, i):
        return pltpu.make_async_remote_copy(
            src_ref=self.src(i),
            dst_ref=self.dst(self.g.me),
            send_sem=self.sems.at[0],
            recv_sem=self.sems.at[1],
            device_id=self.g.dev(i),
            device_id_type=MESH,
        )

    def start(self):
        self.g.each(lambda p, i: self.copy(i).start())
        pltpu.make_async_copy(self.src(self.g.me), self.dst(self.g.me), self.sems.at[1]).start()

    def arrive(self):
        pltpu.make_async_copy(self.whole, self.whole, self.sems.at[1]).wait()

    def drain(self):
        part = self.dst(pl.ds(0, self.g.n - 1))
        pltpu.make_async_copy(part, part, self.sems.at[0]).wait()


def lanes(i, n):
    return pl.ds(pl.multiple_of(i, 128), n)


def rows(i, n):
    return pl.ds(pl.multiple_of(i, n), n)


def chunk_start(i):
    return (7 * lax.div(i, 2) + 3 * lax.rem(i, 2)) * 128


def iota(shape, axis):
    return lax.broadcasted_iota(jnp.int32, shape, axis)


def dot(a, b, cb=0):
    return lax.dot_general(a, b, (((1,), (cb,)), ((), ())), preferred_element_type=F32)


def head_sum(x):
    left = iota(x.shape, 1) < 64
    a = jnp.sum(jnp.where(left, x, 0.0), axis=1, keepdims=True)
    b = jnp.sum(jnp.where(left, 0.0, x), axis=1, keepdims=True)
    return jnp.where(left, a, b)


def split(x):
    high = x.astype(BF16)
    return high, (x - high.astype(F32)).astype(BF16)


def join(stats, per, count):
    blocks = stats[...]
    total = jnp.sum(blocks, axis=0)
    mean = total[0:1] * (1.0 / blocks.shape[0])
    dev = blocks - mean[None]
    between = jnp.sum(dev * dev, axis=0)[0:1]
    return mean, (total[1:2] + per * between) * (1.0 / count)


def block_stats(x, st):
    mean = jnp.sum(x, axis=0, keepdims=True) * (1.0 / x.shape[0])
    dev = x - mean
    st[0:1, :] = mean
    st[1:2, :] = jnp.sum(dev * dev, axis=0, keepdims=True)
    return dev


INPUTS = [
    "ids", "lens", "pos", "gains", "biases", "mixes", "mixes2", "edges", "state", "low", "maps",
    "emit", "look", "acc", "down", "vocab", "second", "floor", "bonus", "gn_gain", "gn_bias",
]
LOCAL = [
    "ids", "lens", "pos", "gains", "biases", "mixes", "mixes2", "edges", "state", "second",
    "floor", "bonus", "gn_gain", "gn_bias",
]
LOCAL_SHAPES = [
    ((1, 4), jnp.int32),
    ((1,), jnp.int32),
    ((1,), jnp.int32),
    ((2, 64), F32),
    ((2, 64), F32),
    ((5, 64), F32),
    ((2, 64), F32),
    ((2, 4096), BF16),
    ((16, 64, 64), BF16),
    ((128, 128), BF16),
    ((8, 128), F32),
    ((8, 128), F32),
    ((8, 128), F32),
    ((8, 128), F32),
]
OUTPUTS = ["hidden", "new_edges", "states"]
SCRATCH = [
    ("meta_s", (1, 128), jnp.int32),
    ("meta_r", (64, 1, 128), jnp.int32),
    ("prm_s", (16, 128), F32),
    ("prm_r", (8, 16, 128), F32),
    ("edges_s", (8, 8, 128), BF16),
    ("edges_r", (64, 8, 128), BF16),
    ("state_p", (64, 8, 128), BF16),
    ("state_n", (8, 64, 128), BF16),
    ("out", (256, 64), F32),
    ("edges_f", (64, 8, 128), F32),
    ("state_r", (64, 8, 128), BF16),
    ("state_s", (64, 8, 128), BF16),
    ("state_z", (8, 8, 8, 128), BF16),
    ("low_w", (8, 64, 128), BF16),
    ("maps_w", (4, 8, 64, 128), BF16),
    ("emit_w", (8, 64, 128), BF16),
    ("look_w", (8, 64, 512), BF16),
    ("acc_w", (8, 64, 128), BF16),
    ("down_w", (8, 64, 512), BF16),
    ("vocab_w", (64, 16384), BF16),
    ("table", (64, 128), F32),
    ("emb_s", (64, 256), BF16),
    ("emb_r", (NX, 64, 256), BF16),
    ("blk", (64, 256), BF16),
    ("st", (2, 256), F32),
    ("st_r", (64, 2, 256), F32),
    ("stream_r", (8, 64, 256), BF16),
    ("part_s", (2, 5, 128, 128), BF16),
    ("part_r", (2, 8, 5, 16, 128), BF16),
    ("bd", (8, 128, 128), BF16),
    ("gated_s", (2, 16, 128), BF16),
    ("gated_r", (2, 8, 16, 128), BF16),
    ("new_s", (8, 64, 128), BF16),
    ("att_s", (2, 8, 64, 128), BF16),
    ("att_r", (2, 8, 64, 128), BF16),
    ("attx_s", (2, 64, 128), BF16),
    ("attx_r", (2, NX, 64, 128), BF16),
    ("two", (64, 256), F32),
    ("dev2_s", (2, 64, 128), BF16),
    ("stats2_s", (2, 2, 128), F32),
    ("stats2_r", (2, 64, 2, 128), F32),
    ("dev2_r", (2, 8, 64, 128), BF16),
    ("up_s", (2, 8, 16, 512), BF16),
    ("up_r", (2, 8, 16, 512), BF16),
    ("rec_s", (8, 16, 256), BF16),
    ("rec_r", (8, 16, 256), BF16),
    ("units_s", (2, 16, 512), BF16),
    ("units_r", (2, 8, 16, 512), BF16),
    ("sig_s", (16, 256), F32),
    ("sig_r", (4, 16, 256), F32),
    ("val_s", (2, 8, 64, 128), BF16),
    ("val_r", (2, 8, 64, 128), BF16),
    ("valx_s", (2, 64, 128), BF16),
    ("valx_r", (2, NX, 64, 128), BF16),
    ("norm_t", (512, 256), F32),
]
SEMS = [
    "meta", "prm", "edges", "state", "zstate", "low", "maps", "emit", "look", "acc", "down", "emb",
    "stats", "stream", "new", "rec",
]
HALVES = [
    "part", "gated", "att", "attx", "dev2", "stats2", "up", "units", "val", "valx",
]


class Refs:
    pass


def kernel(*refs):
    r, s = Refs(), Refs()
    names = INPUTS + OUTPUTS + [n for n, _, _ in SCRATCH]
    refs, meta_m = refs[:-1], refs[-1]
    refs, fetched = refs[: -len(LOCAL)], refs[-len(LOCAL) :]
    for name, ref in zip(names, refs):
        setattr(r, name + ("_o" if name in OUTPUTS else ""), ref)
    for name, ref in zip(SEMS + HALVES + ["sig", "vocab", "smem", "local"], refs[len(names) :]):
        setattr(s, name, ref)
    h, b, y, z, c, q = place()
    gb, gq, gx, gz = Group("b"), Group("q"), Group("x"), Group("z")

    dest = lambda k: (k, batch_of(y, 2 * h + c, lax.div(z, NX)))
    source = lambda k: (lax.div(z, 2), batch_of(y, c * NX + k, lax.rem(z, 2)))
    dest_here = dest(0)[1] == b

    sem = pltpu.get_barrier_semaphore()
    for g in (gb, gx):
        g.each(
            lambda p, i: pl.semaphore_signal(sem, inc=1, device_id=g.dev(i), device_id_type=MESH)
        )
    for k in range(4):
        far = source(k)

        @pl.when(jnp.logical_and(far[0] != h, far[1] != b))
        def _():
            pl.semaphore_signal(sem, inc=1, device_id=far, device_id_type=MESH)

    fetch = {}
    for n, (name, ref) in enumerate(zip(LOCAL, fetched)):
        whole = getattr(r, name)
        if name == "second":
            whole = whole.at[:, lanes(q * 128, 128)]
        fetch[name] = pltpu.make_async_copy(whole, ref, s.local.at[n])
        fetch[name].start()
        setattr(r, name, ref)
    vocab_in = pltpu.make_async_copy(r.vocab, r.vocab_w, s.vocab)
    vocab_in.start()
    for name in LOCAL[:7]:
        fetch[name].wait()
    lane = iota((1, 128), 1)
    meta = jnp.where(lane == 4, r.lens[0], jnp.where(lane == 5, r.pos[0], 0))
    for j in range(4):
        meta = jnp.where(lane == j, r.ids[0, j], meta)
    r.meta_s[...] = meta
    r.prm_s[...] = jnp.zeros((16, 128), F32)
    r.prm_s[0:2, 0:64] = r.gains[...]
    r.prm_s[2:4, 0:64] = r.biases[...]
    r.prm_s[4:9, 0:64] = r.mixes[...]
    r.prm_s[9:11, 0:64] = r.mixes2[...]
    prm = r.prm_s[...]
    r.prm_s[...] = jnp.where(c == 0, prm, pltpu.roll(prm, 64, 1))

    fetch["edges"].wait()
    old = r.edges[...].astype(F32)
    for k in range(NZ):
        tiles = [old[:, (i * NZ + k) * 128 : (i * NZ + k) * 128 + 128] for i in range(NY)]
        r.edges_s[k] = jnp.concatenate(tiles, axis=0).astype(BF16)
    fetch["state"].wait()
    for k in range(16):
        tile = r.state[k].astype(F32)
        tile = jnp.concatenate([tile[0:32], tile[32:64]], axis=1).astype(BF16)
        for i in range(4):
            r.state_p[k * 4 + i] = tile[i * 8 : i * 8 + 8]

    pl.semaphore_wait(sem, gb.n - 1 + gx.n - 1 + 3 * (1 - dest_here.astype(jnp.int32)))

    def same(ref):
        return lambda i: ref

    def slots(ref):
        return lambda m: ref.at[m]

    x_meta = Exchange(gb, same(r.meta_s), slots(r.meta_r), r.meta_r, s.meta)
    x_prm = Exchange(gq, same(r.prm_s), slots(r.prm_r), r.prm_r, s.prm)
    x_edges = Exchange(
        gb, lambda i: r.edges_s.at[lax.rem(lax.div(i, NC), NZ)], slots(r.edges_r), r.edges_r, s.edges
    )
    x_state = Exchange(
        gb,
        lambda i: r.state_p.at[
            (lax.div(i, NC * NZ) * NC + lax.rem(i, NC)) * NZ + lax.rem(lax.div(i, NC), NZ)
        ],
        slots(r.state_r),
        r.state_r,
        s.state,
    )
    x_low = Exchange(gq, same(r.low), slots(r.low_w), r.low_w, s.low)
    x_maps = Exchange(
        gq,
        lambda i: r.maps.at[:, :, lanes(i * 128, 128)],
        lambda m: r.maps_w.at[:, m],
        r.maps_w,
        s.maps,
    )
    x_emit = Exchange(gq, lambda i: r.emit.at[:, lanes(i * 128, 128)], slots(r.emit_w), r.emit_w, s.emit)
    x_look = Exchange(
        gq, lambda i: r.look.at[:, lanes(chunk_start(i), 512)], slots(r.look_w), r.look_w, s.look
    )
    x_acc = Exchange(
        gq,
        lambda i: r.acc.at[:, lanes((lax.div(i, NC) * NZ + 2 * h + lax.rem(i, NC)) * 128, 128)],
        slots(r.acc_w),
        r.acc_w,
        s.acc,
    )
    x_down = Exchange(
        gq, lambda i: r.down.at[:, lanes(chunk_start(i), 512)], slots(r.down_w), r.down_w, s.down
    )
    for x in (x_meta, x_maps, x_low, x_prm, x_edges):
        x.start()

    x_meta.arrive()
    to_smem = pltpu.make_async_copy(r.meta_r, meta_m, s.smem)
    to_smem.start()
    meta = r.meta_r[...].reshape(64, 128)
    high = lax.shift_right_logical(meta, 8)
    lowb = (meta - high * 256).astype(F32).astype(BF16)
    high = high.astype(F32).astype(BF16)

    def device_of(zz, qq):
        return (lax.shift_right_logical(qq, 1) * NZ + zz) * NC + (qq & 1)

    tok = iota((256, 64), 0)
    by_tok = device_of(lax.shift_right_logical(tok, 4) & 7, tok & 7) == iota((256, 64), 1)
    by_tok = jnp.where(by_tok, 1.0, 0.0).astype(BF16)
    cols = dot(by_tok, high) * 256.0 + dot(by_tok, lowb)
    req = iota((64, 64), 0)
    by_req = device_of(lax.shift_right_logical(req, 3), req & 7) == iota((64, 64), 1)
    by_req = jnp.where(by_req, 1.0, 0.0).astype(BF16)
    r.table[...] = dot(by_req, lowb)
    tok_rows = cols.T
    lane_t = iota((1, 256), 1)
    slot = lax.shift_right_logical(lane_t, 7) * 2 + (lax.shift_right_logical(lane_t, 3) & 1)
    ids = tok_rows[0:1]
    for j in range(1, 4):
        ids = jnp.where(slot == j, tok_rows[j : j + 1], ids)
    ids = ids.astype(jnp.int32) - h * 16384
    length = tok_rows[4:5].astype(jnp.int32)

    vocab_in.wait()
    step = 16384

    def look_up(k, acc):
        base = pl.multiple_of(k * step, step)
        hot = jnp.where(iota((step, 256), 0) == ids - base, 1.0, 0.0).astype(BF16)
        return acc + dot(r.vocab_w[:, pl.ds(base, step)], hot)

    emb = lax.fori_loop(0, 16384 // step, look_up, jnp.zeros((64, 256), F32))
    r.emb_s[...] = emb.astype(BF16)
    x_emb = Exchange(gx, same(r.emb_s), slots(r.emb_r), r.emb_r, s.emb)
    x_emb.start()
    x_state.start()

    x_emb.arrive()
    own = jnp.sum(r.emb_r[...].astype(F32), axis=0)
    r.blk[...] = own.astype(BF16)
    x_stream = Exchange(gq, same(r.blk), slots(r.stream_r), r.stream_r, s.stream)
    x_stream.start()
    block_stats(own, r.st)
    x_stats = Exchange(gb, same(r.st), slots(r.st_r), r.st_r, s.stats)
    x_stats.start()

    x_edges.arrive()
    x_state.arrive()
    to_smem.wait()

    def reorder(n, carry):
        zz = lax.div(n, 8)
        qq = lax.rem(n, 8)
        old = meta_m[batch_of(lax.div(qq, 2), zz, lax.rem(qq, 2)), 0, 5]
        r.edges_f[n] = r.edges_r[old].astype(F32)
        r.state_s[n] = r.state_r[old]
        return carry

    lax.fori_loop(0, 64, reorder, 0)
    x_zstate = Exchange(gz, lambda i: r.state_s.at[rows(i * 8, 8)], slots(r.state_z), r.state_z, s.zstate)
    x_zstate.start()

    x_prm.arrive()
    prm = jnp.concatenate([r.prm_r[2 * k] + r.prm_r[2 * k + 1] for k in range(NY)], axis=1)

    def edge_rows(k):
        return jnp.concatenate([r.edges_f[:, i * 2 + k, :] for i in range(NY)], axis=1)

    def shifted(normed, k, first):
        now = normed.astype(F32).reshape(2, 8, 2, 8, 512)
        edge = edge_rows(k)
        before = [
            jnp.concatenate([edge.reshape(8, 1, 8, 512), now[0, :, :1]], axis=1).reshape(128, 512),
            jnp.concatenate([now[0, :, 1:], now[1, :, :1]], axis=1).reshape(128, 512),
        ]
        now = [now[k].reshape(128, 512) for k in range(2)]
        delta = [before[k] - now[k] for k in range(2)]
        return lambda n, k: (now[k] + delta[k] * prm[first + n : first + n + 1]).astype(BF16)

    def halves(group, name, src):
        got, sems = getattr(r, name + "_r"), getattr(s, name)
        return [
            Exchange(
                group,
                lambda i, k=k: src(k, i),
                lambda m, k=k: got.at[k, m],
                got.at[k],
                sems.at[k],
            )
            for k in range(2)
        ]

    last = jnp.logical_and(
        iota((64, 256), 0)
        == device_of(lax.shift_right_logical(lane_t, 4) & 7, lane_t & 7),
        slot == length - 1,
    )
    last = jnp.where(last, 1.0, 0.0).astype(BF16)

    def layer(x, k):
        normed = (x.T * prm[k : k + 1] + prm[2 + k : 3 + k]).astype(BF16)
        return normed

    x_stream.arrive()
    x_stats.arrive()
    mean, var = join(r.st_r, 64.0, 4096.0)
    scaled = (r.stream_r[...].astype(F32).reshape(512, 256) - mean) * lax.rsqrt(var + EPS_LN)
    normed = layer(scaled, 0)
    mixed = shifted(normed, 0, 4)
    x_maps.arrive()
    x_low.arrive()
    x_part = halves(gz, "part", lambda k, i: r.part_s.at[k, :, rows(i * 16, 16)])
    for k in range(2):
        for n in range(5):
            w = r.maps_w[n] if n < 4 else r.low_w[...]
            r.part_s[k, n] = dot(mixed(n, k), w.reshape(512, 128)).astype(BF16)
        x_part[k].start()
    for x in (x_emit, x_look, x_acc, x_down):
        x.start()

    r.norm_t[...] = normed.astype(F32).T
    mine = r.norm_t[rows(q * 64, 64), :].astype(BF16)
    r.new_edges_o[0] = dot(last, mine, 1).astype(BF16)

    x_zstate.arrive()
    left = iota((32, 128), 1) < 64
    for n in range(8):
        tile = r.state_z[:, n].astype(F32).reshape(64, 128)
        turn = pltpu.roll(tile, 64, 1)
        blocks = [
            jnp.where(left, tile[0:32], 0.0),
            jnp.where(left, turn[0:32], 0.0),
            jnp.where(left, 0.0, turn[32:64]),
            jnp.where(left, 0.0, tile[32:64]),
        ]
        r.bd[n] = jnp.concatenate(blocks, axis=0).astype(BF16)
    lens8 = r.table[rows(z * 8, 8), :][:, 4:5].astype(jnp.int32)

    for name in LOCAL[9:]:
        fetch[name].wait()
    floor, bonus, gn_gain, gn_bias = (
        ref[pl.ds(q, 1), :] for ref in (r.floor, r.bonus, r.gn_gain, r.gn_bias)
    )
    alive = [lens8 > j for j in range(4)]

    def spread(x):
        row_q = iota(x.shape, 0) & 7
        return jnp.concatenate([jnp.where(row_q == n, x, 0.0) for n in range(8)], axis=1)

    bd = r.bd[...].reshape(1024, 128)
    rec, key, val, dec = [], [], [], []
    x_gated = halves(gz, "gated", lambda k, i: r.gated_s.at[k])
    for k in range(2):
        x_part[k].arrive()
        proj = jnp.sum(r.part_r[k].astype(F32), axis=0)
        low = jnp.tanh(proj[4]).astype(BF16)
        decay = jnp.exp(-jnp.exp(floor + dot(low, r.second[...])))
        for j in range(2):
            rec.append(proj[0, 8 * j : 8 * j + 8])
            key.append(proj[1, 8 * j : 8 * j + 8])
            val.append(proj[2, 8 * j : 8 * j + 8])
            dec.append(decay[8 * j : 8 * j + 8])
        seen, inner = [], []
        for j in range(2 * k, 2 * k + 2):
            acc = head_sum(rec[j] * bonus * key[j]) * val[j]
            run = rec[j]
            for i in range(j - 1, -1, -1):
                acc = acc + head_sum(run * key[i]) * val[i]
                run = run * dec[i]
            seen.append(run)
            inner.append(acc)
        high, rest = split(spread(jnp.concatenate(seen, axis=0)))
        wkv = dot(high, bd) + dot(rest, bd) + jnp.concatenate(inner, axis=0)
        mu = head_sum(wkv) * (1.0 / 64)
        dev = wkv - mu
        spr = head_sum(dev * dev) * (1.0 / 64)
        grouped = dev * lax.rsqrt(spr + EPS_GN) * gn_gain + gn_bias
        gate = proj[3]
        r.gated_s[k] = (grouped * (gate * jax.nn.sigmoid(gate))).astype(BF16)
        x_gated[k].start()

    x_emit.arrive()
    x_att = halves(gq, "att", lambda k, i: r.att_s.at[k, i])
    x_attx = halves(gx, "attx", lambda k, i: r.attx_s.at[k])
    for k in range(2):
        x_gated[k].arrive()
        att = dot(r.emit_w[...].reshape(512, 128), r.gated_r[k].reshape(128, 128), 1)
        r.att_s[k] = att.astype(BF16).reshape(8, 64, 128)
        x_att[k].start()
    tail, keys = jnp.ones((8, 128), F32), []
    for j in range(3, -1, -1):
        keys.append(jnp.where(alive[j], key[j] * tail, 0.0))
        tail = jnp.where(alive[j], tail * dec[j], tail)
    keys = spread(jnp.concatenate(keys[::-1], axis=0)).T
    vals = jnp.concatenate(val, axis=0)
    kh, kl = split(keys)
    vh, vl = split(vals)
    outer = dot(kh, vh) + dot(kl, vh) + dot(kh, vl)
    tail = tail.T
    for n in range(8):
        new = outer[n * 128 : n * 128 + 128] + tail[:, n : n + 1] * r.bd[n].astype(F32)
        turn = pltpu.roll(new, 64, 1)
        top = jnp.where(left, new[0:32], turn[32:64])
        bottom = jnp.where(left, turn[64:96], new[96:128])
        r.new_s[n] = jnp.concatenate([top, bottom], axis=0).astype(BF16)
    x_new = Exchange(gq, lambda i: r.new_s.at[i], lambda m: r.state_n.at[m], r.state_n, s.new)
    x_new.start()

    for k in range(2):
        x_att[k].arrive()
        r.attx_s[k] = jnp.sum(r.att_r[k].astype(F32), axis=0).astype(BF16)
        x_attx[k].start()
    x_dev = halves(gq, "dev2", lambda k, i: r.dev2_s.at[k])
    x_stats2 = halves(gb, "stats2", lambda k, i: r.stats2_s.at[k])
    for k in range(2):
        x_attx[k].arrive()
        part = slice(k * 128, k * 128 + 128)
        two = r.blk[:, part].astype(F32) + jnp.sum(r.attx_r[k].astype(F32), axis=0)
        r.two[:, part] = two
        r.dev2_s[k] = block_stats(two, r.stats2_s.at[k]).astype(BF16)
        x_dev[k].start()
        x_stats2[k].start()
    edge = edge_rows(1).reshape(8, 1, 8, 512)
    now, delta = [], []

    def second(k):
        x_dev[k].arrive()
        x_stats2[k].arrive()
        mean, var = join(r.stats2_r.at[k], 64.0, 4096.0)
        scale = lax.rsqrt(var + EPS_LN)
        blocks = []
        for n in range(8):
            off = r.stats2_r[k, batch_of(n // 2, z, n % 2)][0:1] - mean
            blocks.append((r.dev2_r[k, n].astype(F32) + off) * scale)
        normed = jnp.concatenate(blocks, axis=0).T * prm[1:2] + prm[3:4]
        normed = normed.astype(BF16).astype(F32)
        r.norm_t[:, k * 128 : k * 128 + 128] = normed.T
        now.append(normed)
        split_now = [n.reshape(8, 2, 8, 512) for n in now]
        ahead = edge if k == 0 else split_now[0][:, 1:]
        before = jnp.concatenate([ahead, split_now[k][:, :1]], axis=1).reshape(128, 512)
        delta.append(before - normed)

    def mixed(n, k):
        return (now[k] + delta[k] * prm[9 + n : 10 + n]).astype(BF16)

    x_look.arrive()
    x_acc.arrive()
    x_up = halves(gz, "up", lambda k, i: r.up_s.at[k, i])
    x_units = halves(gz, "units", lambda k, i: r.units_s.at[k])
    x_val = halves(gq, "val", lambda k, i: r.val_s.at[k, i])
    x_valx = halves(gx, "valx", lambda k, i: r.valx_s.at[k])
    for k in range(2):
        second(k)
        up = dot(mixed(0, k), r.look_w[...].reshape(512, 512))
        r.up_s[k] = up.astype(BF16).reshape(8, 16, 512)
        x_up[k].start()
    for k in range(2):
        x_up[k].arrive()
        up = jnp.maximum(jnp.sum(r.up_r[k].astype(F32), axis=0), 0.0)
        up = jnp.where(jnp.logical_and(c == 1, iota(up.shape, 1) < 128), 0.0, up * up)
        r.units_s[k] = up.astype(BF16)
        x_units[k].start()
    mine = r.norm_t[rows(q * 64, 64), :].astype(BF16)
    r.new_edges_o[1] = dot(last, mine, 1).astype(BF16)
    take = [dot(mixed(1, k), r.acc_w[...].reshape(512, 128)) for k in range(2)]
    take = jnp.concatenate(take, axis=0).T
    r.rec_s[...] = take.astype(BF16).reshape(8, 16, 256)
    x_rec = Exchange(gz, lambda i: r.rec_s.at[i], slots(r.rec_r), r.rec_r, s.rec)
    x_rec.start()
    x_down.arrive()
    for k in range(2):
        x_units[k].arrive()
        value = dot(r.down_w[...].reshape(512, 512), r.units_r[k].reshape(128, 512), 1)
        r.val_s[k] = value.astype(BF16).reshape(8, 64, 128)
        x_val[k].start()
    x_rec.arrive()
    r.sig_s[...] = jax.nn.sigmoid(jnp.sum(r.rec_r[...].astype(F32), axis=0))

    def far_copy(k):
        return pltpu.make_async_remote_copy(
            src_ref=r.sig_s,
            dst_ref=r.sig_r.at[lax.rem(z, NX)],
            send_sem=s.sig.at[0],
            recv_sem=s.sig.at[1],
            device_id=dest(k),
            device_id_type=MESH,
        )

    for k in range(4):
        here = jnp.logical_and(dest_here, h == k)

        @pl.when(jnp.logical_not(here))
        def _():
            far_copy(k).start()

        @pl.when(here)
        def _():
            pltpu.make_async_copy(r.sig_s, r.sig_r.at[lax.rem(z, NX)], s.sig.at[1]).start()

    x_new.arrive()
    for k in range(16):
        tile = r.state_n[k // 2].astype(F32)[(k % 2) * 32 : (k % 2) * 32 + 32]
        r.states_o[k, 0:32] = tile[:, 0:64].astype(BF16)
        r.states_o[k, 32:64] = tile[:, 64:128].astype(BF16)
    for k in range(2):
        x_val[k].arrive()
        r.valx_s[k] = jnp.sum(r.val_r[k].astype(F32), axis=0).astype(BF16)
        x_valx[k].start()
    pltpu.make_async_copy(r.sig_r, r.sig_r, s.sig.at[1]).wait()
    value = []
    for k in range(2):
        x_valx[k].arrive()
        value.append(jnp.sum(r.valx_r[k].astype(F32), axis=0))
    value = jnp.concatenate(value, axis=1)
    result = r.two[...] + r.sig_r[...].reshape(64, 256) * value
    r.out[...] = jnp.where(slot < length, result, 0.0).T
    for k in range(64):
        first = (k // 2 % NZ) * 16 + (k // 16) * 2 + k % 2
        r.hidden_o[k, 0:2] = r.out[pl.ds(first, 2, stride=8), :]
        r.hidden_o[k, 2:4] = r.out[pl.ds(first + 128, 2, stride=8), :]

    for k in range(4):

        @pl.when(jnp.logical_not(jnp.logical_and(dest_here, h == k)))
        def _():
            far_copy(k).wait_send()

    for x in (
        x_meta, x_prm, x_edges, x_state, x_low, x_maps, x_emit, x_look, x_acc, x_down, x_emb,
        x_zstate, x_stream, x_stats, x_new, x_rec, *x_dev, *x_stats2, *x_part, *x_gated, *x_att,
        *x_attx, *x_up, *x_units, *x_val, *x_valx,
    ):
        x.drain()


def local(
    query_symbol_numbers,
    alive_span_sizes,
    former_positions,
    previous_normed_vectors,
    memory_matrices,
    vocabulary_vectors,
    standardize_scales,
    standardize_shifts,
    timemix_blend_factors,
    timemix_linear_maps,
    forgetting_first_lowrank,
    forgetting_second_lowrank,
    forgetting_loglog_floor,
    current_reward_factor,
    perspan_standardize_scale,
    perspan_standardize_shift,
    timemix_emit_matrix,
    feedforward_blend_factors,
    feedforward_lookup_matrix,
    feedforward_accept_matrix,
    feedforward_emit_matrix,
):
    hidden, new_edges, states = pl.pallas_call(
        kernel,
        out_shape=[
            jax.ShapeDtypeStruct((64, 4, 64), F32),
            jax.ShapeDtypeStruct((2, 64, 64), BF16),
            jax.ShapeDtypeStruct((16, 64, 64), BF16),
        ],
        in_specs=[ANY] * len(INPUTS),
        out_specs=[VM] * 3,
        scratch_shapes=[pltpu.VMEM(shape, dtype) for _, shape, dtype in SCRATCH]
        + [DMA((2,)) for _ in SEMS]
        + [DMA((2, 2)) for _ in HALVES]
        + [DMA((2,)), DMA(()), DMA(()), DMA((len(LOCAL),))]
        + [
            (pltpu.SMEM if n < 3 else pltpu.VMEM)(shape, dtype)
            for n, (shape, dtype) in enumerate(LOCAL_SHAPES)
        ]
        + [pltpu.SMEM((64, 1, 128), jnp.int32)],
        compiler_params=pltpu.CompilerParams(
            collective_id=0, has_side_effects=True, vmem_limit_bytes=67043328
        ),
        name="layer",
    )(
        query_symbol_numbers,
        alive_span_sizes,
        former_positions,
        standardize_scales,
        standardize_shifts,
        timemix_blend_factors,
        feedforward_blend_factors,
        previous_normed_vectors.reshape(2, 4096),
        memory_matrices.reshape(16, 64, 64),
        forgetting_first_lowrank,
        timemix_linear_maps,
        timemix_emit_matrix,
        feedforward_lookup_matrix,
        feedforward_accept_matrix,
        feedforward_emit_matrix,
        vocabulary_vectors,
        forgetting_second_lowrank,
        forgetting_loglog_floor.reshape(8, 128),
        current_reward_factor.reshape(8, 128),
        perspan_standardize_scale.reshape(8, 128),
        perspan_standardize_shift.reshape(8, 128),
    )
    return hidden, new_edges, states.reshape(1, 16, 64, 64)


def solution(mesh):
    return jax.shard_map(
        local,
        mesh=mesh,
        in_specs=(
            P("batch", None),
            P("batch"),
            P("batch"),
            P(None, "batch", None),
            P("batch", "head", None, None),
            P("batch", "head"),
            P(None, "batch"),
            P(None, "batch"),
            P(None, "batch"),
            P(None, "batch", "head"),
            P("batch", None),
            P(None, "head"),
            P("head"),
            P("head"),
            P("head"),
            P("head"),
            P("batch", "head"),
            P(None, "batch"),
            P("batch", "head"),
            P("batch", None),
            P("batch", "head"),
        ),
        out_specs=(P(None, None, "batch"), P(None, None, "batch"), P("batch", "head", None, None)),
        check_vma=False,
    )
```
